32 devices in a mesh: segment: 4 (over z), expert: 4 (over y, x), dp: 2 (over core).
Axes of the slice: x: 2, y: 2, z: 4, core: 2. Of those that a mesh axis runs over, the one named last changes fastest.
Arguments:
- x_in: bfloat16 [4, 2, 512, 2048], P('segment', 'dp', 'expert'), may hold values from -6 to 6
- memory: bfloat16 [4, 2, 512, 2048], P('segment', 'dp', 'expert'), may hold values from -6 to 6
- w_qkv: bfloat16 [4, 3, 2048, 2048], P('segment', None, None, 'expert'), may hold values from -0.125 to 0.125
- w_attn_out: bfloat16 [4, 2048, 2048], P('segment', 'expert'), may hold values from -0.125 to 0.125
- norm_gains: float32 [4, 2, 2048], P('segment'), may hold values from 0.1 to 1.9
- router: float32 [4, 2048, 4], P('segment'), may hold values from -0.125 to 0.125
- w_in: bfloat16 [4, 2048, 16384], P('segment', None, 'expert'), may hold values from -0.125 to 0.125
- w_exp_out: bfloat16 [4, 16384, 2048], P('segment', 'expert'), may hold values from -0.09375 to 0.09375
- expert_ids: int32 [4, 2, 512, 2], P('segment', 'dp', 'expert'), may hold values from 0 to 3, all different within a row; in each aligned block of 128 rows (0 to 127, 128 to 255, ..., all dimensions but the last counted through in order) at most 64 rows name the same one
- lengths: int32 [4, 2, 4], P('segment', 'dp'), may hold values from 32 to 128, as said below
- cotangent: bfloat16 [4, 2, 512, 2048], P('segment', 'dp', 'expert'), may hold values from -24 to 24
Outputs:
- next_acts: bfloat16 [4, 2, 512, 2048], P('segment', 'dp', 'expert')
- memory_next: bfloat16 [4, 2, 512, 2048], P('segment', 'dp', 'expert')
- router_grad: float32 [4, 2048, 4], P('segment')
The draws below stay inside these ranges and needn't reach their ends.
Inputs may be any that keep to these rules, and one draw needn't show every extreme that they name: `expert_ids`: each row names 2 different experts. Within the 128 rows of one device (aligned blocks of the flattened leading dimensions) every expert is named by exactly 64 rows. `lengths`: keys of a sequence at or past its length are padding.
All inputs are finite; a program needn't handle non-finite values.
Results may differ from the reference program's by a relative error of at most 0.02.
Values may be sent and summed in bfloat16 or wider, within the bound.
A program may use at most 128 MiB of HBM per device.

```python
import math
import jax
import jax.numpy as jnp
import numpy as np
from jax import lax

D = 2048
HEADS = 16
HEAD_DIM = 128
HIDDEN_SIZE = 4096
EXPERTS = 4
TOP = 2
TOK_DEV = 128
SEQ = 128
SEGMENTS = 4
HID_DEV = 4096
CAP = 64
GROUP = 512
N_EXPERT = 4
N_DP = 2


def draw_lengths(key, part):
    count = GROUP // SEQ
    first_key, second_key = jax.random.split(jax.random.fold_in(key, 17))
    values = jax.random.randint(first_key, (SEGMENTS, N_DP, count), SEQ // 4, SEQ + 1)
    full_at = jax.random.randint(second_key, (SEGMENTS, N_DP, 1), 0, count)
    position = jnp.arange(count)[None, None, :]
    values = jnp.where(position == full_at, SEQ, values)
    values = jnp.where(position == (full_at + 1) % count, SEQ // 4, values)
    return values.astype(jnp.int32)


def block_levels(own_key, shape, cuts, least, top_value):
    def one(dim, parts):
        heights = jax.random.uniform(jax.random.fold_in(jax.random.fold_in(own_key, 6), dim), (parts,), jnp.float32, least / len(cuts), top_value / len(cuts))
        return jnp.repeat(jnp.exp(heights), shape[dim] // parts).reshape((-1,) + (1,) * (len(shape) - dim - 1))

    factor_of = one(*cuts[0])
    for cut in cuts[1:]:
        factor_of = factor_of * one(*cut)
    return factor_of


def routed_block(own_key, own, number, rows, count, top, most, skew):
    ranking = jax.random.permutation(own_key, count)
    heavy_load, ordinary = portions_of(count, rows * top, most, skew, True), portions_of(count, rows * top, most, skew, False)
    places = jnp.arange(count)

    def named(sizes, turn):
        used = int((sizes > 0).sum())
        fixed = max(1, used // 4)
        moved = fixed + (places - fixed + turn * (used - fixed)) % max(1, count - fixed)
        return jnp.zeros((count,), jnp.int32).at[ranking[jnp.where(places < fixed, places, moved)]].set(jnp.asarray(sizes, jnp.int32))

    sizes = jnp.where(number % 4 == 0, named(heavy_load, number // 4), named(ordinary, number - number // 4 - 1))
    mixed = jax.random.permutation(jax.random.fold_in(own, 3), count)
    source_of, sink = mixed[0:count // 2 * 2:2], mixed[1:count // 2 * 2:2]
    margin = jnp.minimum(sizes[source_of] - 1, most - sizes[sink]) // 2
    margin = jnp.where((source_of == ranking[0]) | (sink == ranking[0]) | (sizes[sink] == 0), 0, jnp.maximum(margin, 0))
    moved = jax.random.randint(jax.random.fold_in(own, 4), (count // 2,), 0, 1 << 20) % (margin + 1)
    sizes = sizes.at[source_of].add(-moved).at[sink].add(moved)
    items = jnp.searchsorted(jnp.cumsum(sizes), jnp.arange(rows * top), side="right").astype(jnp.int32)
    grid = items.reshape(top, rows).T
    grid = grid[jax.random.permutation(jax.random.fold_in(own, 1), rows)]
    turn = jax.random.randint(jax.random.fold_in(own, 2), (rows, 1), 0, top)
    return jnp.take_along_axis(grid, (jnp.arange(top)[None, :] + turn) % top, axis=1)


def portions_of(amount, total, limit, skew, full):
    loads = [(1 << 20) // math.isqrt(rank ** skew) + 1 for rank in range(1, amount + 1)]
    largest = limit if full else min(limit, max(-(-total // amount), total * loads[0] // sum(loads)))
    least = 1 if total - largest >= amount - 1 else 0
    holding, surplus = [largest] + [least] * (amount - 1), total - largest - least * (amount - 1)
    while surplus > 0:
        movable = [i for i in range(1, amount) if holding[i] < largest] or [i for i in range(1, amount) if holding[i] < limit]
        pool, left = sum([loads[i] for i in movable]), surplus
        for i in movable:
            more = min(limit - holding[i], max(1, left * loads[i] // pool), surplus)
            holding[i] = holding[i] + more
            surplus = surplus - more
    return np.array(holding)


def scatter_about(key, shape, scale, most, shards=(), kind=jnp.bfloat16):
    loudness = block_levels(key, shape, shards, -0.22, 0.18) if shards else 1.0
    values = jax.random.normal(key, shape, jnp.float32) * scale * loudness
    return jnp.minimum(jnp.maximum(values, -most), most).astype(kind)


def setup_inputs(seed: int = 0) -> dict:
    splits = jax.random.split(jax.random.key(seed), 12)
    x_in = scatter_about(splits[0], (SEGMENTS, N_DP, GROUP, D), 1.0, 6.0, ((0, 4), (1, 2), (2, 4)))
    memory = scatter_about(splits[1], (SEGMENTS, N_DP, GROUP, D), 1.0, 6.0, ((0, 4), (1, 2), (2, 4)))
    w_qkv = scatter_about(splits[2], (SEGMENTS, 3, D, D), D ** -0.5, 0.125, ((0, 4), (3, 4)))
    w_attn_out = scatter_about(splits[3], (SEGMENTS, D, D), D ** -0.5, 0.125, ((0, 4), (1, 4)))
    norm_gains = jnp.clip(1.0 + 0.18 * jax.random.normal(splits[4], (SEGMENTS, 2, D), jnp.float32), 0.1, 1.9)
    router = scatter_about(splits[5], (SEGMENTS, D, EXPERTS), D ** -0.5, 0.125, ((0, 4),), jnp.float32)
    w_in = scatter_about(splits[6], (SEGMENTS, D, EXPERTS * HIDDEN_SIZE), D ** -0.5, 0.125, ((0, 4), (2, 4)))
    w_exp_out = scatter_about(splits[7], (SEGMENTS, EXPERTS * HIDDEN_SIZE, D), HIDDEN_SIZE ** -0.5, 0.09375, ((0, 4), (1, 4)))
    expert_ids_keys = jax.random.split(jax.random.fold_in(splits[8], 1), SEGMENTS * N_DP * GROUP // TOK_DEV)
    expert_ids_turns = jax.random.permutation(jax.random.fold_in(splits[8], 3), SEGMENTS * N_DP * GROUP // TOK_DEV)
    expert_ids = jax.vmap(lambda own, number: routed_block(jax.random.fold_in(splits[8], 2), own, number, TOK_DEV, EXPERTS, TOP, CAP, 0))(expert_ids_keys, expert_ids_turns).reshape((SEGMENTS, N_DP, GROUP, TOP))
    lengths = draw_lengths(jax.random.fold_in(splits[11], 71), 0)
    cotangent = scatter_about(splits[10], (SEGMENTS, N_DP, GROUP, D), 4.0, 24.0, ((0, 4), (1, 2), (2, 4)))
    return dict(x_in=x_in, memory=memory, w_qkv=w_qkv, w_attn_out=w_attn_out, norm_gains=norm_gains, router=router, w_in=w_in, w_exp_out=w_exp_out, expert_ids=expert_ids, lengths=lengths, cotangent=cotangent)


eps = 1e-05
highest = lax.Precision.HIGHEST

def layer_norm(values, gain):
    centered = values - lax.optimization_barrier(jnp.mean(values, axis=-1, keepdims=True))
    variance = lax.optimization_barrier(jnp.mean(centered * centered, axis=-1, keepdims=True))
    return centered * lax.rsqrt(variance + eps) * gain

def attention(normed, key_source, weights_qkv, w_attn_out, lengths_row):
    query = jnp.dot(normed, weights_qkv[0], preferred_element_type=jnp.float32).astype(jnp.bfloat16)
    keys = jnp.dot(key_source, weights_qkv[1], preferred_element_type=jnp.float32).astype(jnp.bfloat16)
    values = jnp.dot(key_source, weights_qkv[2], preferred_element_type=jnp.float32).astype(jnp.bfloat16)
    count = GROUP // SEQ
    shape = (count, SEQ, HEADS, HEAD_DIM)
    query = query.reshape(shape).astype(jnp.float32)
    keys = keys.reshape(shape).astype(jnp.float32)
    values = values.reshape(shape).astype(jnp.float32)
    scores = jnp.einsum('nihd,njhd->nhij', query, keys) * HEAD_DIM ** (-0.5)
    live = (jnp.arange(SEQ)[None, :] < lengths_row[:, None]).astype(jnp.float32)
    raised = jnp.exp(scores) * live[:, None, None, :]
    probs = (raised / lax.optimization_barrier(jnp.sum(raised, axis=-1, keepdims=True))).astype(jnp.bfloat16)
    context = jnp.einsum('nhij,njhd->nihd', probs.astype(jnp.float32), values)
    context = context.astype(jnp.bfloat16).reshape(GROUP, D)
    head_cols = HEADS // N_EXPERT * HEAD_DIM
    blocks_ctx = jnp.transpose(context.reshape(GROUP, N_EXPERT, head_cols), (1, 0, 2))
    blocks_w = w_attn_out.reshape(N_EXPERT, head_cols, D)

    def add_block(total, pair):
        part = jnp.dot(pair[0], pair[1], preferred_element_type=jnp.float32)
        return (total + lax.optimization_barrier(part.astype(jnp.bfloat16)).astype(jnp.float32), None)
    total, _ = lax.scan(add_block, jnp.zeros((GROUP, D), jnp.float32), (blocks_ctx, blocks_w))
    return total

def experts(moe_in, ids, w_in_s, w_out_s):
    copies = N_EXPERT // EXPERTS
    per_expert = GROUP * TOP // EXPERTS
    expert_rows = jnp.zeros((GROUP, TOP, D), jnp.float32)
    for index in range(EXPERTS):
        member = jnp.any(ids == index, axis=1)
        rows_idx = jnp.nonzero(member, size=per_expert)[0]
        inputs = moe_in[rows_idx]
        weights_in = w_in_s[:, index * HIDDEN_SIZE:(index + 1) * HIDDEN_SIZE]
        hidden = jnp.maximum(jnp.dot(inputs, weights_in, preferred_element_type=jnp.float32), 0.0).astype(jnp.bfloat16)
        result = jnp.zeros((per_expert, D), jnp.float32)
        for block in range(copies):
            low = block * HID_DEV
            part = jnp.dot(hidden[:, low:low + HID_DEV], w_out_s[index * HIDDEN_SIZE + low:index * HIDDEN_SIZE + low + HID_DEV, :], preferred_element_type=jnp.float32)
            result = result + lax.optimization_barrier(part.astype(jnp.bfloat16)).astype(jnp.float32)
        spread = jnp.zeros((GROUP, D), jnp.float32).at[rows_idx].set(result)
        expert_rows = expert_rows + (ids == index).astype(jnp.float32)[:, :, None] * spread[:, None, :]
    return expert_rows

def reference(x_in, memory, w_qkv, w_attn_out, norm_gains, router, w_in, w_exp_out, expert_ids, lengths, cotangent):
    segment_outs = []
    grads = []
    for segment in range(SEGMENTS):
        grad = jnp.zeros((D, EXPERTS), jnp.float32)
        group_outs = []
        for group in range(N_DP):
            rows = x_in[segment, group]
            normed = layer_norm(rows.astype(jnp.float32), norm_gains[segment, 0]).astype(jnp.bfloat16)
            if segment == 0:
                key_source = normed
            else:
                key_source = memory[segment, group]
            attn_sum = attention(normed, key_source, w_qkv[segment], w_attn_out[segment], lengths[segment, group])
            resid = rows.astype(jnp.float32) + attn_sum
            moe_in = layer_norm(resid, norm_gains[segment, 1]).astype(jnp.bfloat16)
            moe_wide = moe_in.astype(jnp.float32)
            logits = jnp.dot(moe_wide, router[segment], precision=highest)
            ids = expert_ids[segment, group]
            pick = (ids[:, :, None] == jnp.arange(EXPERTS)[None, None, :]).astype(jnp.float32)
            chosen = lax.optimization_barrier(jnp.sum(pick * logits[:, None, :], axis=2))
            gates = jax.nn.sigmoid(chosen - chosen[:, ::-1])
            expert_rows = experts(moe_in, ids, w_in[segment], w_exp_out[segment])
            mixed = lax.optimization_barrier(jnp.sum(gates[:, :, None] * expert_rows, axis=1))
            group_outs.append((resid + mixed).astype(jnp.bfloat16))
            cot = cotangent[segment, group].astype(jnp.float32)
            intersection = lax.optimization_barrier(jnp.sum(cot[:, None, :] * expert_rows, axis=2))
            delta = gates[:, 0] * gates[:, 1] * (intersection[:, 0] - intersection[:, 1])
            dlogits = delta[:, None] * (pick[:, 0] - pick[:, 1])
            grad = grad + jnp.dot(moe_wide.T, dlogits, precision=highest)
        segment_outs.append(jnp.stack(group_outs))
        grads.append(grad / (N_DP * GROUP))
    layer_out = jnp.stack(segment_outs)
    next_acts = jnp.roll(layer_out, 1, axis=0)
    carry = jnp.concatenate((layer_out[:1], memory[1:]), axis=0)
    memory_next = jnp.roll(carry, 1, axis=0)
    return (next_acts, memory_next, jnp.stack(grads))
```

```python
import jax
import jax.numpy as jnp
from jax import lax
from jax.experimental import pallas as pl
from jax.experimental.pallas import tpu as pltpu
from jax.sharding import PartitionSpec as P

HEAD_DIM = 128
TOP = 2
SEQ = 128


eps = 1e-05
highest = lax.Precision.HIGHEST


def from_behind(block, axis, distance):
    devices = range(lax.axis_size(axis))
    route = [((i - distance) % len(devices), i) for i in devices]
    return lax.ppermute(block, axis, route)


def layer_norm(values, gain):
    centered = values - jnp.mean(values, axis=-1, keepdims=True)
    variance = jnp.mean(centered * centered, axis=-1, keepdims=True)
    return centered * lax.rsqrt(variance + eps) * gain


def shards(
    x_in,
    memory,
    w_qkv,
    w_attn_out,
    norm_gains,
    router,
    w_in,
    w_exp_out,
    expert_ids,
    lengths,
    cotangent,
):
    segment_pos = lax.axis_index("segment")
    rows_here = x_in[0, 0]
    tok_dev = rows_here.shape[0]
    width = rows_here.shape[1]
    head_cols = w_attn_out.shape[1]
    gains = norm_gains[0]
    weights_qkv = w_qkv[0]
    normed = layer_norm(rows_here.astype(jnp.float32), gains[0]).astype(jnp.bfloat16)
    key_source = jnp.where(segment_pos == 0, normed, memory[0, 0])
    stacked = jnp.stack((normed, key_source), axis=0)
    piece = lax.all_gather(stacked, "expert", axis=1, tiled=True)
    query = jnp.dot(piece[0], weights_qkv[0], preferred_element_type=jnp.float32)
    keys = jnp.dot(piece[1], weights_qkv[1], preferred_element_type=jnp.float32)
    values = jnp.dot(piece[1], weights_qkv[2], preferred_element_type=jnp.float32)
    projected = jnp.concatenate((query, keys, values), axis=1).astype(jnp.bfloat16)
    group_rows = projected.shape[0]
    count = group_rows // SEQ
    heads_here = head_cols // HEAD_DIM
    shaped = projected.reshape(count, SEQ, 3, heads_here, HEAD_DIM)
    scores = jnp.einsum(
        "nihd,njhd->nhij", shaped[:, :, 0], shaped[:, :, 1], preferred_element_type=jnp.float32
    ) * HEAD_DIM ** (-0.5)
    live = (jnp.arange(SEQ)[None, :] < lengths[0, 0][:, None]).astype(jnp.float32)
    raised = jnp.exp(scores) * live[:, None, None, :]
    probs = (raised / jnp.sum(raised, axis=-1, keepdims=True)).astype(jnp.bfloat16)
    context = jnp.einsum(
        "nhij,njhd->nihd", probs, shaped[:, :, 2], preferred_element_type=jnp.float32
    )
    context = context.astype(jnp.bfloat16).reshape(group_rows, head_cols)
    attn_sum = lax.psum_scatter(
        jnp.dot(context, w_attn_out[0], preferred_element_type=jnp.float32).astype(jnp.bfloat16),
        "expert",
        scatter_dimension=0,
        tiled=True,
    ).astype(jnp.float32)
    resid = rows_here.astype(jnp.float32) + attn_sum
    moe_in = layer_norm(resid, gains[1]).astype(jnp.bfloat16)
    moe_wide = moe_in.astype(jnp.float32)
    logits = jnp.dot(moe_wide, router[0], precision=highest)
    ids = expert_ids[0, 0]
    n_exp = router.shape[2]
    pick_int = (ids[:, :, None] == jnp.arange(n_exp)[None, None, :]).astype(jnp.int32)
    pick = pick_int.astype(jnp.float32)
    chosen = jnp.sum(pick * logits[:, None, :], axis=2)
    gates = jax.nn.sigmoid(chosen - chosen[:, ::-1])
    flat_pick = pick_int.reshape(tok_dev * TOP, n_exp)
    assigned = flat_pick.shape[0]
    earlier = (jnp.arange(assigned)[:, None] > jnp.arange(assigned)[None, :]).astype(jnp.bfloat16)
    before = jnp.dot(
        earlier, flat_pick.astype(jnp.bfloat16), preferred_element_type=jnp.float32
    ).astype(jnp.int32)
    slot = jnp.sum(before * flat_pick, axis=1)
    capacity = tok_dev * TOP // n_exp
    target = ids.reshape(-1) * capacity + slot
    place = (jnp.arange(n_exp * capacity)[:, None] == target[None, :]).astype(jnp.bfloat16)
    place = jnp.sum(place.reshape(n_exp * capacity, tok_dev, TOP), axis=2)
    send_rows = jnp.dot(place, moe_in, preferred_element_type=jnp.float32).astype(jnp.bfloat16)
    copies = lax.axis_size("expert") // n_exp
    outgoing = jnp.broadcast_to(
        send_rows.reshape(n_exp, 1, capacity, width), (n_exp, copies, capacity, width)
    )
    outgoing = outgoing.reshape(n_exp * copies, capacity, width)
    arrived = lax.all_to_all(outgoing, "expert", split_axis=0, concat_axis=0, tiled=True)
    sources = arrived.shape[0]
    slots_now = arrived.shape[1]
    flat = arrived.reshape(sources * slots_now, width)
    hidden = jnp.maximum(jnp.dot(flat, w_in[0], preferred_element_type=jnp.float32), 0.0).astype(
        jnp.bfloat16
    )
    partial_value = jnp.dot(hidden, w_exp_out[0], preferred_element_type=jnp.float32).astype(
        jnp.bfloat16
    )
    returned = lax.all_to_all(
        partial_value.reshape(sources, slots_now, width),
        "expert",
        split_axis=0,
        concat_axis=0,
        tiled=True,
    )
    expert_out = jnp.sum(
        returned.reshape(n_exp, copies, capacity, width).astype(jnp.float32), axis=1
    )
    expert_out = expert_out.reshape(n_exp * capacity, width)
    selected = expert_out[target].reshape(tok_dev, TOP, width)
    mixed = jnp.sum(gates[:, :, None] * selected, axis=1)
    layer_out = (resid + mixed).astype(jnp.bfloat16)
    cot = cotangent[0, 0].astype(jnp.float32)
    intersection = jnp.sum(cot[:, None, :] * selected, axis=2)
    delta = gates[:, 0] * gates[:, 1] * (intersection[:, 0] - intersection[:, 1])
    dlogits = delta[:, None] * (pick[:, 0] - pick[:, 1])
    local_grad = lax.dot_general(moe_wide, dlogits, (((0,), (0,)), ((), ())), precision=highest)
    total_rows = tok_dev * lax.axis_size("expert") * lax.axis_size("dp")
    router_grad = (
        lax.psum(local_grad.astype(jnp.bfloat16), ("expert", "dp")).astype(jnp.float32) / total_rows
    )
    carry = jnp.where(segment_pos == 0, layer_out, memory[0, 0])
    handed = from_behind(jnp.stack((layer_out, carry), axis=0), "segment", 1)
    return (handed[0][None, None], handed[1][None, None], router_grad[None])


BF = jnp.bfloat16
F32 = jnp.float32
MESH = pl.DeviceIdType.MESH
HALF = 64
CHUNK = 512
DEPTH = 1024
STRIP = 256


def tick(
    x_hbm, mem_hbm, wqkv_hbm, wo_hbm, gains_hbm, router_hbm, win_hbm, wout_hbm, ids_hbm, lengths_hbm, cot_hbm,
    acts_out, memory_out, grad_out,
    gains, router_t, ids_t, lengths, wqkv, wo, win, wout, xv, rows, qkv, csend, crecv, resid, moe_in, cot,
    dsend, arr, acc, hidden, rsend, rrecv, lo, gsend, grecv,
    wsem, winsem, woutsem, ag_s, ag_r, c_s, c_r, d_s, d_r, r_s, r_r, z_s, z_r, g_s, g_r, m_s, m_r, small_sem, turn,
):
    seg = lax.axis_index("segment")
    exp = lax.axis_index("expert")
    dp = lax.axis_index("dp")
    n_seg = lax.axis_size("segment")
    following = lax.rem(seg + 1, n_seg)
    behind = lax.rem(seg + n_seg - 1, n_seg)
    col = lax.rem(exp, 2)
    row = exp // 2

    def peer(r):
        return lax.rem(col + r % 2, 2) + 2 * lax.rem(row + r // 2, 2)

    def send(src, dst, s, r, device):
        return pltpu.make_async_remote_copy(
            src_ref=src, dst_ref=dst, send_sem=s, recv_sem=r, device_id=device, device_id_type=MESH
        )

    local = [
        pltpu.make_async_copy(mem_hbm, rows.at[1, 0], wsem.at[0]),
        pltpu.make_async_copy(x_hbm, xv, wsem.at[1]),
        pltpu.make_async_copy(wqkv_hbm, wqkv, wsem.at[2]),
        pltpu.make_async_copy(wo_hbm, wo, wsem.at[3]),
        pltpu.make_async_copy(cot_hbm, cot, wsem.at[4]),
    ]
    small = [
        pltpu.make_async_copy(gains_hbm, gains, small_sem.at[0]),
        pltpu.make_async_copy(lengths_hbm, lengths, small_sem.at[1]),
        pltpu.make_async_copy(ids_hbm, ids_t, small_sem.at[2]),
        pltpu.make_async_copy(router_hbm, router_t, small_sem.at[3]),
    ]
    def win_copy(c):
        part = pl.ds(pl.multiple_of(c * CHUNK, CHUNK), CHUNK)
        return pltpu.make_async_copy(win_hbm.at[:, part], win.at[c], winsem.at[c])

    def wout_copy(c):
        part = pl.ds(pl.multiple_of(c * CHUNK, CHUNK), CHUNK)
        return pltpu.make_async_copy(wout_hbm.at[:, part], wout.at[c], woutsem.at[c])

    barrier = pltpu.get_barrier_semaphore()
    others = [(r, d) for r in range(4) for d in range(2) if r + d > 0]
    for r, d in others:
        pl.semaphore_signal(
            barrier, 1, device_id={"expert": peer(r), "dp": lax.rem(dp + d, 2)}, device_id_type=MESH
        )
    pl.semaphore_signal(barrier, 1, device_id={"segment": behind}, device_id_type=MESH)
    for copy in (local[0], local[1], small[0], small[1], *local[2:], *small[2:]):
        copy.start()

    top, low = pl.ds(0, HALF), pl.ds(HALF, HALF)

    def gather_copies(a):
        along_x, along_y = {"expert": peer(1)}, {"expert": peer(2)}
        plan = [
            (0, top, 1, along_x), (0, low, 1, along_x), (0, low, 2, along_y), (0, top, 2, along_y),
            (1, top, 3, along_y), (2, low, 3, along_x),
        ]
        return [
            send(rows.at[a, source, part], rows.at[a, slot, part], ag_s.at[a, i], ag_r.at[a, i], dev)
            for i, (source, part, slot, dev) in enumerate(plan)
        ]

    along_x, along_y = {"expert": peer(1)}, {"expert": peer(2)}
    plan = [
        (1, top, 1, along_x), (2, low, 2, along_y), (3, top, 0, along_x), (3, low, 0, along_y),
        (2, top, 2, along_y), (1, low, 1, along_x),
    ]
    shares = [
        send(csend.at[source, part], crecv.at[slot, part], c_s.at[i], c_r.at[i], dev)
        for i, (source, part, slot, dev) in enumerate(plan)
    ]
    norm_ag, mem_ag = gather_copies(0), gather_copies(1)
    mem_relay = send(rows.at[1, 0], memory_out, m_s.at[0], m_r.at[0], {"segment": following})

    local[0].wait()
    pl.semaphore_wait(barrier, len(others) + 1)
    own = (0, 2, 1, 3)

    @pl.when((seg != 0) & (dp == 0))
    def _():
        for i in own:
            mem_ag[i].start()
        mem_relay.start()

    local[1].wait()
    small[0].wait()

    def norm_rows(i, _):
        part = pl.ds(pl.multiple_of(i * 32, 32), 32)
        values = xv[part, :].astype(F32)
        normed = layer_norm(values, gains[0:1, :]).astype(BF)
        rows[0, 0, part, :] = normed

        @pl.when(seg == 0)
        def _():
            rows[1, 0, part, :] = normed

        return 0

    lax.fori_loop(0, 4, norm_rows, 0)

    @pl.when(dp == 0)
    def _():
        @pl.when(seg == 0)
        def _():
            for i in own:
                mem_ag[i].start()

        for i in own:
            norm_ag[i].start()

    def start_weights(c, _):
        win_copy(c).start()
        return 0

    def start_weights_out(c, _):
        wout_copy(c).start()
        return 0

    lax.fori_loop(0, win.shape[0], start_weights, 0)
    lax.fori_loop(0, wout.shape[0], start_weights_out, 0)

    @pl.when(dp == 0)
    def _():
        for i in own[0:4]:
            mem_ag[i].wait_send()
        pl.semaphore_signal(turn, 1, device_id={"dp": 1}, device_id_type=MESH)

    @pl.when(dp == 1)
    def _():
        pl.semaphore_wait(turn, 1)
        for i in own:
            mem_ag[i].start()
        for i in own:
            norm_ag[i].start()

        @pl.when(seg != 0)
        def _():
            mem_relay.start()

    local[2].wait()
    local[3].wait()
    small[1].wait()

    def section(r, _):
        @pl.when(r == 1)
        def _():
            mem_ag[0].wait_recv()
            mem_ag[4].start()
            mem_ag[2].wait_recv()
            mem_ag[5].start()
            norm_ag[0].wait_recv()
            norm_ag[4].start()
            norm_ag[2].wait_recv()
            norm_ag[5].start()
            mem_ag[1].wait_recv()
            norm_ag[1].wait_recv()

        @pl.when(r == 2)
        def _():
            mem_ag[3].wait_recv()
            norm_ag[3].wait_recv()

        @pl.when(r == 3)
        def _():
            for i in (4, 5):
                mem_ag[i].wait_recv()
                norm_ag[i].wait_recv()

        def project(j, _):
            got = jnp.dot(rows[(j + 1) // 2, r], wqkv[j], preferred_element_type=F32)
            qkv[j] = got.astype(BF)
            return 0

        lax.fori_loop(0, 3, project, 0)
        owner = peer(r)
        live = (lax.broadcasted_iota(jnp.int32, (1, SEQ), 1) < lengths[owner]).astype(F32)
        parts = []
        for h in range(wo.shape[0] // HEAD_DIM):
            cols = slice(h * HEAD_DIM, (h + 1) * HEAD_DIM)
            scores = lax.dot_general(
                qkv[0, :, cols], qkv[1, :, cols], (((1,), (1,)), ((), ())), preferred_element_type=F32
            ) * HEAD_DIM ** (-0.5)
            raised = jnp.exp(scores) * live
            probs = (raised / jnp.sum(raised, axis=-1, keepdims=True)).astype(BF)
            parts.append(jnp.dot(probs, qkv[2, :, cols], preferred_element_type=F32).astype(BF))
        context = jnp.concatenate(parts, axis=1)
        for c in range(4):
            cols = slice(c * CHUNK, (c + 1) * CHUNK)
            csend[r, :, cols] = jnp.dot(context, wo[:, cols], preferred_element_type=F32).astype(BF)

        @pl.when(r == 1)
        def _():
            shares[0].start()

        @pl.when(r == 2)
        def _():
            shares[1].start()

        @pl.when(r == 3)
        def _():
            shares[2].start()
            shares[3].start()

        return 0

    lax.fori_loop(0, 4, section, 0)

    tokens = SEQ
    small[2].wait()
    small[3].wait()
    first, second = ids_t[0:1, :], ids_t[1:2, :]
    earlier = (
        lax.broadcasted_iota(jnp.int32, (tokens, tokens), 0)
        < lax.broadcasted_iota(jnp.int32, (tokens, tokens), 1)
    ).astype(BF)
    place, pick0, pick1 = [], [], []
    slot_no = lax.broadcasted_iota(jnp.int32, (HALF, tokens), 0).astype(F32)
    for r in range(4):
        one = (first == peer(r)).astype(F32)
        two = (second == peer(r)).astype(F32)
        named = one + two
        slot = jnp.dot(
            jnp.broadcast_to(named, (16, tokens)).astype(BF), earlier, preferred_element_type=F32
        )[0:1, :]
        hit = (slot_no == slot).astype(F32)
        place.append((hit * named).astype(BF))
        pick0.append(hit * one)
        pick1.append(hit * two)
    back = jnp.concatenate(
        [jnp.concatenate(pick0, axis=0).T, jnp.concatenate(pick1, axis=0).T], axis=0
    ).astype(BF)

    for base, source, came, goes in ((0, 2, 2, 4), (HALF, 1, 3, 5)):
        shares[came].wait_recv()

        def join(i, _, base=base, source=source):
            part = pl.ds(pl.multiple_of(base + i * 32, 32), 32)
            both = csend[source, part, :].astype(F32) + crecv[0, part, :].astype(F32)
            csend[source, part, :] = both.astype(BF)
            return 0

        lax.fori_loop(0, HALF // 32, join, 0)
        shares[goes].start()
    for i in (0, 1, 4, 5):
        shares[i].wait_recv()

    def second_norm(i, _):
        part = pl.ds(pl.multiple_of(i * 32, 32), 32)
        total = csend[0, part, :].astype(F32)
        for r in (1, 2):
            total = total + crecv[r, part, :].astype(F32)
        values = xv[part, :].astype(F32) + total
        resid[part, :] = values
        moe_in[part, :] = layer_norm(values, gains[1:2, :]).astype(BF)
        return 0

    lax.fori_loop(0, 4, second_norm, 0)

    def dispatch(k, r):
        part = pl.ds(r * HALF, HALF)
        return send(dsend.at[k, part], arr.at[k, part], d_s.at[k, r], d_r.at[k, r], {"expert": peer(r)})

    placed = jnp.concatenate(place, axis=0)

    for k in range(arr.shape[0]):
        for j in range(DEPTH // CHUNK):
            cols = slice(k * DEPTH + j * CHUNK, k * DEPTH + (j + 1) * CHUNK)
            chosen = jnp.dot(placed, moe_in[:, cols], preferred_element_type=F32).astype(BF)
            dsend[k, :, j * CHUNK:(j + 1) * CHUNK] = chosen
            arr[k, 0:HALF, j * CHUNK:(j + 1) * CHUNK] = chosen[0:HALF, :]
        for r in (3, 1, 2):
            dispatch(k, r).start()

    logits = lax.dot_general(
        router_t[...], moe_in[...].astype(F32), (((1,), (1,)), ((), ())),
        precision=highest, preferred_element_type=F32,
    )
    chosen0 = jnp.zeros((1, tokens), F32)
    chosen1 = jnp.zeros((1, tokens), F32)
    for e in range(4):
        chosen0 = chosen0 + (first == e).astype(F32) * logits[e:e + 1, :]
        chosen1 = chosen1 + (second == e).astype(F32) * logits[e:e + 1, :]
    gate0 = jax.nn.sigmoid(chosen0 - chosen1)
    gate1 = jax.nn.sigmoid(chosen1 - chosen0)
    gate0 = jnp.broadcast_to(gate0, (tokens, tokens)).T[:, 0:1]
    gate1 = jnp.broadcast_to(gate1, (tokens, tokens)).T[:, 0:1]

    for r in (3, 1, 2):
        dispatch(0, r).wait_recv()

    def columns_first(c, _):
        win_copy(c).wait()
        acc[c] = jnp.dot(arr[0], win[c, 0:DEPTH, :], preferred_element_type=F32)
        return 0

    lax.fori_loop(0, win.shape[0], columns_first, 0)
    for r in (3, 1, 2):
        dispatch(1, r).wait_recv()

    def columns_last(c, _):
        got = jnp.dot(arr[1], win[c, DEPTH:2 * DEPTH, :], preferred_element_type=F32)
        cols = pl.ds(pl.multiple_of(c * CHUNK, CHUNK), CHUNK)
        hidden[:, cols] = jnp.maximum(acc[c] + got, 0.0).astype(BF)
        return 0

    lax.fori_loop(0, win.shape[0], columns_last, 0)

    def give_back(c, r):
        part = pl.ds(r * HALF, HALF)
        return send(rsend.at[c, part], rrecv.at[c, part], r_s.at[c, r], r_r.at[c, r], {"expert": peer(r)})

    def expert_out(c, _):
        wout_copy(c).wait()
        got = jnp.dot(hidden[...], wout[c], preferred_element_type=F32).astype(BF)
        for j in range(CHUNK // STRIP):
            strip = got[:, j * STRIP:(j + 1) * STRIP]
            n = c * (CHUNK // STRIP) + j
            rsend[n] = strip
            rrecv[n, 0:HALF, :] = strip[0:HALF, :]
            for r in (3, 1, 2):
                give_back(n, r).start()
        return 0

    lax.fori_loop(0, wout.shape[0], expert_out, 0)
    local[4].wait()

    def onward(c):
        cols = pl.ds(pl.multiple_of(c * STRIP, STRIP), STRIP)
        return send(lo.at[c], acts_out.at[:, cols], z_s.at[c], z_r.at[c], {"segment": following})

    def combine(c, gap):
        for r in (3, 1, 2):
            give_back(c, r).wait_recv()
        cols = pl.ds(pl.multiple_of(c * STRIP, STRIP), STRIP)
        both = jnp.dot(back, rrecv[c], preferred_element_type=F32)
        sel0, sel1 = both[0:tokens, :], both[tokens:2 * tokens, :]
        lo[c] = (resid[:, cols] + (gate0 * sel0 + gate1 * sel1)).astype(BF)
        onward(c).start()
        terms = cot[:, cols].astype(F32) * (sel0 - sel1)
        for j in range(STRIP // tokens):
            gap = gap + terms[:, j * tokens:(j + 1) * tokens]
        return gap

    strips = rsend.shape[0]
    gap = lax.fori_loop(0, strips, combine, jnp.zeros((tokens, tokens), F32))
    gap = jnp.sum(gap, axis=1, keepdims=True)
    delta = jnp.broadcast_to(gate0 * gate1 * gap, (tokens, tokens)).T[0:1, :]
    dlogits = [delta * ((first == e).astype(F32) - (second == e).astype(F32)) for e in range(4)]
    dlogits = jnp.concatenate(dlogits + [jnp.zeros((4, tokens), F32)], axis=0)
    grad = jnp.dot(
        dlogits, moe_in[...].astype(F32), precision=highest, preferred_element_type=F32
    )
    gsend[...] = jnp.concatenate(
        [grad[0:4, c * CHUNK:(c + 1) * CHUNK] for c in range(4)], axis=0
    ).astype(BF)

    def share(r, d):
        i = r * 2 + d
        device = {"expert": peer(r), "dp": lax.rem(dp + d, 2)}
        return send(gsend, grecv.at[i], g_s.at[i], g_r.at[i], device)

    for r, d in others:
        share(r, d).start()
    for r, d in others:
        share(r, d).wait_recv()
    total = gsend[...].astype(F32)
    for r, d in others:
        total = total + grecv[r * 2 + d].astype(F32)
    total = total / (tokens * lax.axis_size("expert") * lax.axis_size("dp"))
    for c in range(4):
        grad_out[:, c * CHUNK:(c + 1) * CHUNK] = total[c * 4:(c + 1) * 4, :]

    for i in range(6):
        norm_ag[i].wait_send()
    for i in (4, 5, *own[4:]):
        mem_ag[i].wait_send()

    @pl.when(dp == 1)
    def _():
        for i in own[0:4]:
            mem_ag[i].wait_send()

    for r in (1, 2, 3):
        for c in range(arr.shape[0]):
            dispatch(c, r).wait_send()
        for c in range(strips):
            give_back(c, r).wait_send()
    for copy in shares:
        copy.wait_send()
    for r, d in others:
        share(r, d).wait_send()
    for c in range(strips):
        onward(c).wait_send()
        onward(c).wait_recv()

    @pl.when(seg != 0)
    def _():
        mem_relay.wait_send()

    @pl.when(seg != 1)
    def _():
        mem_relay.wait_recv()


def hand_over(first_decoder, acts, kept, grad, acts_out, memory_out, grad_out):
    acts_out[...] = acts[...]
    memory_out[...] = jnp.where(first_decoder[0] == 1, acts[...], kept[...])
    grad_out[...] = grad[...]


def fused(
    x_in, memory, w_qkv, w_attn_out, norm_gains, router, w_in, w_exp_out, expert_ids, lengths, cotangent
):
    tokens, width = x_in.shape[2:]
    head_cols = w_attn_out.shape[1]
    hid = w_in.shape[2]
    n_in, n_out, strips, deep = hid // CHUNK, width // CHUNK, width // STRIP, width // DEPTH
    hbm = pl.BlockSpec(memory_space=pl.ANY)
    vmem = pl.BlockSpec(memory_space=pltpu.VMEM)
    smem = pl.BlockSpec(memory_space=pltpu.SMEM)
    dma = pltpu.SemaphoreType.DMA
    acts, kept, grad = pl.pallas_call(
        tick,
        out_shape=(
            jax.ShapeDtypeStruct((tokens, width), BF),
            jax.ShapeDtypeStruct((tokens, width), BF),
            jax.ShapeDtypeStruct((4, width), F32),
        ),
        in_specs=[hbm] * 11,
        out_specs=(hbm, hbm, vmem),
        scratch_shapes=[
            pltpu.VMEM((2, width), F32),
            pltpu.VMEM((4, width), F32),
            pltpu.VMEM((2, tokens), jnp.int32),
            pltpu.SMEM((4,), jnp.int32),
            pltpu.VMEM((3, width, head_cols), BF),
            pltpu.VMEM((head_cols, width), BF),
            pltpu.VMEM((n_in, width, CHUNK), BF),
            pltpu.VMEM((n_out, hid, CHUNK), BF),
            pltpu.VMEM((tokens, width), BF),
            pltpu.VMEM((2, 4, tokens, width), BF),
            pltpu.VMEM((3, tokens, head_cols), BF),
            pltpu.VMEM((4, tokens, width), BF),
            pltpu.VMEM((4, tokens, width), BF),
            pltpu.VMEM((tokens, width), F32),
            pltpu.VMEM((tokens, width), BF),
            pltpu.VMEM((tokens, width), BF),
            pltpu.VMEM((deep, 4 * HALF, DEPTH), BF),
            pltpu.VMEM((deep, 4 * HALF, DEPTH), BF),
            pltpu.VMEM((n_in, 4 * HALF, CHUNK), F32),
            pltpu.VMEM((4 * HALF, hid), BF),
            pltpu.VMEM((strips, 4 * HALF, STRIP), BF),
            pltpu.VMEM((strips, 4 * HALF, STRIP), BF),
            pltpu.VMEM((strips, tokens, STRIP), BF),
            pltpu.VMEM((16, CHUNK), BF),
            pltpu.VMEM((8, 16, CHUNK), BF),
            dma((5,)), dma((n_in,)), dma((n_out,)),
            dma((2, 6)), dma((2, 6)), dma((6,)), dma((6,)), dma((deep, 4)), dma((deep, 4)),
            dma((strips, 4)), dma((strips, 4)), dma((strips,)), dma((strips,)),
            dma((8,)), dma((8,)), dma((1,)), dma((1,)), dma((4,)), pltpu.SemaphoreType.REGULAR,
        ],
        compiler_params=pltpu.CompilerParams(
            collective_id=0, has_side_effects=True, vmem_limit_bytes=64 * 2**20 - 2**18
        ),
    )(
        x_in[0, 0], memory[0, 0], w_qkv[0], w_attn_out[0], norm_gains[0], router[0].T, w_in[0],
        w_exp_out[0], expert_ids[0, 0].T, lengths[0, 0], cotangent[0, 0],
    )
    first_decoder = (lax.axis_index("segment") == 1).astype(jnp.int32).reshape(1)
    acts, kept, grad = pl.pallas_call(
        hand_over,
        out_shape=(acts, kept, grad),
        in_specs=[smem, vmem, vmem, vmem],
        out_specs=(vmem, vmem, vmem),
    )(first_decoder, acts, kept, grad)
    return acts[None, None], kept[None, None], grad.T[None]


def solution(mesh):
    small = (mesh.shape["expert"], mesh.shape["dp"]) == (4, 2) and mesh.shape["segment"] > 2
    placed = (
        P("segment", "dp", "expert", None),
        P("segment", "dp", "expert", None),
        P("segment", None, None, "expert"),
        P("segment", "expert", None),
        P("segment", None, None),
        P("segment", None, None),
        P("segment", None, "expert"),
        P("segment", "expert", None),
        P("segment", "dp", "expert", None),
        P("segment", "dp", None),
        P("segment", "dp", "expert", None),
    )
    return jax.shard_map(
        fused if small else shards,
        mesh=mesh,
        in_specs=placed,
        out_specs=(
            P("segment", "dp", "expert", None),
            P("segment", "dp", "expert", None),
            P("segment", None, None),
        ),
        check_vma=False,
    )
```

```python
import jax
import jax.numpy as jnp
from jax import lax
from jax.experimental import pallas as pl
from jax.experimental.pallas import tpu as pltpu
from jax.sharding import PartitionSpec as P

HEAD_DIM = 128
TOP = 2
SEQ = 128


eps = 1e-05
highest = lax.Precision.HIGHEST


def from_behind(block, axis, distance):
    devices = range(lax.axis_size(axis))
    route = [((i - distance) % len(devices), i) for i in devices]
    return lax.ppermute(block, axis, route)


def layer_norm(values, gain):
    centered = values - jnp.mean(values, axis=-1, keepdims=True)
    variance = jnp.mean(centered * centered, axis=-1, keepdims=True)
    return centered * lax.rsqrt(variance + eps) * gain


def shards(
    x_in,
    memory,
    w_qkv,
    w_attn_out,
    norm_gains,
    router,
    w_in,
    w_exp_out,
    expert_ids,
    lengths,
    cotangent,
):
    segment_pos = lax.axis_index("segment")
    rows_here = x_in[0, 0]
    tok_dev = rows_here.shape[0]
    width = rows_here.shape[1]
    head_cols = w_attn_out.shape[1]
    gains = norm_gains[0]
    weights_qkv = w_qkv[0]
    normed = layer_norm(rows_here.astype(jnp.float32), gains[0]).astype(jnp.bfloat16)
    key_source = jnp.where(segment_pos == 0, normed, memory[0, 0])
    stacked = jnp.stack((normed, key_source), axis=0)
    piece = lax.all_gather(stacked, "expert", axis=1, tiled=True)
    query = jnp.dot(piece[0], weights_qkv[0], preferred_element_type=jnp.float32)
    keys = jnp.dot(piece[1], weights_qkv[1], preferred_element_type=jnp.float32)
    values = jnp.dot(piece[1], weights_qkv[2], preferred_element_type=jnp.float32)
    projected = jnp.concatenate((query, keys, values), axis=1).astype(jnp.bfloat16)
    group_rows = projected.shape[0]
    count = group_rows // SEQ
    heads_here = head_cols // HEAD_DIM
    shaped = projected.reshape(count, SEQ, 3, heads_here, HEAD_DIM)
    scores = jnp.einsum(
        "nihd,njhd->nhij", shaped[:, :, 0], shaped[:, :, 1], preferred_element_type=jnp.float32
    ) * HEAD_DIM ** (-0.5)
    live = (jnp.arange(SEQ)[None, :] < lengths[0, 0][:, None]).astype(jnp.float32)
    raised = jnp.exp(scores) * live[:, None, None, :]
    probs = (raised / jnp.sum(raised, axis=-1, keepdims=True)).astype(jnp.bfloat16)
    context = jnp.einsum(
        "nhij,njhd->nihd", probs, shaped[:, :, 2], preferred_element_type=jnp.float32
    )
    context = context.astype(jnp.bfloat16).reshape(group_rows, head_cols)
    attn_sum = lax.psum_scatter(
        jnp.dot(context, w_attn_out[0], preferred_element_type=jnp.float32).astype(jnp.bfloat16),
        "expert",
        scatter_dimension=0,
        tiled=True,
    ).astype(jnp.float32)
    resid = rows_here.astype(jnp.float32) + attn_sum
    moe_in = layer_norm(resid, gains[1]).astype(jnp.bfloat16)
    moe_wide = moe_in.astype(jnp.float32)
    logits = jnp.dot(moe_wide, router[0], precision=highest)
    ids = expert_ids[0, 0]
    n_exp = router.shape[2]
    pick_int = (ids[:, :, None] == jnp.arange(n_exp)[None, None, :]).astype(jnp.int32)
    pick = pick_int.astype(jnp.float32)
    chosen = jnp.sum(pick * logits[:, None, :], axis=2)
    gates = jax.nn.sigmoid(chosen - chosen[:, ::-1])
    flat_pick = pick_int.reshape(tok_dev * TOP, n_exp)
    assigned = flat_pick.shape[0]
    earlier = (jnp.arange(assigned)[:, None] > jnp.arange(assigned)[None, :]).astype(jnp.bfloat16)
    before = jnp.dot(
        earlier, flat_pick.astype(jnp.bfloat16), preferred_element_type=jnp.float32
    ).astype(jnp.int32)
    slot = jnp.sum(before * flat_pick, axis=1)
    capacity = tok_dev * TOP // n_exp
    target = ids.reshape(-1) * capacity + slot
    place = (jnp.arange(n_exp * capacity)[:, None] == target[None, :]).astype(jnp.bfloat16)
    place = jnp.sum(place.reshape(n_exp * capacity, tok_dev, TOP), axis=2)
    send_rows = jnp.dot(place, moe_in, preferred_element_type=jnp.float32).astype(jnp.bfloat16)
    copies = lax.axis_size("expert") // n_exp
    outgoing = jnp.broadcast_to(
        send_rows.reshape(n_exp, 1, capacity, width), (n_exp, copies, capacity, width)
    )
    outgoing = outgoing.reshape(n_exp * copies, capacity, width)
    arrived = lax.all_to_all(outgoing, "expert", split_axis=0, concat_axis=0, tiled=True)
    sources = arrived.shape[0]
    slots_now = arrived.shape[1]
    flat = arrived.reshape(sources * slots_now, width)
    hidden = jnp.maximum(jnp.dot(flat, w_in[0], preferred_element_type=jnp.float32), 0.0).astype(
        jnp.bfloat16
    )
    partial_value = jnp.dot(hidden, w_exp_out[0], preferred_element_type=jnp.float32).astype(
        jnp.bfloat16
    )
    returned = lax.all_to_all(
        partial_value.reshape(sources, slots_now, width),
        "expert",
        split_axis=0,
        concat_axis=0,
        tiled=True,
    )
    expert_out = jnp.sum(
        returned.reshape(n_exp, copies, capacity, width).astype(jnp.float32), axis=1
    )
    expert_out = expert_out.reshape(n_exp * capacity, width)
    selected = expert_out[target].reshape(tok_dev, TOP, width)
    mixed = jnp.sum(gates[:, :, None] * selected, axis=1)
    layer_out = (resid + mixed).astype(jnp.bfloat16)
    cot = cotangent[0, 0].astype(jnp.float32)
    intersection = jnp.sum(cot[:, None, :] * selected, axis=2)
    delta = gates[:, 0] * gates[:, 1] * (intersection[:, 0] - intersection[:, 1])
    dlogits = delta[:, None] * (pick[:, 0] - pick[:, 1])
    local_grad = lax.dot_general(moe_wide, dlogits, (((0,), (0,)), ((), ())), precision=highest)
    total_rows = tok_dev * lax.axis_size("expert") * lax.axis_size("dp")
    router_grad = (
        lax.psum(local_grad.astype(jnp.bfloat16), ("expert", "dp")).astype(jnp.float32) / total_rows
    )
    carry = jnp.where(segment_pos == 0, layer_out, memory[0, 0])
    handed = from_behind(jnp.stack((layer_out, carry), axis=0), "segment", 1)
    return (handed[0][None, None], handed[1][None, None], router_grad[None])


BF = jnp.bfloat16
F32 = jnp.float32
MESH = pl.DeviceIdType.MESH
HALF = 64
CHUNK = 512
DEPTH = 1024
STRIP = 256
WIDE = 1024


def tick(
    x_hbm, mem_hbm, wqkv_hbm, wo_hbm, gains_hbm, router_hbm, win_hbm, wout_hbm, ids_hbm, lengths_hbm, cot_hbm,
    acts_out, memory_out, grad_out,
    gains, router_t, ids_t, lengths, wqkv, wo, win, wout, xv, rows, qkv, csend, crecv, resid, moe_in, cot,
    dsend, arr, acc, hidden, rsend, rrecv, lo, gsend, grecv,
    wsem, winsem, woutsem, ag_s, ag_r, c_s, c_r, d_s, d_r, r_s, r_r, z_s, z_r, g_s, g_r, m_s, m_r, small_sem, turn, grad_here,
):
    seg = lax.axis_index("segment")
    exp = lax.axis_index("expert")
    dp = lax.axis_index("dp")
    n_seg = lax.axis_size("segment")
    following = lax.rem(seg + 1, n_seg)
    behind = lax.rem(seg + n_seg - 1, n_seg)
    col = lax.rem(exp, 2)
    row = exp // 2

    def peer(r):
        return lax.rem(col + r % 2, 2) + 2 * lax.rem(row + r // 2, 2)

    def send(src, dst, s, r, device):
        return pltpu.make_async_remote_copy(
            src_ref=src, dst_ref=dst, send_sem=s, recv_sem=r, device_id=device, device_id_type=MESH
        )

    local = [
        pltpu.make_async_copy(mem_hbm, rows.at[1, 0], wsem.at[0]),
        pltpu.make_async_copy(x_hbm, xv, wsem.at[1]),
        pltpu.make_async_copy(wqkv_hbm, wqkv, wsem.at[2]),
        pltpu.make_async_copy(wo_hbm, wo, wsem.at[3]),
        pltpu.make_async_copy(cot_hbm, cot, wsem.at[4]),
    ]
    small = [
        pltpu.make_async_copy(gains_hbm, gains, small_sem.at[0]),
        pltpu.make_async_copy(lengths_hbm, lengths, small_sem.at[1]),
        pltpu.make_async_copy(ids_hbm, ids_t, small_sem.at[2]),
        pltpu.make_async_copy(router_hbm, router_t, small_sem.at[3]),
    ]
    def win_copy(c):
        part = pl.ds(pl.multiple_of(c * WIDE, WIDE), WIDE)
        return pltpu.make_async_copy(win_hbm.at[:, part], win.at[c], winsem.at[c])

    def wout_copy(c):
        part = pl.ds(pl.multiple_of(c * CHUNK, CHUNK), CHUNK)
        return pltpu.make_async_copy(wout_hbm.at[:, part], wout.at[c], woutsem.at[c])

    barrier = pltpu.get_barrier_semaphore()
    others = [(r, d) for r in range(4) for d in range(2) if r + d > 0]
    for r, d in others:
        pl.semaphore_signal(
            barrier, 1, device_id={"expert": peer(r), "dp": lax.rem(dp + d, 2)}, device_id_type=MESH
        )
    pl.semaphore_signal(barrier, 1, device_id={"segment": behind}, device_id_type=MESH)
    for copy in (local[0], local[1], small[0], small[1], *local[2:], *small[2:]):
        copy.start()

    top, low = pl.ds(0, HALF), pl.ds(HALF, HALF)

    def gather_copies(a):
        along_x, along_y = {"expert": peer(1)}, {"expert": peer(2)}
        plan = [
            (0, top, 1, along_x), (0, low, 1, along_x), (0, low, 2, along_y), (0, top, 2, along_y),
            (1, top, 3, along_y), (2, low, 3, along_x),
        ]
        return [
            send(rows.at[a, source, part], rows.at[a, slot, part], ag_s.at[a, i], ag_r.at[a, i], dev)
            for i, (source, part, slot, dev) in enumerate(plan)
        ]

    along_x, along_y = {"expert": peer(1)}, {"expert": peer(2)}
    plan = [
        (1, top, 1, along_x), (2, low, 2, along_y), (3, top, 0, along_x), (3, low, 0, along_y),
        (2, top, 2, along_y), (1, low, 1, along_x),
    ]
    shares = [
        send(csend.at[source, part], crecv.at[slot, part], c_s.at[i], c_r.at[i], dev)
        for i, (source, part, slot, dev) in enumerate(plan)
    ]
    norm_ag, mem_ag = gather_copies(0), gather_copies(1)
    mem_relay = send(rows.at[1, 0], memory_out, m_s.at[0], m_r.at[0], {"segment": following})

    local[0].wait()
    pl.semaphore_wait(barrier, len(others) + 1)
    early, late = (0, 2), (1, 3)

    @pl.when((seg != 0) & (dp == 0))
    def _():
        for i in early:
            mem_ag[i].start()

    local[1].wait()
    small[0].wait()

    def norm_rows(i, _):
        part = pl.ds(pl.multiple_of(i * 32, 32), 32)
        values = xv[part, :].astype(F32)
        normed = layer_norm(values, gains[0:1, :]).astype(BF)
        rows[0, 0, part, :] = normed

        @pl.when(seg == 0)
        def _():
            rows[1, 0, part, :] = normed

        return 0

    lax.fori_loop(0, 4, norm_rows, 0)

    @pl.when((seg == 0) & (dp == 0))
    def _():
        for i in early:
            mem_ag[i].start()

    @pl.when((dp == 0))
    def _():
        for i in early:
            norm_ag[i].start()

    def start_weights(c, _):
        win_copy(c).start()
        return 0

    def start_weights_out(c, _):
        wout_copy(c).start()
        return 0

    lax.fori_loop(0, win.shape[0], start_weights, 0)
    lax.fori_loop(0, wout.shape[0], start_weights_out, 0)

    @pl.when(dp == 0)
    def _():
        for i in early:
            mem_ag[i].wait_send()
        pl.semaphore_signal(turn, 1, device_id={"dp": 1}, device_id_type=MESH)

    @pl.when(dp == 1)
    def _():
        pl.semaphore_wait(turn, 1)
        for i in early:
            mem_ag[i].start()
        for i in early:
            norm_ag[i].start()

    local[2].wait()
    local[3].wait()
    small[1].wait()

    tokens = SEQ
    small[2].wait()
    first, second = ids_t[0:1, :], ids_t[1:2, :]
    earlier = (
        lax.broadcasted_iota(jnp.int32, (tokens, tokens), 0)
        < lax.broadcasted_iota(jnp.int32, (tokens, tokens), 1)
    ).astype(BF)
    place, pick0, pick1 = [], [], []
    slot_no = lax.broadcasted_iota(jnp.int32, (HALF, tokens), 0).astype(F32)
    for r in range(4):
        one = (first == peer(r)).astype(F32)
        two = (second == peer(r)).astype(F32)
        named = one + two
        slot = jnp.dot(
            jnp.broadcast_to(named, (16, tokens)).astype(BF), earlier, preferred_element_type=F32
        )[0:1, :]
        hit = (slot_no == slot).astype(F32)
        place.append((hit * named).astype(BF))
        pick0.append(hit * one)
        pick1.append(hit * two)
    back = jnp.concatenate(
        [jnp.concatenate(pick0, axis=0).T, jnp.concatenate(pick1, axis=0).T], axis=0
    ).astype(BF)

    def project(r, j):
        got = jnp.dot(rows[(j + 1) // 2, r], wqkv[j], preferred_element_type=F32)
        qkv[r, j] = got.astype(BF)

    def section(step, _):
        r = (lax.rem(step + 1, 3) + 1) * ((step + 2) // 3)

        @pl.when(step == 1)
        def _():
            for i in early:
                mem_ag[i].wait_recv()
                mem_ag[4 + i // 2].start()
            for i in early:
                norm_ag[i].wait_recv()
                norm_ag[4 + i // 2].start()
            for i in late:
                mem_ag[i].start()
            for i in late:
                norm_ag[i].start()

            @pl.when(seg != 0)
            def _():
                mem_relay.start()

            for i in (4, 5):
                mem_ag[i].wait_recv()
                norm_ag[i].wait_recv()

        @pl.when(step == 2)
        def _():
            for i in late:
                mem_ag[i].wait_recv()

            def keys_values(n, _):
                project(1 + n // 2, 1 + lax.rem(n, 2))
                return 0

            lax.fori_loop(0, 4, keys_values, 0)
            for i in late:
                norm_ag[i].wait_recv()

        def project_step(j, _):
            project(r, j)
            return 0

        lax.fori_loop(0, 3 - 2 * (step // 2), project_step, 0)
        owner = peer(r)
        live = (lax.broadcasted_iota(jnp.int32, (1, SEQ), 1) < lengths[owner]).astype(F32)
        parts = []
        for h in range(wo.shape[0] // HEAD_DIM):
            cols = slice(h * HEAD_DIM, (h + 1) * HEAD_DIM)
            scores = lax.dot_general(
                qkv[r, 0, :, cols], qkv[r, 1, :, cols], (((1,), (1,)), ((), ())), preferred_element_type=F32
            ) * HEAD_DIM ** (-0.5)
            raised = jnp.exp(scores) * live
            probs = (raised / jnp.sum(raised, axis=-1, keepdims=True)).astype(BF)
            parts.append(jnp.dot(probs, qkv[r, 2, :, cols], preferred_element_type=F32).astype(BF))
        context = jnp.concatenate(parts, axis=1)
        for c in range(4):
            cols = slice(c * CHUNK, (c + 1) * CHUNK)
            csend[r, :, cols] = jnp.dot(context, wo[:, cols], preferred_element_type=F32).astype(BF)

        @pl.when(step == 1)
        def _():
            shares[2].start()
            shares[3].start()

        @pl.when(step == 2)
        def _():
            shares[0].start()

        @pl.when(step == 3)
        def _():
            shares[1].start()

        return 0

    lax.fori_loop(0, 4, section, 0)

    for base, source, came, goes in ((HALF, 1, 3, 5), (0, 2, 2, 4)):
        shares[came].wait_recv()

        def join(i, _, base=base, source=source):
            part = pl.ds(pl.multiple_of(base + i * 32, 32), 32)
            both = csend[source, part, :].astype(F32) + crecv[0, part, :].astype(F32)
            csend[source, part, :] = both.astype(BF)
            return 0

        lax.fori_loop(0, HALF // 32, join, 0)
        shares[goes].start()
    def second_norm(i, _):
        part = pl.ds(pl.multiple_of(i * 32, 32), 32)
        total = csend[0, part, :].astype(F32)
        for r in (1, 2):
            total = total + crecv[r, part, :].astype(F32)
        values = xv[part, :].astype(F32) + total
        resid[part, :] = values
        moe_in[part, :] = layer_norm(values, gains[1:2, :]).astype(BF)
        return 0

    def finish(half, _):
        @pl.when(half == 0)
        def _():
            shares[1].wait_recv()
            shares[5].wait_recv()

        @pl.when(half == 1)
        def _():
            shares[0].wait_recv()
            shares[4].wait_recv()

        lax.fori_loop(2 - 2 * half, 4 - 2 * half, second_norm, 0)
        return 0

    lax.fori_loop(0, 2, finish, 0)

    def dispatch(k, r):
        part = pl.ds(r * HALF, HALF)
        return send(dsend.at[k, part], arr.at[k, part], d_s.at[k, r], d_r.at[k, r], {"expert": peer(r)})

    placed = jnp.concatenate(place, axis=0)

    for k in range(arr.shape[0]):
        for j in range(DEPTH // CHUNK):
            cols = slice(k * DEPTH + j * CHUNK, k * DEPTH + (j + 1) * CHUNK)
            chosen = jnp.dot(placed, moe_in[:, cols], preferred_element_type=F32).astype(BF)
            dsend[k, :, j * CHUNK:(j + 1) * CHUNK] = chosen
            arr[k, 0:HALF, j * CHUNK:(j + 1) * CHUNK] = chosen[0:HALF, :]
        if k == 0:
            @pl.when(dp == 1)
            def _():
                pl.semaphore_wait(turn, 1)

        for r in (3, 1, 2):
            dispatch(k, r).start()

    small[3].wait()
    logits = lax.dot_general(
        router_t[...], moe_in[...].astype(F32), (((1,), (1,)), ((), ())),
        precision=highest, preferred_element_type=F32,
    )
    chosen0 = jnp.zeros((1, tokens), F32)
    chosen1 = jnp.zeros((1, tokens), F32)
    for e in range(4):
        chosen0 = chosen0 + (first == e).astype(F32) * logits[e:e + 1, :]
        chosen1 = chosen1 + (second == e).astype(F32) * logits[e:e + 1, :]
    gate0 = jax.nn.sigmoid(chosen0 - chosen1)
    gate1 = jax.nn.sigmoid(chosen1 - chosen0)
    slope = gate0 * gate1
    gate0 = jnp.broadcast_to(gate0, (tokens, tokens)).T[:, 0:1]
    gate1 = jnp.broadcast_to(gate1, (tokens, tokens)).T[:, 0:1]

    for r in (3, 1, 2):
        dispatch(0, r).wait_recv()

    @pl.when(dp == 0)
    def _():
        pl.semaphore_signal(turn, 1, device_id={"dp": 1}, device_id_type=MESH)

    def columns_first(c, _):
        win_copy(c).wait()
        acc[c] = jnp.dot(arr[0], win[c, 0:DEPTH, :], preferred_element_type=F32)
        return 0

    lax.fori_loop(0, win.shape[0], columns_first, 0)
    for r in (3, 1, 2):
        dispatch(1, r).wait_recv()

    def columns_last(c, _):
        got = jnp.dot(arr[1], win[c, DEPTH:2 * DEPTH, :], preferred_element_type=F32)
        cols = pl.ds(pl.multiple_of(c * WIDE, WIDE), WIDE)
        hidden[:, cols] = jnp.maximum(acc[c] + got, 0.0).astype(BF)
        return 0

    lax.fori_loop(0, win.shape[0], columns_last, 0)

    def give_back(c, r):
        part = pl.ds(r * HALF, HALF)
        return send(rsend.at[c, part], rrecv.at[c, part], r_s.at[c, r], r_r.at[c, r], {"expert": peer(r)})

    def expert_out(c, _):
        wout_copy(c).wait()
        got = jnp.dot(hidden[...], wout[c], preferred_element_type=F32).astype(BF)
        for j in range(CHUNK // STRIP):
            strip = got[:, j * STRIP:(j + 1) * STRIP]
            n = c * (CHUNK // STRIP) + j
            rsend[n] = strip
            rrecv[n, 0:HALF, :] = strip[0:HALF, :]
            for r in (3, 1, 2):
                give_back(n, r).start()
        return 0

    lax.fori_loop(0, wout.shape[0], expert_out, 0)
    local[4].wait()

    def onward(c):
        cols = pl.ds(pl.multiple_of(c * STRIP, STRIP), STRIP)
        return send(lo.at[c], acts_out.at[:, cols], z_s.at[c], z_r.at[c], {"segment": following})

    def combine(c, gap):
        for r in (3, 1, 2):
            give_back(c, r).wait_recv()
        cols = pl.ds(pl.multiple_of(c * STRIP, STRIP), STRIP)
        both = jnp.dot(back, rrecv[c], preferred_element_type=F32)
        sel0, sel1 = both[0:tokens, :], both[tokens:2 * tokens, :]
        lo[c] = (resid[:, cols] + (gate0 * sel0 + gate1 * sel1)).astype(BF)
        onward(c).start()
        terms = cot[:, cols].astype(F32) * (sel0 - sel1)
        for j in range(STRIP // tokens):
            gap = gap + terms[:, j * tokens:(j + 1) * tokens]
        return gap

    strips = rsend.shape[0]
    gap = lax.fori_loop(0, strips, combine, jnp.zeros((tokens, tokens), F32))
    gap_row = jnp.zeros((16, tokens), F32)
    for _ in range(3):
        part = gap.astype(BF)
        gap = gap - part.astype(F32)
        gap_row = gap_row + lax.dot_general(
            jnp.ones((16, tokens), BF), part, (((1,), (1,)), ((), ())), preferred_element_type=F32
        )
    delta = slope * gap_row[0:1, :]
    rest = jnp.concatenate(
        [delta * ((first == e).astype(F32) - (second == e).astype(F32)) for e in range(4)], axis=0
    )
    terms = []
    for _ in range(3):
        terms.append(rest.astype(BF))
        rest = rest - terms[-1].astype(F32)
    terms = jnp.concatenate([term.astype(F32) for term in terms] + [jnp.zeros((4, tokens), F32)], axis=0)
    products = jnp.dot(terms.astype(BF), moe_in[...], preferred_element_type=F32)
    grad = products[0:4, :] + products[4:8, :] + products[8:12, :]
    gsend[...] = jnp.concatenate(
        [grad[0:4, c * CHUNK:(c + 1) * CHUNK] for c in range(4)], axis=0
    ).astype(BF)

    def share(r, d):
        i = r * 2 + d
        device = {"expert": peer(r), "dp": lax.rem(dp + d, 2)}
        return send(gsend, grecv.at[i], g_s.at[i], g_r.at[i], device)

    for r, d in others:
        share(r, d).start()
    @pl.when(seg != 0)
    def _():
        mem_relay.wait_send()

    @pl.when(seg != 1)
    def _():
        mem_relay.wait_recv()

    for i in (1, 3, 4, 5):
        mem_ag[i].wait_send()
        norm_ag[i].wait_send()

    @pl.when(dp == 1)
    def _():
        for i in early:
            mem_ag[i].wait_send()

    for i in early:
        norm_ag[i].wait_send()

    for r in (1, 2, 3):
        for c in range(arr.shape[0]):
            dispatch(c, r).wait_send()
        for c in range(strips):
            give_back(c, r).wait_send()
    for copy in shares:
        copy.wait_send()
    def drain(c, _):
        onward(c).wait_send()
        onward(c).wait_recv()
        return 0

    lax.fori_loop(0, strips - 1, drain, 0)
    for r, d in others:
        share(r, d).wait_recv()
    total = gsend[...].astype(F32)
    for r, d in others:
        total = total + grecv[r * 2 + d].astype(F32)
    total = total / (tokens * lax.axis_size("expert") * lax.axis_size("dp"))
    for c in range(4):
        grad_here[:, c * CHUNK:(c + 1) * CHUNK] = total[c * 4:(c + 1) * 4, :]

    for r, d in others:
        share(r, d).wait_send()
    done = pltpu.make_async_copy(grad_here, grad_out, small_sem.at[0])
    done.start()
    drain(strips - 1, 0)
    done.wait()


def hand_over(first_decoder, acts, kept, grad, acts_out, memory_out, grad_out):
    acts_out[...] = acts[...]
    memory_out[...] = jnp.where(first_decoder[0] == 1, acts[...], kept[...])
    grad_out[...] = grad[...]


def fused(
    x_in, memory, w_qkv, w_attn_out, norm_gains, router, w_in, w_exp_out, expert_ids, lengths, cotangent
):
    tokens, width = x_in.shape[2:]
    head_cols = w_attn_out.shape[1]
    hid = w_in.shape[2]
    n_in, n_out, strips, deep = hid // WIDE, width // CHUNK, width // STRIP, width // DEPTH
    hbm = pl.BlockSpec(memory_space=pl.ANY)
    vmem = pl.BlockSpec(memory_space=pltpu.VMEM)
    smem = pl.BlockSpec(memory_space=pltpu.SMEM)
    dma = pltpu.SemaphoreType.DMA
    acts, kept, grad = pl.pallas_call(
        tick,
        out_shape=(
            jax.ShapeDtypeStruct((tokens, width), BF),
            jax.ShapeDtypeStruct((tokens, width), BF),
            jax.ShapeDtypeStruct((4, width), F32),
        ),
        in_specs=[hbm] * 11,
        out_specs=(hbm, hbm, hbm),
        scratch_shapes=[
            pltpu.VMEM((2, width), F32),
            pltpu.VMEM((4, width), F32),
            pltpu.VMEM((2, tokens), jnp.int32),
            pltpu.SMEM((4,), jnp.int32),
            pltpu.VMEM((3, width, head_cols), BF),
            pltpu.VMEM((head_cols, width), BF),
            pltpu.VMEM((n_in, width, WIDE), BF),
            pltpu.VMEM((n_out, hid, CHUNK), BF),
            pltpu.VMEM((tokens, width), BF),
            pltpu.VMEM((2, 4, tokens, width), BF),
            pltpu.VMEM((4, 3, tokens, head_cols), BF),
            pltpu.VMEM((4, tokens, width), BF),
            pltpu.VMEM((3, tokens, width), BF),
            pltpu.VMEM((tokens, width), F32),
            pltpu.VMEM((tokens, width), BF),
            pltpu.VMEM((tokens, width), BF),
            pltpu.VMEM((deep, 4 * HALF, DEPTH), BF),
            pltpu.VMEM((deep, 4 * HALF, DEPTH), BF),
            pltpu.VMEM((n_in, 4 * HALF, WIDE), F32),
            pltpu.VMEM((4 * HALF, hid), BF),
            pltpu.VMEM((strips, 4 * HALF, STRIP), BF),
            pltpu.VMEM((strips, 4 * HALF, STRIP), BF),
            pltpu.VMEM((strips, tokens, STRIP), BF),
            pltpu.VMEM((16, CHUNK), BF),
            pltpu.VMEM((8, 16, CHUNK), BF),
            dma((5,)), dma((n_in,)), dma((n_out,)),
            dma((2, 6)), dma((2, 6)), dma((6,)), dma((6,)), dma((deep, 4)), dma((deep, 4)),
            dma((strips, 4)), dma((strips, 4)), dma((strips,)), dma((strips,)),
            dma((8,)), dma((8,)), dma((1,)), dma((1,)), dma((4,)), pltpu.SemaphoreType.REGULAR,
            pltpu.VMEM((4, width), F32),
        ],
        compiler_params=pltpu.CompilerParams(
            collective_id=0, has_side_effects=True, vmem_limit_bytes=64 * 2**20 - 2**18
        ),
    )(
        x_in[0, 0], memory[0, 0], w_qkv[0], w_attn_out[0], norm_gains[0], router[0].T, w_in[0],
        w_exp_out[0], expert_ids[0, 0].T, lengths[0, 0], cotangent[0, 0],
    )
    first_decoder = (lax.axis_index("segment") == 1).astype(jnp.int32).reshape(1)
    acts, kept, grad = pl.pallas_call(
        hand_over,
        out_shape=(acts, kept, grad),
        in_specs=[smem, vmem, vmem, vmem],
        out_specs=(vmem, vmem, vmem),
    )(first_decoder, acts, kept, grad)
    return acts[None, None], kept[None, None], grad.T[None]


def solution(mesh):
    small = (mesh.shape["expert"], mesh.shape["dp"]) == (4, 2) and mesh.shape["segment"] > 2
    placed = (
        P("segment", "dp", "expert", None),
        P("segment", "dp", "expert", None),
        P("segment", None, None, "expert"),
        P("segment", "expert", None),
        P("segment", None, None),
        P("segment", None, None),
        P("segment", None, "expert"),
        P("segment", "expert", None),
        P("segment", "dp", "expert", None),
        P("segment", "dp", None),
        P("segment", "dp", "expert", None),
    )
    return jax.shard_map(
        fused if small else shards,
        mesh=mesh,
        in_specs=placed,
        out_specs=(
            P("segment", "dp", "expert", None),
            P("segment", "dp", "expert", None),
            P("segment", None, None),
        ),
        check_vma=False,
    )
```

```python
import jax
import jax.numpy as jnp
from jax import lax
from jax.experimental import pallas as pl
from jax.experimental.pallas import tpu as pltpu
from jax.sharding import PartitionSpec as P

HEAD_DIM = 128
TOP = 2
SEQ = 128


eps = 1e-05
highest = lax.Precision.HIGHEST


def from_behind(block, axis, distance):
    devices = range(lax.axis_size(axis))
    route = [((i - distance) % len(devices), i) for i in devices]
    return lax.ppermute(block, axis, route)


def layer_norm(values, gain):
    centered = values - jnp.mean(values, axis=-1, keepdims=True)
    variance = jnp.mean(centered * centered, axis=-1, keepdims=True)
    return centered * lax.rsqrt(variance + eps) * gain


def shards(
    x_in,
    memory,
    w_qkv,
    w_attn_out,
    norm_gains,
    router,
    w_in,
    w_exp_out,
    expert_ids,
    lengths,
    cotangent,
):
    segment_pos = lax.axis_index("segment")
    rows_here = x_in[0, 0]
    tok_dev = rows_here.shape[0]
    width = rows_here.shape[1]
    head_cols = w_attn_out.shape[1]
    gains = norm_gains[0]
    weights_qkv = w_qkv[0]
    normed = layer_norm(rows_here.astype(jnp.float32), gains[0]).astype(jnp.bfloat16)
    key_source = jnp.where(segment_pos == 0, normed, memory[0, 0])
    stacked = jnp.stack((normed, key_source), axis=0)
    piece = lax.all_gather(stacked, "expert", axis=1, tiled=True)
    query = jnp.dot(piece[0], weights_qkv[0], preferred_element_type=jnp.float32)
    keys = jnp.dot(piece[1], weights_qkv[1], preferred_element_type=jnp.float32)
    values = jnp.dot(piece[1], weights_qkv[2], preferred_element_type=jnp.float32)
    projected = jnp.concatenate((query, keys, values), axis=1).astype(jnp.bfloat16)
    group_rows = projected.shape[0]
    count = group_rows // SEQ
    heads_here = head_cols // HEAD_DIM
    shaped = projected.reshape(count, SEQ, 3, heads_here, HEAD_DIM)
    scores = jnp.einsum(
        "nihd,njhd->nhij", shaped[:, :, 0], shaped[:, :, 1], preferred_element_type=jnp.float32
    ) * HEAD_DIM ** (-0.5)
    live = (jnp.arange(SEQ)[None, :] < lengths[0, 0][:, None]).astype(jnp.float32)
    raised = jnp.exp(scores) * live[:, None, None, :]
    probs = (raised / jnp.sum(raised, axis=-1, keepdims=True)).astype(jnp.bfloat16)
    context = jnp.einsum(
        "nhij,njhd->nihd", probs, shaped[:, :, 2], preferred_element_type=jnp.float32
    )
    context = context.astype(jnp.bfloat16).reshape(group_rows, head_cols)
    attn_sum = lax.psum_scatter(
        jnp.dot(context, w_attn_out[0], preferred_element_type=jnp.float32).astype(jnp.bfloat16),
        "expert",
        scatter_dimension=0,
        tiled=True,
    ).astype(jnp.float32)
    resid = rows_here.astype(jnp.float32) + attn_sum
    moe_in = layer_norm(resid, gains[1]).astype(jnp.bfloat16)
    moe_wide = moe_in.astype(jnp.float32)
    logits = jnp.dot(moe_wide, router[0], precision=highest)
    ids = expert_ids[0, 0]
    n_exp = router.shape[2]
    pick_int = (ids[:, :, None] == jnp.arange(n_exp)[None, None, :]).astype(jnp.int32)
    pick = pick_int.astype(jnp.float32)
    chosen = jnp.sum(pick * logits[:, None, :], axis=2)
    gates = jax.nn.sigmoid(chosen - chosen[:, ::-1])
    flat_pick = pick_int.reshape(tok_dev * TOP, n_exp)
    assigned = flat_pick.shape[0]
    earlier = (jnp.arange(assigned)[:, None] > jnp.arange(assigned)[None, :]).astype(jnp.bfloat16)
    before = jnp.dot(
        earlier, flat_pick.astype(jnp.bfloat16), preferred_element_type=jnp.float32
    ).astype(jnp.int32)
    slot = jnp.sum(before * flat_pick, axis=1)
    capacity = tok_dev * TOP // n_exp
    target = ids.reshape(-1) * capacity + slot
    place = (jnp.arange(n_exp * capacity)[:, None] == target[None, :]).astype(jnp.bfloat16)
    place = jnp.sum(place.reshape(n_exp * capacity, tok_dev, TOP), axis=2)
    send_rows = jnp.dot(place, moe_in, preferred_element_type=jnp.float32).astype(jnp.bfloat16)
    copies = lax.axis_size("expert") // n_exp
    outgoing = jnp.broadcast_to(
        send_rows.reshape(n_exp, 1, capacity, width), (n_exp, copies, capacity, width)
    )
    outgoing = outgoing.reshape(n_exp * copies, capacity, width)
    arrived = lax.all_to_all(outgoing, "expert", split_axis=0, concat_axis=0, tiled=True)
    sources = arrived.shape[0]
    slots_now = arrived.shape[1]
    flat = arrived.reshape(sources * slots_now, width)
    hidden = jnp.maximum(jnp.dot(flat, w_in[0], preferred_element_type=jnp.float32), 0.0).astype(
        jnp.bfloat16
    )
    partial_value = jnp.dot(hidden, w_exp_out[0], preferred_element_type=jnp.float32).astype(
        jnp.bfloat16
    )
    returned = lax.all_to_all(
        partial_value.reshape(sources, slots_now, width),
        "expert",
        split_axis=0,
        concat_axis=0,
        tiled=True,
    )
    expert_out = jnp.sum(
        returned.reshape(n_exp, copies, capacity, width).astype(jnp.float32), axis=1
    )
    expert_out = expert_out.reshape(n_exp * capacity, width)
    selected = expert_out[target].reshape(tok_dev, TOP, width)
    mixed = jnp.sum(gates[:, :, None] * selected, axis=1)
    layer_out = (resid + mixed).astype(jnp.bfloat16)
    cot = cotangent[0, 0].astype(jnp.float32)
    intersection = jnp.sum(cot[:, None, :] * selected, axis=2)
    delta = gates[:, 0] * gates[:, 1] * (intersection[:, 0] - intersection[:, 1])
    dlogits = delta[:, None] * (pick[:, 0] - pick[:, 1])
    local_grad = lax.dot_general(moe_wide, dlogits, (((0,), (0,)), ((), ())), precision=highest)
    total_rows = tok_dev * lax.axis_size("expert") * lax.axis_size("dp")
    router_grad = (
        lax.psum(local_grad.astype(jnp.bfloat16), ("expert", "dp")).astype(jnp.float32) / total_rows
    )
    carry = jnp.where(segment_pos == 0, layer_out, memory[0, 0])
    handed = from_behind(jnp.stack((layer_out, carry), axis=0), "segment", 1)
    return (handed[0][None, None], handed[1][None, None], router_grad[None])


BF = jnp.bfloat16
F32 = jnp.float32
MESH = pl.DeviceIdType.MESH
HALF = 64
CHUNK = 512
DEPTH = 1024
STRIP = 256
WIDE = 1024
LOAN = 16
PIECE = 16


def tick(
    x_hbm, mem_hbm, wqkv_hbm, wo_hbm, gains_hbm, router_hbm, win_hbm, wout_hbm, ids_hbm, lengths_hbm, cot_hbm,
    acts_out, memory_out, grad_out,
    gains, router_t, ids_t, lengths, wqkv, wo, win, wout, xv, rows, qkv, csend, crecv, resid, moe_in, cot,
    dsend, arr, acc, hidden, rsend, rrecv, lo, gsend, grecv,
    wsem, winsem, woutsem, ag_s, ag_r, c_s, c_r, d_s, d_r, r_s, r_r, z_s, z_r, g_s, g_r, m_s, m_r, small_sem, turn, grad_here,
    loan, ld_s, ld_r, lu_s, lu_r,
):
    seg = lax.axis_index("segment")
    exp = lax.axis_index("expert")
    dp = lax.axis_index("dp")
    n_seg = lax.axis_size("segment")
    following = lax.rem(seg + 1, n_seg)
    behind = lax.rem(seg + n_seg - 1, n_seg)
    col = lax.rem(exp, 2)
    row = exp // 2

    def peer(r):
        return lax.rem(col + r % 2, 2) + 2 * lax.rem(row + r // 2, 2)

    def send(src, dst, s, r, device):
        return pltpu.make_async_remote_copy(
            src_ref=src, dst_ref=dst, send_sem=s, recv_sem=r, device_id=device, device_id_type=MESH
        )

    local = [
        pltpu.make_async_copy(mem_hbm, rows.at[1, 0], wsem.at[0]),
        pltpu.make_async_copy(x_hbm, xv, wsem.at[1]),
        pltpu.make_async_copy(wqkv_hbm, wqkv, wsem.at[2]),
        pltpu.make_async_copy(wo_hbm, wo, wsem.at[3]),
        pltpu.make_async_copy(cot_hbm, cot, wsem.at[4]),
    ]
    small = [
        pltpu.make_async_copy(gains_hbm, gains, small_sem.at[0]),
        pltpu.make_async_copy(lengths_hbm, lengths, small_sem.at[1]),
        pltpu.make_async_copy(ids_hbm, ids_t, small_sem.at[2]),
        pltpu.make_async_copy(router_hbm, router_t, small_sem.at[3]),
    ]
    def win_copy(c):
        part = pl.ds(pl.multiple_of(c * WIDE, WIDE), WIDE)
        return pltpu.make_async_copy(win_hbm.at[:, part], win.at[c], winsem.at[c])

    def wout_copy(c):
        part = pl.ds(pl.multiple_of(c * CHUNK, CHUNK), CHUNK)
        return pltpu.make_async_copy(wout_hbm.at[:, part], wout.at[c], woutsem.at[c])

    barrier = pltpu.get_barrier_semaphore()
    others = [(r, d) for r in range(4) for d in range(2) if r + d > 0]
    for r, d in others:
        pl.semaphore_signal(
            barrier, 1, device_id={"expert": peer(r), "dp": lax.rem(dp + d, 2)}, device_id_type=MESH
        )
    pl.semaphore_signal(barrier, 1, device_id={"segment": behind}, device_id_type=MESH)

    @pl.when(seg == 0)
    def _():
        for far in range(1, n_seg):
            for r in (1, 2):
                pl.semaphore_signal(barrier, 1, device_id={"segment": far, "expert": peer(r)}, device_id_type=MESH)

    @pl.when(seg != 0)
    def _():
        pl.semaphore_signal(barrier, 1, device_id={"segment": 0}, device_id_type=MESH)

    for copy in (local[0], local[1], small[0], small[1], *local[2:], *small[2:]):
        copy.start()

    top, low = pl.ds(0, HALF), pl.ds(HALF, HALF)

    def gather_copies(a):
        along_x, along_y = {"expert": peer(1)}, {"expert": peer(2)}
        low_rest, top_rest = (pl.ds(HALF + a * LOAN, HALF - a * LOAN), pl.ds(a * LOAN, HALF - a * LOAN))
        plan = [
            (0, top, 1, along_x), (0, low_rest, 1, along_x), (0, low, 2, along_y), (0, top_rest, 2, along_y),
            (1, top, 3, along_y), (2, low, 3, along_x),
        ]
        return [
            send(rows.at[a, source, part], rows.at[a, slot, part], ag_s.at[a, i], ag_r.at[a, i], dev)
            for i, (source, part, slot, dev) in enumerate(plan)
        ]

    along_x, along_y = {"expert": peer(1)}, {"expert": peer(2)}
    plan = [
        (1, top, 1, along_x), (2, low, 2, along_y), (3, top, 0, along_x), (3, low, 0, along_y),
        (2, top, 2, along_y), (1, low, 1, along_x),
    ]
    shares = [
        send(csend.at[source, part], crecv.at[slot, part], c_s.at[i], c_r.at[i], dev)
        for i, (source, part, slot, dev) in enumerate(plan)
    ]
    norm_ag, mem_ag = gather_copies(0), gather_copies(1)
    loans = [(k, p) for p in range(LOAN // PIECE) for k in range(2)]

    def lend(i, k, p):
        part = pl.ds(HALF * (1 - k) + p * PIECE, PIECE)
        device = {"segment": 0, "expert": peer(1 + k)}
        spot = loan.at[i, k, pl.ds(p * PIECE, PIECE)]
        return send(rows.at[1, 0, part], spot, ld_s.at[k, p], ld_r.at[i, k, p], device)

    def pass_on(i, k, p):
        part = pl.ds(HALF * (1 - k) + p * PIECE, PIECE)
        spot = loan.at[i, k, pl.ds(p * PIECE, PIECE)]
        return send(spot, rows.at[1, 1 + k, part], lu_s.at[i, k, p], lu_r.at[k, p], {"segment": i + 1})

    mem_relay = send(rows.at[1, 0], memory_out, m_s.at[0], m_r.at[0], {"segment": following})

    local[0].wait()

    @pl.when(seg == 0)
    def _():
        pl.semaphore_wait(barrier, len(others) + n_seg)

    @pl.when(seg != 0)
    def _():
        pl.semaphore_wait(barrier, len(others) + 3)

    early, late = (0, 2), (1, 3)

    @pl.when((seg != 0) & (dp == 0))
    def _():
        for i in early:
            mem_ag[i].start()

    @pl.when(seg != 0)
    def _():
        for k, p in loans:
            lend(behind, k, p).start()

    local[1].wait()
    small[0].wait()

    def norm_rows(i, _):
        part = pl.ds(pl.multiple_of(i * 32, 32), 32)
        values = xv[part, :].astype(F32)
        normed = layer_norm(values, gains[0:1, :]).astype(BF)
        rows[0, 0, part, :] = normed
        return 0

    lax.fori_loop(0, 4, norm_rows, 0)

    @pl.when((dp == 0))
    def _():
        for i in early:
            norm_ag[i].start()

    def start_weights(c, _):
        win_copy(c).start()
        return 0

    def start_weights_out(c, _):
        wout_copy(c).start()
        return 0

    lax.fori_loop(0, win.shape[0], start_weights, 0)
    lax.fori_loop(0, wout.shape[0], start_weights_out, 0)

    @pl.when((dp == 0) & (seg != 0))
    def _():
        for i in early:
            mem_ag[i].wait_send()

    @pl.when(dp == 0)
    def _():
        pl.semaphore_signal(turn, 1, device_id={"dp": 1}, device_id_type=MESH)

    @pl.when(dp == 1)
    def _():
        pl.semaphore_wait(turn, 1)

        @pl.when(seg != 0)
        def _():
            for i in early:
                mem_ag[i].start()

        for i in early:
            norm_ag[i].start()

    @pl.when(seg == 0)
    def _():
        for i in early:
            norm_ag[i].wait_recv()
            norm_ag[4 + i // 2].start()
        for i in late:
            norm_ag[i].start()
        for k, p in loans:
            for i in reversed(range(n_seg - 1)):
                lend(i, k, p).wait_recv()
                pass_on(i, k, p).start()

    local[2].wait()
    local[3].wait()
    small[1].wait()

    tokens = SEQ
    small[2].wait()
    first, second = ids_t[0:1, :], ids_t[1:2, :]
    earlier = (
        lax.broadcasted_iota(jnp.int32, (tokens, tokens), 0)
        < lax.broadcasted_iota(jnp.int32, (tokens, tokens), 1)
    ).astype(BF)
    place, pick0, pick1 = [], [], []
    slot_no = lax.broadcasted_iota(jnp.int32, (HALF, tokens), 0).astype(F32)
    for r in range(4):
        one = (first == peer(r)).astype(F32)
        two = (second == peer(r)).astype(F32)
        named = one + two
        slot = jnp.dot(
            jnp.broadcast_to(named, (16, tokens)).astype(BF), earlier, preferred_element_type=F32
        )[0:1, :]
        hit = (slot_no == slot).astype(F32)
        place.append((hit * named).astype(BF))
        pick0.append(hit * one)
        pick1.append(hit * two)
    back = jnp.concatenate(
        [jnp.concatenate(pick0, axis=0).T, jnp.concatenate(pick1, axis=0).T], axis=0
    ).astype(BF)

    def project(r, j):
        source = ((j + 1) // 2) * ((seg + n_seg - 1) // n_seg)
        got = jnp.dot(rows[source, r], wqkv[j], preferred_element_type=F32)
        qkv[lax.rem(r, 3), j] = got.astype(BF)

    def section(step, _):
        r = (lax.rem(step + 1, 3) + 1) * ((step + 2) // 3)

        @pl.when((step == 1) & (seg != 0))
        def _():
            for i in early:
                mem_ag[i].wait_recv()
                mem_ag[4 + i // 2].start()
            for i in early:
                norm_ag[i].wait_recv()
                norm_ag[4 + i // 2].start()
            for i in late:
                mem_ag[i].start()
            for i in late:
                norm_ag[i].start()
            for i in (4, 5):
                mem_ag[i].wait_recv()

        @pl.when(step == 1)
        def _():
            for i in (4, 5):
                norm_ag[i].wait_recv()

        @pl.when((step == 2) & (seg != 0))
        def _():
            for i in late:
                mem_ag[i].wait_recv()
            for k, p in loans:
                pass_on(0, k, p).wait_recv()
            mem_relay.start()

        @pl.when(step == 2)
        def _():
            @pl.when(seg == 0)
            def _():
                for i in late:
                    norm_ag[i].wait_recv()

            def keys_values(n, _):
                project(1 + n // 2, 1 + lax.rem(n, 2))
                return 0

            lax.fori_loop(0, 4, keys_values, 0)

            @pl.when(seg != 0)
            def _():
                for i in late:
                    norm_ag[i].wait_recv()

        def project_step(j, _):
            project(r, j)
            return 0

        lax.fori_loop(0, 3 - 2 * (step // 2), project_step, 0)
        owner = peer(r)
        held = lax.rem(r, 3)
        live = (lax.broadcasted_iota(jnp.int32, (1, SEQ), 1) < lengths[owner]).astype(F32)
        parts = []
        for h in range(wo.shape[0] // HEAD_DIM):
            cols = slice(h * HEAD_DIM, (h + 1) * HEAD_DIM)
            scores = lax.dot_general(
                qkv[held, 0, :, cols], qkv[held, 1, :, cols], (((1,), (1,)), ((), ())), preferred_element_type=F32
            ) * HEAD_DIM ** (-0.5)
            raised = jnp.exp(scores) * live
            probs = (raised / jnp.sum(raised, axis=-1, keepdims=True)).astype(BF)
            parts.append(jnp.dot(probs, qkv[held, 2, :, cols], preferred_element_type=F32).astype(BF))
        context = jnp.concatenate(parts, axis=1)
        for c in range(4):
            cols = slice(c * CHUNK, (c + 1) * CHUNK)
            csend[r, :, cols] = jnp.dot(context, wo[:, cols], preferred_element_type=F32).astype(BF)

        @pl.when(step == 1)
        def _():
            shares[2].start()
            shares[3].start()

        @pl.when(step == 2)
        def _():
            shares[0].start()

        @pl.when(step == 3)
        def _():
            shares[1].start()

        return 0

    lax.fori_loop(0, 4, section, 0)

    for base, source, came, goes in ((HALF, 1, 3, 5), (0, 2, 2, 4)):
        shares[came].wait_recv()

        def join(i, _, base=base, source=source):
            part = pl.ds(pl.multiple_of(base + i * 32, 32), 32)
            both = csend[source, part, :].astype(F32) + crecv[0, part, :].astype(F32)
            csend[source, part, :] = both.astype(BF)
            return 0

        lax.fori_loop(0, HALF // 32, join, 0)
        shares[goes].start()
    def second_norm(i, _):
        part = pl.ds(pl.multiple_of(i * 32, 32), 32)
        total = csend[0, part, :].astype(F32)
        for r in (1, 2):
            total = total + crecv[r, part, :].astype(F32)
        values = xv[part, :].astype(F32) + total
        resid[part, :] = values
        moe_in[part, :] = layer_norm(values, gains[1:2, :]).astype(BF)
        return 0

    def finish(half, _):
        @pl.when(half == 0)
        def _():
            shares[1].wait_recv()
            shares[5].wait_recv()

        @pl.when(half == 1)
        def _():
            shares[0].wait_recv()
            shares[4].wait_recv()

        lax.fori_loop(2 - 2 * half, 4 - 2 * half, second_norm, 0)
        return 0

    lax.fori_loop(0, 2, finish, 0)

    def dispatch(k, r):
        part = pl.ds(r * HALF, HALF)
        return send(dsend.at[k, part], arr.at[k, part], d_s.at[k, r], d_r.at[k, r], {"expert": peer(r)})

    placed = jnp.concatenate(place, axis=0)

    for k in range(arr.shape[0]):
        for j in range(DEPTH // CHUNK):
            cols = slice(k * DEPTH + j * CHUNK, k * DEPTH + (j + 1) * CHUNK)
            chosen = jnp.dot(placed, moe_in[:, cols], preferred_element_type=F32).astype(BF)
            dsend[k, :, j * CHUNK:(j + 1) * CHUNK] = chosen
            arr[k, 0:HALF, j * CHUNK:(j + 1) * CHUNK] = chosen[0:HALF, :]
        if k == 0:
            @pl.when(dp == 1)
            def _():
                pl.semaphore_wait(turn, 1)

        for r in (3, 1, 2):
            dispatch(k, r).start()

    small[3].wait()
    logits = lax.dot_general(
        router_t[...], moe_in[...].astype(F32), (((1,), (1,)), ((), ())),
        precision=highest, preferred_element_type=F32,
    )
    chosen0 = jnp.zeros((1, tokens), F32)
    chosen1 = jnp.zeros((1, tokens), F32)
    for e in range(4):
        chosen0 = chosen0 + (first == e).astype(F32) * logits[e:e + 1, :]
        chosen1 = chosen1 + (second == e).astype(F32) * logits[e:e + 1, :]
    gate0 = jax.nn.sigmoid(chosen0 - chosen1)
    gate1 = jax.nn.sigmoid(chosen1 - chosen0)
    slope = gate0 * gate1
    gate0 = jnp.broadcast_to(gate0, (tokens, tokens)).T[:, 0:1]
    gate1 = jnp.broadcast_to(gate1, (tokens, tokens)).T[:, 0:1]

    for r in (3, 1, 2):
        dispatch(0, r).wait_recv()

    @pl.when(dp == 0)
    def _():
        pl.semaphore_signal(turn, 1, device_id={"dp": 1}, device_id_type=MESH)

    def columns_first(c, _):
        win_copy(c).wait()
        acc[c] = jnp.dot(arr[0], win[c, 0:DEPTH, :], preferred_element_type=F32)
        return 0

    lax.fori_loop(0, win.shape[0], columns_first, 0)
    for r in (3, 1, 2):
        dispatch(1, r).wait_recv()

    def columns_last(c, _):
        got = jnp.dot(arr[1], win[c, DEPTH:2 * DEPTH, :], preferred_element_type=F32)
        cols = pl.ds(pl.multiple_of(c * WIDE, WIDE), WIDE)
        hidden[:, cols] = jnp.maximum(acc[c] + got, 0.0).astype(BF)
        return 0

    lax.fori_loop(0, win.shape[0], columns_last, 0)

    def give_back(c, r):
        part = pl.ds(r * HALF, HALF)
        return send(rsend.at[c, part], rrecv.at[c, part], r_s.at[c, r], r_r.at[c, r], {"expert": peer(r)})

    def expert_out(c, _):
        wout_copy(c).wait()
        got = jnp.dot(hidden[...], wout[c], preferred_element_type=F32).astype(BF)
        for j in range(CHUNK // STRIP):
            strip = got[:, j * STRIP:(j + 1) * STRIP]
            n = c * (CHUNK // STRIP) + j
            rsend[n] = strip
            rrecv[n, 0:HALF, :] = strip[0:HALF, :]
            for r in (3, 1, 2):
                give_back(n, r).start()
        return 0

    lax.fori_loop(0, wout.shape[0], expert_out, 0)
    local[4].wait()

    def onward(c):
        cols = pl.ds(pl.multiple_of(c * STRIP, STRIP), STRIP)
        return send(lo.at[c], acts_out.at[:, cols], z_s.at[c], z_r.at[c], {"segment": following})

    def combine(c, gap):
        for r in (3, 1, 2):
            give_back(c, r).wait_recv()
        cols = pl.ds(pl.multiple_of(c * STRIP, STRIP), STRIP)
        both = jnp.dot(back, rrecv[c], preferred_element_type=F32)
        sel0, sel1 = both[0:tokens, :], both[tokens:2 * tokens, :]
        lo[c] = (resid[:, cols] + (gate0 * sel0 + gate1 * sel1)).astype(BF)
        onward(c).start()
        terms = cot[:, cols].astype(F32) * (sel0 - sel1)
        for j in range(STRIP // tokens):
            gap = gap + terms[:, j * tokens:(j + 1) * tokens]
        return gap

    strips = rsend.shape[0]
    gap = lax.fori_loop(0, strips, combine, jnp.zeros((tokens, tokens), F32))
    gap_row = jnp.zeros((16, tokens), F32)
    for _ in range(3):
        part = gap.astype(BF)
        gap = gap - part.astype(F32)
        gap_row = gap_row + lax.dot_general(
            jnp.ones((16, tokens), BF), part, (((1,), (1,)), ((), ())), preferred_element_type=F32
        )
    delta = slope * gap_row[0:1, :]
    rest = jnp.concatenate(
        [delta * ((first == e).astype(F32) - (second == e).astype(F32)) for e in range(4)], axis=0
    )
    terms = []
    for _ in range(3):
        terms.append(rest.astype(BF))
        rest = rest - terms[-1].astype(F32)
    terms = jnp.concatenate([term.astype(F32) for term in terms] + [jnp.zeros((4, tokens), F32)], axis=0)
    products = jnp.dot(terms.astype(BF), moe_in[...], preferred_element_type=F32)
    grad = products[0:4, :] + products[4:8, :] + products[8:12, :]
    gsend[...] = jnp.concatenate(
        [grad[0:4, c * CHUNK:(c + 1) * CHUNK] for c in range(4)], axis=0
    ).astype(BF)

    def share(r, d):
        i = r * 2 + d
        device = {"expert": peer(r), "dp": lax.rem(dp + d, 2)}
        return send(gsend, grecv.at[i], g_s.at[i], g_r.at[i], device)

    for r, d in others:
        share(r, d).start()
    @pl.when(seg != 0)
    def _():
        mem_relay.wait_send()

    @pl.when(seg != 1)
    def _():
        mem_relay.wait_recv()

    for i in range(6):
        norm_ag[i].wait_send()

    @pl.when(seg != 0)
    def _():
        for i in (1, 3, 4, 5):
            mem_ag[i].wait_send()
        for k, p in loans:
            lend(behind, k, p).wait_send()

    @pl.when((seg != 0) & (dp == 1))
    def _():
        for i in early:
            mem_ag[i].wait_send()

    @pl.when(seg == 0)
    def _():
        for i in range(n_seg - 1):
            for k, p in loans:
                pass_on(i, k, p).wait_send()

    for r in (1, 2, 3):
        for c in range(arr.shape[0]):
            dispatch(c, r).wait_send()
        for c in range(strips):
            give_back(c, r).wait_send()
    for copy in shares:
        copy.wait_send()
    def drain(c, _):
        onward(c).wait_send()
        onward(c).wait_recv()
        return 0

    lax.fori_loop(0, strips - 1, drain, 0)
    for r, d in others:
        share(r, d).wait_recv()
    total = gsend[...].astype(F32)
    for r, d in others:
        total = total + grecv[r * 2 + d].astype(F32)
    total = total / (tokens * lax.axis_size("expert") * lax.axis_size("dp"))
    for c in range(4):
        grad_here[:, c * CHUNK:(c + 1) * CHUNK] = total[c * 4:(c + 1) * 4, :]

    for r, d in others:
        share(r, d).wait_send()
    done = pltpu.make_async_copy(grad_here, grad_out, small_sem.at[0])
    done.start()
    drain(strips - 1, 0)
    done.wait()


def hand_over(first_decoder, acts, kept, grad, acts_out, memory_out, grad_out):
    acts_out[...] = acts[...]
    memory_out[...] = jnp.where(first_decoder[0] == 1, acts[...], kept[...])
    grad_out[...] = grad[...]


def fused(
    x_in, memory, w_qkv, w_attn_out, norm_gains, router, w_in, w_exp_out, expert_ids, lengths, cotangent
):
    tokens, width = x_in.shape[2:]
    head_cols = w_attn_out.shape[1]
    hid = w_in.shape[2]
    n_in, n_out, strips, deep = hid // WIDE, width // CHUNK, width // STRIP, width // DEPTH
    n_seg = lax.axis_size("segment")
    hbm = pl.BlockSpec(memory_space=pl.ANY)
    vmem = pl.BlockSpec(memory_space=pltpu.VMEM)
    smem = pl.BlockSpec(memory_space=pltpu.SMEM)
    dma = pltpu.SemaphoreType.DMA
    acts, kept, grad = pl.pallas_call(
        tick,
        out_shape=(
            jax.ShapeDtypeStruct((tokens, width), BF),
            jax.ShapeDtypeStruct((tokens, width), BF),
            jax.ShapeDtypeStruct((4, width), F32),
        ),
        in_specs=[hbm] * 11,
        out_specs=(hbm, hbm, hbm),
        scratch_shapes=[
            pltpu.VMEM((2, width), F32),
            pltpu.VMEM((4, width), F32),
            pltpu.VMEM((2, tokens), jnp.int32),
            pltpu.SMEM((4,), jnp.int32),
            pltpu.VMEM((3, width, head_cols), BF),
            pltpu.VMEM((head_cols, width), BF),
            pltpu.VMEM((n_in, width, WIDE), BF),
            pltpu.VMEM((n_out, hid, CHUNK), BF),
            pltpu.VMEM((tokens, width), BF),
            pltpu.VMEM((2, 4, tokens, width), BF),
            pltpu.VMEM((3, 3, tokens, head_cols), BF),
            pltpu.VMEM((4, tokens, width), BF),
            pltpu.VMEM((3, tokens, width), BF),
            pltpu.VMEM((tokens, width), F32),
            pltpu.VMEM((tokens, width), BF),
            pltpu.VMEM((tokens, width), BF),
            pltpu.VMEM((deep, 4 * HALF, DEPTH), BF),
            pltpu.VMEM((deep, 4 * HALF, DEPTH), BF),
            pltpu.VMEM((n_in, 4 * HALF, WIDE), F32),
            pltpu.VMEM((4 * HALF, hid), BF),
            pltpu.VMEM((strips, 4 * HALF, STRIP), BF),
            pltpu.VMEM((strips, 4 * HALF, STRIP), BF),
            pltpu.VMEM((strips, tokens, STRIP), BF),
            pltpu.VMEM((16, CHUNK), BF),
            pltpu.VMEM((8, 16, CHUNK), BF),
            dma((5,)), dma((n_in,)), dma((n_out,)),
            dma((2, 6)), dma((2, 6)), dma((6,)), dma((6,)), dma((deep, 4)), dma((deep, 4)),
            dma((strips, 4)), dma((strips, 4)), dma((strips,)), dma((strips,)),
            dma((8,)), dma((8,)), dma((1,)), dma((1,)), dma((4,)), pltpu.SemaphoreType.REGULAR,
            pltpu.VMEM((4, width), F32),
            pltpu.VMEM((n_seg - 1, 2, LOAN, width), BF),
            dma((2, LOAN // PIECE)), dma((n_seg - 1, 2, LOAN // PIECE)),
            dma((n_seg - 1, 2, LOAN // PIECE)), dma((2, LOAN // PIECE)),
        ],
        compiler_params=pltpu.CompilerParams(
            collective_id=0, has_side_effects=True, vmem_limit_bytes=64 * 2**20 - 2**18
        ),
    )(
        x_in[0, 0], memory[0, 0], w_qkv[0], w_attn_out[0], norm_gains[0], router[0].T, w_in[0],
        w_exp_out[0], expert_ids[0, 0].T, lengths[0, 0], cotangent[0, 0],
    )
    first_decoder = (lax.axis_index("segment") == 1).astype(jnp.int32).reshape(1)
    acts, kept, grad = pl.pallas_call(
        hand_over,
        out_shape=(acts, kept, grad),
        in_specs=[smem, vmem, vmem, vmem],
        out_specs=(vmem, vmem, vmem),
    )(first_decoder, acts, kept, grad)
    return acts[None, None], kept[None, None], grad.T[None]


def solution(mesh):
    small = (mesh.shape["expert"], mesh.shape["dp"]) == (4, 2) and mesh.shape["segment"] > 2
    placed = (
        P("segment", "dp", "expert", None),
        P("segment", "dp", "expert", None),
        P("segment", None, None, "expert"),
        P("segment", "expert", None),
        P("segment", None, None),
        P("segment", None, None),
        P("segment", None, "expert"),
        P("segment", "expert", None),
        P("segment", "dp", "expert", None),
        P("segment", "dp", None),
        P("segment", "dp", "expert", None),
    )
    return jax.shard_map(
        fused if small else shards,
        mesh=mesh,
        in_specs=placed,
        out_specs=(
            P("segment", "dp", "expert", None),
            P("segment", "dp", "expert", None),
            P("segment", None, None),
        ),
        check_vma=False,
    )
```

```python
import jax
import jax.numpy as jnp
from jax import lax
from jax.experimental import pallas as pl
from jax.experimental.pallas import tpu as pltpu
from jax.sharding import PartitionSpec as P

HEAD_DIM = 128
TOP = 2
SEQ = 128


eps = 1e-05
highest = lax.Precision.HIGHEST


def from_behind(block, axis, distance):
    devices = range(lax.axis_size(axis))
    route = [((i - distance) % len(devices), i) for i in devices]
    return lax.ppermute(block, axis, route)


def layer_norm(values, gain):
    centered = values - jnp.mean(values, axis=-1, keepdims=True)
    variance = jnp.mean(centered * centered, axis=-1, keepdims=True)
    return centered * lax.rsqrt(variance + eps) * gain


def shards(
    x_in,
    memory,
    w_qkv,
    w_attn_out,
    norm_gains,
    router,
    w_in,
    w_exp_out,
    expert_ids,
    lengths,
    cotangent,
):
    segment_pos = lax.axis_index("segment")
    rows_here = x_in[0, 0]
    tok_dev = rows_here.shape[0]
    width = rows_here.shape[1]
    head_cols = w_attn_out.shape[1]
    gains = norm_gains[0]
    weights_qkv = w_qkv[0]
    normed = layer_norm(rows_here.astype(jnp.float32), gains[0]).astype(jnp.bfloat16)
    key_source = jnp.where(segment_pos == 0, normed, memory[0, 0])
    stacked = jnp.stack((normed, key_source), axis=0)
    piece = lax.all_gather(stacked, "expert", axis=1, tiled=True)
    query = jnp.dot(piece[0], weights_qkv[0], preferred_element_type=jnp.float32)
    keys = jnp.dot(piece[1], weights_qkv[1], preferred_element_type=jnp.float32)
    values = jnp.dot(piece[1], weights_qkv[2], preferred_element_type=jnp.float32)
    projected = jnp.concatenate((query, keys, values), axis=1).astype(jnp.bfloat16)
    group_rows = projected.shape[0]
    count = group_rows // SEQ
    heads_here = head_cols // HEAD_DIM
    shaped = projected.reshape(count, SEQ, 3, heads_here, HEAD_DIM)
    scores = jnp.einsum(
        "nihd,njhd->nhij", shaped[:, :, 0], shaped[:, :, 1], preferred_element_type=jnp.float32
    ) * HEAD_DIM ** (-0.5)
    live = (jnp.arange(SEQ)[None, :] < lengths[0, 0][:, None]).astype(jnp.float32)
    raised = jnp.exp(scores) * live[:, None, None, :]
    probs = (raised / jnp.sum(raised, axis=-1, keepdims=True)).astype(jnp.bfloat16)
    context = jnp.einsum(
        "nhij,njhd->nihd", probs, shaped[:, :, 2], preferred_element_type=jnp.float32
    )
    context = context.astype(jnp.bfloat16).reshape(group_rows, head_cols)
    attn_sum = lax.psum_scatter(
        jnp.dot(context, w_attn_out[0], preferred_element_type=jnp.float32).astype(jnp.bfloat16),
        "expert",
        scatter_dimension=0,
        tiled=True,
    ).astype(jnp.float32)
    resid = rows_here.astype(jnp.float32) + attn_sum
    moe_in = layer_norm(resid, gains[1]).astype(jnp.bfloat16)
    moe_wide = moe_in.astype(jnp.float32)
    logits = jnp.dot(moe_wide, router[0], precision=highest)
    ids = expert_ids[0, 0]
    n_exp = router.shape[2]
    pick_int = (ids[:, :, None] == jnp.arange(n_exp)[None, None, :]).astype(jnp.int32)
    pick = pick_int.astype(jnp.float32)
    chosen = jnp.sum(pick * logits[:, None, :], axis=2)
    gates = jax.nn.sigmoid(chosen - chosen[:, ::-1])
    flat_pick = pick_int.reshape(tok_dev * TOP, n_exp)
    assigned = flat_pick.shape[0]
    earlier = (jnp.arange(assigned)[:, None] > jnp.arange(assigned)[None, :]).astype(jnp.bfloat16)
    before = jnp.dot(
        earlier, flat_pick.astype(jnp.bfloat16), preferred_element_type=jnp.float32
    ).astype(jnp.int32)
    slot = jnp.sum(before * flat_pick, axis=1)
    capacity = tok_dev * TOP // n_exp
    target = ids.reshape(-1) * capacity + slot
    place = (jnp.arange(n_exp * capacity)[:, None] == target[None, :]).astype(jnp.bfloat16)
    place = jnp.sum(place.reshape(n_exp * capacity, tok_dev, TOP), axis=2)
    send_rows = jnp.dot(place, moe_in, preferred_element_type=jnp.float32).astype(jnp.bfloat16)
    copies = lax.axis_size("expert") // n_exp
    outgoing = jnp.broadcast_to(
        send_rows.reshape(n_exp, 1, capacity, width), (n_exp, copies, capacity, width)
    )
    outgoing = outgoing.reshape(n_exp * copies, capacity, width)
    arrived = lax.all_to_all(outgoing, "expert", split_axis=0, concat_axis=0, tiled=True)
    sources = arrived.shape[0]
    slots_now = arrived.shape[1]
    flat = arrived.reshape(sources * slots_now, width)
    hidden = jnp.maximum(jnp.dot(flat, w_in[0], preferred_element_type=jnp.float32), 0.0).astype(
        jnp.bfloat16
    )
    partial_value = jnp.dot(hidden, w_exp_out[0], preferred_element_type=jnp.float32).astype(
        jnp.bfloat16
    )
    returned = lax.all_to_all(
        partial_value.reshape(sources, slots_now, width),
        "expert",
        split_axis=0,
        concat_axis=0,
        tiled=True,
    )
    expert_out = jnp.sum(
        returned.reshape(n_exp, copies, capacity, width).astype(jnp.float32), axis=1
    )
    expert_out = expert_out.reshape(n_exp * capacity, width)
    selected = expert_out[target].reshape(tok_dev, TOP, width)
    mixed = jnp.sum(gates[:, :, None] * selected, axis=1)
    layer_out = (resid + mixed).astype(jnp.bfloat16)
    cot = cotangent[0, 0].astype(jnp.float32)
    intersection = jnp.sum(cot[:, None, :] * selected, axis=2)
    delta = gates[:, 0] * gates[:, 1] * (intersection[:, 0] - intersection[:, 1])
    dlogits = delta[:, None] * (pick[:, 0] - pick[:, 1])
    local_grad = lax.dot_general(moe_wide, dlogits, (((0,), (0,)), ((), ())), precision=highest)
    total_rows = tok_dev * lax.axis_size("expert") * lax.axis_size("dp")
    router_grad = (
        lax.psum(local_grad.astype(jnp.bfloat16), ("expert", "dp")).astype(jnp.float32) / total_rows
    )
    carry = jnp.where(segment_pos == 0, layer_out, memory[0, 0])
    handed = from_behind(jnp.stack((layer_out, carry), axis=0), "segment", 1)
    return (handed[0][None, None], handed[1][None, None], router_grad[None])


BF = jnp.bfloat16
F32 = jnp.float32
MESH = pl.DeviceIdType.MESH
HALF = 64
CHUNK = 512
DEPTH = 1024
STRIP = 256
WIDE = 1024
LOAN = 32
PIECE = 16
LENDERS = (0, 1)


def tick(
    x_hbm, mem_hbm, wqkv_hbm, wo_hbm, gains_hbm, router_hbm, win_hbm, wout_hbm, ids_hbm, lengths_hbm, cot_hbm,
    acts_out, memory_out, grad_out,
    gains, router_t, ids_t, lengths, wqkv, wo, win, wout, xv, rows, qkv, csend, crecv, resid, moe_in, cot,
    dsend, arr, acc, hidden, rsend, rrecv, lo, gsend, grecv,
    wsem, winsem, woutsem, ag_s, ag_r, c_s, c_r, d_s, d_r, r_s, r_r, z_s, z_r, g_s, g_r, m_s, m_r, small_sem, turn, grad_here,
    loan, ld_s, ld_r, lu_s, lu_r, near_s, near_r,
):
    seg = lax.axis_index("segment")
    exp = lax.axis_index("expert")
    dp = lax.axis_index("dp")
    n_seg = lax.axis_size("segment")
    following = lax.rem(seg + 1, n_seg)
    behind = lax.rem(seg + n_seg - 1, n_seg)
    col = lax.rem(exp, 2)
    row = exp // 2

    def peer(r):
        return lax.rem(col + r % 2, 2) + 2 * lax.rem(row + r // 2, 2)

    def send(src, dst, s, r, device):
        return pltpu.make_async_remote_copy(
            src_ref=src, dst_ref=dst, send_sem=s, recv_sem=r, device_id=device, device_id_type=MESH
        )

    local = [
        pltpu.make_async_copy(mem_hbm, rows.at[1, 0], wsem.at[0]),
        pltpu.make_async_copy(x_hbm, xv, wsem.at[1]),
        pltpu.make_async_copy(wqkv_hbm, wqkv, wsem.at[2]),
        pltpu.make_async_copy(wo_hbm, wo, wsem.at[3]),
        pltpu.make_async_copy(cot_hbm, cot, wsem.at[4]),
    ]
    small = [
        pltpu.make_async_copy(gains_hbm, gains, small_sem.at[0]),
        pltpu.make_async_copy(lengths_hbm, lengths, small_sem.at[1]),
        pltpu.make_async_copy(ids_hbm, ids_t, small_sem.at[2]),
        pltpu.make_async_copy(router_hbm, router_t, small_sem.at[3]),
    ]
    def win_copy(c):
        part = pl.ds(pl.multiple_of(c * WIDE, WIDE), WIDE)
        return pltpu.make_async_copy(win_hbm.at[:, part], win.at[c], winsem.at[c])

    def wout_copy(c):
        part = pl.ds(pl.multiple_of(c * CHUNK, CHUNK), CHUNK)
        return pltpu.make_async_copy(wout_hbm.at[:, part], wout.at[c], woutsem.at[c])

    barrier = pltpu.get_barrier_semaphore()
    others = [(r, d) for r in range(4) for d in range(2) if r + d > 0]
    for r, d in others:
        pl.semaphore_signal(
            barrier, 1, device_id={"expert": peer(r), "dp": lax.rem(dp + d, 2)}, device_id_type=MESH
        )
    pl.semaphore_signal(barrier, 1, device_id={"segment": behind}, device_id_type=MESH)

    @pl.when(seg == 0)
    def _():
        for far in range(1, n_seg):
            for r in (1, 2):
                pl.semaphore_signal(barrier, 1, device_id={"segment": far, "expert": peer(r)}, device_id_type=MESH)

    @pl.when(seg != 0)
    def _():
        pl.semaphore_signal(barrier, 1, device_id={"segment": 0}, device_id_type=MESH)

    for copy in (local[0], local[1], small[0], small[1], *local[2:], *small[2:]):
        copy.start()

    top, low = pl.ds(0, HALF), pl.ds(HALF, HALF)

    def gather_copies(a):
        along_x, along_y = {"expert": peer(1)}, {"expert": peer(2)}
        low_rest, top_rest = (pl.ds(HALF + a * LOAN, HALF - a * LOAN), pl.ds(a * LOAN, HALF - a * LOAN))
        plan = [
            (0, top, 1, along_x), (0, low_rest, 1, along_x), (0, low, 2, along_y), (0, top_rest, 2, along_y),
            (1, top, 3, along_y), (2, low, 3, along_x),
        ]
        return [
            send(rows.at[a, source, part], rows.at[a, slot, part], ag_s.at[a, i], ag_r.at[a, i], dev)
            for i, (source, part, slot, dev) in enumerate(plan)
        ]

    along_x, along_y = {"expert": peer(1)}, {"expert": peer(2)}
    plan = [
        (1, top, 1, along_x), (2, low, 2, along_y), (3, top, 0, along_x), (3, low, 0, along_y),
        (2, top, 2, along_y), (1, low, 1, along_x),
    ]
    shares = [
        send(csend.at[source, part], crecv.at[slot, part], c_s.at[i], c_r.at[i], dev)
        for i, (source, part, slot, dev) in enumerate(plan)
    ]
    norm_ag, mem_ag = gather_copies(0), gather_copies(1)
    loans = [(k, p) for p in range(LOAN // PIECE) for k in range(2)]

    nearest = [n_seg - 1 - LENDERS[p] if LENDERS[p] else 0 for p in range(LOAN // PIECE)]

    def keep(k, p):
        part = pl.ds(HALF * (1 - k) + p * PIECE, PIECE)
        spot = rows.at[1, 1 + k, part]
        return send(rows.at[1, 0, part], spot, near_s.at[k, p], near_r.at[k, p], {"expert": peer(1 + k)})

    def each_loan(lent, kept=None):
        for k, p in loans:
            @pl.when(seg > nearest[p])
            def _(k=k, p=p):
                lent(k, p)

            if kept is not None and nearest[p] > 0:
                @pl.when((seg != 0) & (seg <= nearest[p]))
                def _(k=k, p=p):
                    kept(k, p)

    def lend(i, k, p):
        part = pl.ds(HALF * (1 - k) + p * PIECE, PIECE)
        device = {"segment": 0, "expert": peer(1 + k)}
        spot = loan.at[i, k, pl.ds(p * PIECE, PIECE)]
        return send(rows.at[1, 0, part], spot, ld_s.at[k, p], ld_r.at[i, k, p], device)

    def pass_on(i, k, p):
        part = pl.ds(HALF * (1 - k) + p * PIECE, PIECE)
        spot = loan.at[i, k, pl.ds(p * PIECE, PIECE)]
        return send(spot, rows.at[1, 1 + k, part], lu_s.at[i, k, p], lu_r.at[k, p], {"segment": i + 1})

    mem_relay = send(rows.at[1, 0], memory_out, m_s.at[0], m_r.at[0], {"segment": following})

    local[0].wait()

    @pl.when(seg == 0)
    def _():
        pl.semaphore_wait(barrier, len(others) + n_seg)

    @pl.when(seg != 0)
    def _():
        pl.semaphore_wait(barrier, len(others) + 3)

    early, late = (0, 2), (1, 3)

    @pl.when((seg != 0) & (dp == 0))
    def _():
        for i in early:
            mem_ag[i].start()

    each_loan(lambda k, p: lend(behind, k, p).start())

    local[1].wait()
    small[0].wait()

    def norm_rows(i, _):
        part = pl.ds(pl.multiple_of(i * 32, 32), 32)
        values = xv[part, :].astype(F32)
        normed = layer_norm(values, gains[0:1, :]).astype(BF)
        rows[0, 0, part, :] = normed
        return 0

    lax.fori_loop(0, 4, norm_rows, 0)

    @pl.when((dp == 0))
    def _():
        for i in early:
            norm_ag[i].start()

    def start_weights(c, _):
        win_copy(c).start()
        return 0

    def start_weights_out(c, _):
        wout_copy(c).start()
        return 0

    lax.fori_loop(0, win.shape[0], start_weights, 0)
    lax.fori_loop(0, wout.shape[0], start_weights_out, 0)

    @pl.when((dp == 0) & (seg != 0))
    def _():
        for i in early:
            mem_ag[i].wait_send()

    @pl.when(dp == 0)
    def _():
        pl.semaphore_signal(turn, 1, device_id={"dp": 1}, device_id_type=MESH)

    @pl.when(dp == 1)
    def _():
        pl.semaphore_wait(turn, 1)

        @pl.when(seg != 0)
        def _():
            for i in early:
                mem_ag[i].start()

        for i in early:
            norm_ag[i].start()

    @pl.when(seg == 0)
    def _():
        for i in early:
            norm_ag[i].wait_recv()
            norm_ag[4 + i // 2].start()
        for i in late:
            norm_ag[i].start()
        for k, p in loans:
            for i in reversed(range(nearest[p], n_seg - 1)):
                lend(i, k, p).wait_recv()
                pass_on(i, k, p).start()

    local[2].wait()
    local[3].wait()
    small[1].wait()

    tokens = SEQ
    small[2].wait()
    first, second = ids_t[0:1, :], ids_t[1:2, :]
    earlier = (
        lax.broadcasted_iota(jnp.int32, (tokens, tokens), 0)
        < lax.broadcasted_iota(jnp.int32, (tokens, tokens), 1)
    ).astype(BF)
    place, pick0, pick1 = [], [], []
    slot_no = lax.broadcasted_iota(jnp.int32, (HALF, tokens), 0).astype(F32)
    for r in range(4):
        one = (first == peer(r)).astype(F32)
        two = (second == peer(r)).astype(F32)
        named = one + two
        slot = jnp.dot(
            jnp.broadcast_to(named, (16, tokens)).astype(BF), earlier, preferred_element_type=F32
        )[0:1, :]
        hit = (slot_no == slot).astype(F32)
        place.append((hit * named).astype(BF))
        pick0.append(hit * one)
        pick1.append(hit * two)
    back = jnp.concatenate(
        [jnp.concatenate(pick0, axis=0).T, jnp.concatenate(pick1, axis=0).T], axis=0
    ).astype(BF)

    def project(r, j):
        source = ((j + 1) // 2) * ((seg + n_seg - 1) // n_seg)
        got = jnp.dot(rows[source, r], wqkv[j], preferred_element_type=F32)
        qkv[lax.rem(r, 3), j] = got.astype(BF)

    def section(step, _):
        r = (lax.rem(step + 1, 3) + 1) * ((step + 2) // 3)

        @pl.when((step == 1) & (seg != 0))
        def _():
            for i in early:
                mem_ag[i].wait_recv()
                mem_ag[4 + i // 2].start()
            for i in early:
                norm_ag[i].wait_recv()
                norm_ag[4 + i // 2].start()
            each_loan(lambda k, p: None, lambda k, p: keep(k, p).start())
            for i in late:
                mem_ag[i].start()
            for i in late:
                norm_ag[i].start()
            for i in (4, 5):
                mem_ag[i].wait_recv()

        @pl.when(step == 1)
        def _():
            for i in (4, 5):
                norm_ag[i].wait_recv()

        @pl.when((step == 2) & (seg != 0))
        def _():
            for i in late:
                mem_ag[i].wait_recv()
            each_loan(lambda k, p: pass_on(0, k, p).wait_recv(), lambda k, p: keep(k, p).wait_recv())
            mem_relay.start()

        @pl.when(step == 2)
        def _():
            @pl.when(seg == 0)
            def _():
                for i in late:
                    norm_ag[i].wait_recv()

            def keys_values(n, _):
                project(1 + n // 2, 1 + lax.rem(n, 2))
                return 0

            lax.fori_loop(0, 4, keys_values, 0)

            @pl.when(seg != 0)
            def _():
                for i in late:
                    norm_ag[i].wait_recv()

        def project_step(j, _):
            project(r, j)
            return 0

        lax.fori_loop(0, 3 - 2 * (step // 2), project_step, 0)
        owner = peer(r)
        held = lax.rem(r, 3)
        live = (lax.broadcasted_iota(jnp.int32, (1, SEQ), 1) < lengths[owner]).astype(F32)
        parts = []
        for h in range(wo.shape[0] // HEAD_DIM):
            cols = slice(h * HEAD_DIM, (h + 1) * HEAD_DIM)
            scores = lax.dot_general(
                qkv[held, 0, :, cols], qkv[held, 1, :, cols], (((1,), (1,)), ((), ())), preferred_element_type=F32
            ) * HEAD_DIM ** (-0.5)
            raised = jnp.exp(scores) * live
            probs = (raised / jnp.sum(raised, axis=-1, keepdims=True)).astype(BF)
            parts.append(jnp.dot(probs, qkv[held, 2, :, cols], preferred_element_type=F32).astype(BF))
        context = jnp.concatenate(parts, axis=1)
        for c in range(4):
            cols = slice(c * CHUNK, (c + 1) * CHUNK)
            csend[r, :, cols] = jnp.dot(context, wo[:, cols], preferred_element_type=F32).astype(BF)

        @pl.when(step == 1)
        def _():
            shares[2].start()
            shares[3].start()

        @pl.when(step == 2)
        def _():
            shares[0].start()

        @pl.when(step == 3)
        def _():
            shares[1].start()

        return 0

    lax.fori_loop(0, 4, section, 0)

    for base, source, came, goes in ((HALF, 1, 3, 5), (0, 2, 2, 4)):
        shares[came].wait_recv()

        def join(i, _, base=base, source=source):
            part = pl.ds(pl.multiple_of(base + i * 32, 32), 32)
            both = csend[source, part, :].astype(F32) + crecv[0, part, :].astype(F32)
            csend[source, part, :] = both.astype(BF)
            return 0

        lax.fori_loop(0, HALF // 32, join, 0)
        shares[goes].start()
    def second_norm(i, _):
        part = pl.ds(pl.multiple_of(i * 32, 32), 32)
        total = csend[0, part, :].astype(F32)
        for r in (1, 2):
            total = total + crecv[r, part, :].astype(F32)
        values = xv[part, :].astype(F32) + total
        resid[part, :] = values
        moe_in[part, :] = layer_norm(values, gains[1:2, :]).astype(BF)
        return 0

    def finish(half, _):
        @pl.when(half == 0)
        def _():
            shares[1].wait_recv()
            shares[5].wait_recv()

        @pl.when(half == 1)
        def _():
            shares[0].wait_recv()
            shares[4].wait_recv()

        lax.fori_loop(2 - 2 * half, 4 - 2 * half, second_norm, 0)
        return 0

    lax.fori_loop(0, 2, finish, 0)

    def dispatch(k, r):
        part = pl.ds(r * HALF, HALF)
        return send(dsend.at[k, part], arr.at[k, part], d_s.at[k, r], d_r.at[k, r], {"expert": peer(r)})

    placed = jnp.concatenate(place, axis=0)

    for k in range(arr.shape[0]):
        for j in range(DEPTH // CHUNK):
            cols = slice(k * DEPTH + j * CHUNK, k * DEPTH + (j + 1) * CHUNK)
            chosen = jnp.dot(placed, moe_in[:, cols], preferred_element_type=F32).astype(BF)
            dsend[k, :, j * CHUNK:(j + 1) * CHUNK] = chosen
            arr[k, 0:HALF, j * CHUNK:(j + 1) * CHUNK] = chosen[0:HALF, :]
        if k == 0:
            @pl.when(dp == 1)
            def _():
                pl.semaphore_wait(turn, 1)

        for r in (3, 1, 2):
            dispatch(k, r).start()

    small[3].wait()
    logits = lax.dot_general(
        router_t[...], moe_in[...].astype(F32), (((1,), (1,)), ((), ())),
        precision=highest, preferred_element_type=F32,
    )
    chosen0 = jnp.zeros((1, tokens), F32)
    chosen1 = jnp.zeros((1, tokens), F32)
    for e in range(4):
        chosen0 = chosen0 + (first == e).astype(F32) * logits[e:e + 1, :]
        chosen1 = chosen1 + (second == e).astype(F32) * logits[e:e + 1, :]
    gate0 = jax.nn.sigmoid(chosen0 - chosen1)
    gate1 = jax.nn.sigmoid(chosen1 - chosen0)
    slope = gate0 * gate1
    gate0 = jnp.broadcast_to(gate0, (tokens, tokens)).T[:, 0:1]
    gate1 = jnp.broadcast_to(gate1, (tokens, tokens)).T[:, 0:1]

    for r in (3, 1, 2):
        dispatch(0, r).wait_recv()

    @pl.when(dp == 0)
    def _():
        pl.semaphore_signal(turn, 1, device_id={"dp": 1}, device_id_type=MESH)

    def columns_first(c, _):
        win_copy(c).wait()
        acc[c] = jnp.dot(arr[0], win[c, 0:DEPTH, :], preferred_element_type=F32)
        return 0

    lax.fori_loop(0, win.shape[0], columns_first, 0)
    for r in (3, 1, 2):
        dispatch(1, r).wait_recv()

    def columns_last(c, _):
        got = jnp.dot(arr[1], win[c, DEPTH:2 * DEPTH, :], preferred_element_type=F32)
        cols = pl.ds(pl.multiple_of(c * WIDE, WIDE), WIDE)
        hidden[:, cols] = jnp.maximum(acc[c] + got, 0.0).astype(BF)
        return 0

    lax.fori_loop(0, win.shape[0], columns_last, 0)

    def give_back(c, r):
        part = pl.ds(r * HALF, HALF)
        return send(rsend.at[c, part], rrecv.at[c, part], r_s.at[c, r], r_r.at[c, r], {"expert": peer(r)})

    def expert_out(c, _):
        wout_copy(c).wait()
        got = jnp.dot(hidden[...], wout[c], preferred_element_type=F32).astype(BF)
        for j in range(CHUNK // STRIP):
            strip = got[:, j * STRIP:(j + 1) * STRIP]
            n = c * (CHUNK // STRIP) + j
            rsend[n] = strip
            rrecv[n, 0:HALF, :] = strip[0:HALF, :]
            for r in (3, 1, 2):
                give_back(n, r).start()
        return 0

    lax.fori_loop(0, wout.shape[0], expert_out, 0)
    local[4].wait()

    def onward(c):
        cols = pl.ds(pl.multiple_of(c * STRIP, STRIP), STRIP)
        return send(lo.at[c], acts_out.at[:, cols], z_s.at[c], z_r.at[c], {"segment": following})

    def combine(c, gap):
        for r in (3, 1, 2):
            give_back(c, r).wait_recv()
        cols = pl.ds(pl.multiple_of(c * STRIP, STRIP), STRIP)
        both = jnp.dot(back, rrecv[c], preferred_element_type=F32)
        sel0, sel1 = both[0:tokens, :], both[tokens:2 * tokens, :]
        lo[c] = (resid[:, cols] + (gate0 * sel0 + gate1 * sel1)).astype(BF)
        onward(c).start()
        terms = cot[:, cols].astype(F32) * (sel0 - sel1)
        for j in range(STRIP // tokens):
            gap = gap + terms[:, j * tokens:(j + 1) * tokens]
        return gap

    strips = rsend.shape[0]
    gap = lax.fori_loop(0, strips, combine, jnp.zeros((tokens, tokens), F32))
    gap_row = jnp.zeros((16, tokens), F32)
    for _ in range(3):
        part = gap.astype(BF)
        gap = gap - part.astype(F32)
        gap_row = gap_row + lax.dot_general(
            jnp.ones((16, tokens), BF), part, (((1,), (1,)), ((), ())), preferred_element_type=F32
        )
    delta = slope * gap_row[0:1, :]
    rest = jnp.concatenate(
        [delta * ((first == e).astype(F32) - (second == e).astype(F32)) for e in range(4)], axis=0
    )
    terms = []
    for _ in range(3):
        terms.append(rest.astype(BF))
        rest = rest - terms[-1].astype(F32)
    terms = jnp.concatenate([term.astype(F32) for term in terms] + [jnp.zeros((4, tokens), F32)], axis=0)
    products = jnp.dot(terms.astype(BF), moe_in[...], preferred_element_type=F32)
    grad = products[0:4, :] + products[4:8, :] + products[8:12, :]
    gsend[...] = jnp.concatenate(
        [grad[0:4, c * CHUNK:(c + 1) * CHUNK] for c in range(4)], axis=0
    ).astype(BF)

    def share(r, d):
        i = r * 2 + d
        device = {"expert": peer(r), "dp": lax.rem(dp + d, 2)}
        return send(gsend, grecv.at[i], g_s.at[i], g_r.at[i], device)

    for r, d in others:
        share(r, d).start()
    @pl.when(seg != 0)
    def _():
        mem_relay.wait_send()

    @pl.when(seg != 1)
    def _():
        mem_relay.wait_recv()

    for i in range(6):
        norm_ag[i].wait_send()

    @pl.when(seg != 0)
    def _():
        for i in (1, 3, 4, 5):
            mem_ag[i].wait_send()
        each_loan(lambda k, p: lend(behind, k, p).wait_send(), lambda k, p: keep(k, p).wait_send())

    @pl.when((seg != 0) & (dp == 1))
    def _():
        for i in early:
            mem_ag[i].wait_send()

    @pl.when(seg == 0)
    def _():
        for k, p in loans:
            for i in range(nearest[p], n_seg - 1):
                pass_on(i, k, p).wait_send()

    for r in (1, 2, 3):
        for c in range(arr.shape[0]):
            dispatch(c, r).wait_send()
        for c in range(strips):
            give_back(c, r).wait_send()
    for copy in shares:
        copy.wait_send()
    def drain(c, _):
        onward(c).wait_send()
        onward(c).wait_recv()
        return 0

    lax.fori_loop(0, strips - 1, drain, 0)
    for r, d in others:
        share(r, d).wait_recv()
    total = gsend[...].astype(F32)
    for r, d in others:
        total = total + grecv[r * 2 + d].astype(F32)
    total = total / (tokens * lax.axis_size("expert") * lax.axis_size("dp"))
    for c in range(4):
        grad_here[:, c * CHUNK:(c + 1) * CHUNK] = total[c * 4:(c + 1) * 4, :]

    for r, d in others:
        share(r, d).wait_send()
    done = pltpu.make_async_copy(grad_here, grad_out, small_sem.at[0])
    done.start()
    drain(strips - 1, 0)
    done.wait()


def hand_over(first_decoder, acts, kept, grad, acts_out, memory_out, grad_out):
    acts_out[...] = acts[...]
    memory_out[...] = jnp.where(first_decoder[0] == 1, acts[...], kept[...])
    grad_out[...] = grad[...]


def fused(
    x_in, memory, w_qkv, w_attn_out, norm_gains, router, w_in, w_exp_out, expert_ids, lengths, cotangent
):
    tokens, width = x_in.shape[2:]
    head_cols = w_attn_out.shape[1]
    hid = w_in.shape[2]
    n_in, n_out, strips, deep = hid // WIDE, width // CHUNK, width // STRIP, width // DEPTH
    n_seg = lax.axis_size("segment")
    hbm = pl.BlockSpec(memory_space=pl.ANY)
    vmem = pl.BlockSpec(memory_space=pltpu.VMEM)
    smem = pl.BlockSpec(memory_space=pltpu.SMEM)
    dma = pltpu.SemaphoreType.DMA
    acts, kept, grad = pl.pallas_call(
        tick,
        out_shape=(
            jax.ShapeDtypeStruct((tokens, width), BF),
            jax.ShapeDtypeStruct((tokens, width), BF),
            jax.ShapeDtypeStruct((4, width), F32),
        ),
        in_specs=[hbm] * 11,
        out_specs=(hbm, hbm, hbm),
        scratch_shapes=[
            pltpu.VMEM((2, width), F32),
            pltpu.VMEM((4, width), F32),
            pltpu.VMEM((2, tokens), jnp.int32),
            pltpu.SMEM((4,), jnp.int32),
            pltpu.VMEM((3, width, head_cols), BF),
            pltpu.VMEM((head_cols, width), BF),
            pltpu.VMEM((n_in, width, WIDE), BF),
            pltpu.VMEM((n_out, hid, CHUNK), BF),
            pltpu.VMEM((tokens, width), BF),
            pltpu.VMEM((2, 4, tokens, width), BF),
            pltpu.VMEM((3, 3, tokens, head_cols), BF),
            pltpu.VMEM((4, tokens, width), BF),
            pltpu.VMEM((3, tokens, width), BF),
            pltpu.VMEM((tokens, width), F32),
            pltpu.VMEM((tokens, width), BF),
            pltpu.VMEM((tokens, width), BF),
            pltpu.VMEM((deep, 4 * HALF, DEPTH), BF),
            pltpu.VMEM((deep, 4 * HALF, DEPTH), BF),
            pltpu.VMEM((n_in, 4 * HALF, WIDE), F32),
            pltpu.VMEM((4 * HALF, hid), BF),
            pltpu.VMEM((strips, 4 * HALF, STRIP), BF),
            pltpu.VMEM((strips, 4 * HALF, STRIP), BF),
            pltpu.VMEM((strips, tokens, STRIP), BF),
            pltpu.VMEM((16, CHUNK), BF),
            pltpu.VMEM((8, 16, CHUNK), BF),
            dma((5,)), dma((n_in,)), dma((n_out,)),
            dma((2, 6)), dma((2, 6)), dma((6,)), dma((6,)), dma((deep, 4)), dma((deep, 4)),
            dma((strips, 4)), dma((strips, 4)), dma((strips,)), dma((strips,)),
            dma((8,)), dma((8,)), dma((1,)), dma((1,)), dma((4,)), pltpu.SemaphoreType.REGULAR,
            pltpu.VMEM((4, width), F32),
            pltpu.VMEM((n_seg - 1, 2, LOAN, width), BF),
            dma((2, LOAN // PIECE)), dma((n_seg - 1, 2, LOAN // PIECE)),
            dma((n_seg - 1, 2, LOAN // PIECE)), dma((2, LOAN // PIECE)), dma((2, LOAN // PIECE)), dma((2, LOAN // PIECE)),
        ],
        compiler_params=pltpu.CompilerParams(
            collective_id=0, has_side_effects=True, vmem_limit_bytes=64 * 2**20 - 2**18
        ),
    )(
        x_in[0, 0], memory[0, 0], w_qkv[0], w_attn_out[0], norm_gains[0], router[0].T, w_in[0],
        w_exp_out[0], expert_ids[0, 0].T, lengths[0, 0], cotangent[0, 0],
    )
    first_decoder = (lax.axis_index("segment") == 1).astype(jnp.int32).reshape(1)
    acts, kept, grad = pl.pallas_call(
        hand_over,
        out_shape=(acts, kept, grad),
        in_specs=[smem, vmem, vmem, vmem],
        out_specs=(vmem, vmem, vmem),
    )(first_decoder, acts, kept, grad)
    return acts[None, None], kept[None, None], grad.T[None]


def solution(mesh):
    small = (mesh.shape["expert"], mesh.shape["dp"]) == (4, 2) and mesh.shape["segment"] > 2
    placed = (
        P("segment", "dp", "expert", None),
        P("segment", "dp", "expert", None),
        P("segment", None, None, "expert"),
        P("segment", "expert", None),
        P("segment", None, None),
        P("segment", None, None),
        P("segment", None, "expert"),
        P("segment", "expert", None),
        P("segment", "dp", "expert", None),
        P("segment", "dp", None),
        P("segment", "dp", "expert", None),
    )
    return jax.shard_map(
        fused if small else shards,
        mesh=mesh,
        in_specs=placed,
        out_specs=(
            P("segment", "dp", "expert", None),
            P("segment", "dp", "expert", None),
            P("segment", None, None),
        ),
        check_vma=False,
    )
```

```python
import jax
import jax.numpy as jnp
from jax import lax
from jax.experimental import pallas as pl
from jax.experimental.pallas import tpu as pltpu
from jax.sharding import PartitionSpec as P

HEAD_DIM = 128
TOP = 2
SEQ = 128


eps = 1e-05
highest = lax.Precision.HIGHEST


def from_behind(block, axis, distance):
    devices = range(lax.axis_size(axis))
    route = [((i - distance) % len(devices), i) for i in devices]
    return lax.ppermute(block, axis, route)


def layer_norm(values, gain):
    centered = values - jnp.mean(values, axis=-1, keepdims=True)
    variance = jnp.mean(centered * centered, axis=-1, keepdims=True)
    return centered * lax.rsqrt(variance + eps) * gain


def shards(
    x_in,
    memory,
    w_qkv,
    w_attn_out,
    norm_gains,
    router,
    w_in,
    w_exp_out,
    expert_ids,
    lengths,
    cotangent,
):
    segment_pos = lax.axis_index("segment")
    rows_here = x_in[0, 0]
    tok_dev = rows_here.shape[0]
    width = rows_here.shape[1]
    head_cols = w_attn_out.shape[1]
    gains = norm_gains[0]
    weights_qkv = w_qkv[0]
    normed = layer_norm(rows_here.astype(jnp.float32), gains[0]).astype(jnp.bfloat16)
    key_source = jnp.where(segment_pos == 0, normed, memory[0, 0])
    stacked = jnp.stack((normed, key_source), axis=0)
    piece = lax.all_gather(stacked, "expert", axis=1, tiled=True)
    query = jnp.dot(piece[0], weights_qkv[0], preferred_element_type=jnp.float32)
    keys = jnp.dot(piece[1], weights_qkv[1], preferred_element_type=jnp.float32)
    values = jnp.dot(piece[1], weights_qkv[2], preferred_element_type=jnp.float32)
    projected = jnp.concatenate((query, keys, values), axis=1).astype(jnp.bfloat16)
    group_rows = projected.shape[0]
    count = group_rows // SEQ
    heads_here = head_cols // HEAD_DIM
    shaped = projected.reshape(count, SEQ, 3, heads_here, HEAD_DIM)
    scores = jnp.einsum(
        "nihd,njhd->nhij", shaped[:, :, 0], shaped[:, :, 1], preferred_element_type=jnp.float32
    ) * HEAD_DIM ** (-0.5)
    live = (jnp.arange(SEQ)[None, :] < lengths[0, 0][:, None]).astype(jnp.float32)
    raised = jnp.exp(scores) * live[:, None, None, :]
    probs = (raised / jnp.sum(raised, axis=-1, keepdims=True)).astype(jnp.bfloat16)
    context = jnp.einsum(
        "nhij,njhd->nihd", probs, shaped[:, :, 2], preferred_element_type=jnp.float32
    )
    context = context.astype(jnp.bfloat16).reshape(group_rows, head_cols)
    attn_sum = lax.psum_scatter(
        jnp.dot(context, w_attn_out[0], preferred_element_type=jnp.float32).astype(jnp.bfloat16),
        "expert",
        scatter_dimension=0,
        tiled=True,
    ).astype(jnp.float32)
    resid = rows_here.astype(jnp.float32) + attn_sum
    moe_in = layer_norm(resid, gains[1]).astype(jnp.bfloat16)
    moe_wide = moe_in.astype(jnp.float32)
    logits = jnp.dot(moe_wide, router[0], precision=highest)
    ids = expert_ids[0, 0]
    n_exp = router.shape[2]
    pick_int = (ids[:, :, None] == jnp.arange(n_exp)[None, None, :]).astype(jnp.int32)
    pick = pick_int.astype(jnp.float32)
    chosen = jnp.sum(pick * logits[:, None, :], axis=2)
    gates = jax.nn.sigmoid(chosen - chosen[:, ::-1])
    flat_pick = pick_int.reshape(tok_dev * TOP, n_exp)
    assigned = flat_pick.shape[0]
    earlier = (jnp.arange(assigned)[:, None] > jnp.arange(assigned)[None, :]).astype(jnp.bfloat16)
    before = jnp.dot(
        earlier, flat_pick.astype(jnp.bfloat16), preferred_element_type=jnp.float32
    ).astype(jnp.int32)
    slot = jnp.sum(before * flat_pick, axis=1)
    capacity = tok_dev * TOP // n_exp
    target = ids.reshape(-1) * capacity + slot
    place = (jnp.arange(n_exp * capacity)[:, None] == target[None, :]).astype(jnp.bfloat16)
    place = jnp.sum(place.reshape(n_exp * capacity, tok_dev, TOP), axis=2)
    send_rows = jnp.dot(place, moe_in, preferred_element_type=jnp.float32).astype(jnp.bfloat16)
    copies = lax.axis_size("expert") // n_exp
    outgoing = jnp.broadcast_to(
        send_rows.reshape(n_exp, 1, capacity, width), (n_exp, copies, capacity, width)
    )
    outgoing = outgoing.reshape(n_exp * copies, capacity, width)
    arrived = lax.all_to_all(outgoing, "expert", split_axis=0, concat_axis=0, tiled=True)
    sources = arrived.shape[0]
    slots_now = arrived.shape[1]
    flat = arrived.reshape(sources * slots_now, width)
    hidden = jnp.maximum(jnp.dot(flat, w_in[0], preferred_element_type=jnp.float32), 0.0).astype(
        jnp.bfloat16
    )
    partial_value = jnp.dot(hidden, w_exp_out[0], preferred_element_type=jnp.float32).astype(
        jnp.bfloat16
    )
    returned = lax.all_to_all(
        partial_value.reshape(sources, slots_now, width),
        "expert",
        split_axis=0,
        concat_axis=0,
        tiled=True,
    )
    expert_out = jnp.sum(
        returned.reshape(n_exp, copies, capacity, width).astype(jnp.float32), axis=1
    )
    expert_out = expert_out.reshape(n_exp * capacity, width)
    selected = expert_out[target].reshape(tok_dev, TOP, width)
    mixed = jnp.sum(gates[:, :, None] * selected, axis=1)
    layer_out = (resid + mixed).astype(jnp.bfloat16)
    cot = cotangent[0, 0].astype(jnp.float32)
    intersection = jnp.sum(cot[:, None, :] * selected, axis=2)
    delta = gates[:, 0] * gates[:, 1] * (intersection[:, 0] - intersection[:, 1])
    dlogits = delta[:, None] * (pick[:, 0] - pick[:, 1])
    local_grad = lax.dot_general(moe_wide, dlogits, (((0,), (0,)), ((), ())), precision=highest)
    total_rows = tok_dev * lax.axis_size("expert") * lax.axis_size("dp")
    router_grad = (
        lax.psum(local_grad.astype(jnp.bfloat16), ("expert", "dp")).astype(jnp.float32) / total_rows
    )
    carry = jnp.where(segment_pos == 0, layer_out, memory[0, 0])
    handed = from_behind(jnp.stack((layer_out, carry), axis=0), "segment", 1)
    return (handed[0][None, None], handed[1][None, None], router_grad[None])


BF = jnp.bfloat16
F32 = jnp.float32
MESH = pl.DeviceIdType.MESH
HALF = 64
CHUNK = 512
DEPTH = 1024
STRIP = 256
WIDE = 1024
LOAN = 32
PIECE = 16
LENDERS = (0, 1)


def tick(
    x_hbm, mem_hbm, wqkv_hbm, wo_hbm, gains_hbm, router_hbm, win_hbm, wout_hbm, ids_hbm, lengths_hbm, cot_hbm,
    acts_out, memory_out, grad_out,
    gains, router_t, ids_t, lengths, wqkv, wo, win, wout, xv, rows, qkv, csend, crecv, resid, moe_in, cot,
    dsend, arr, acc, hidden, rsend, rrecv, lo, gsend, grecv,
    wsem, winsem, woutsem, ag_s, ag_r, c_s, c_r, d_s, d_r, r_s, r_r, z_s, z_r, g_s, g_r, m_s, m_r, small_sem, turn, grad_here,
    loan, ld_s, ld_r, lu_s, lu_r, near_s, near_r,
):
    seg = lax.axis_index("segment")
    exp = lax.axis_index("expert")
    dp = lax.axis_index("dp")
    n_seg = lax.axis_size("segment")
    following = lax.rem(seg + 1, n_seg)
    behind = lax.rem(seg + n_seg - 1, n_seg)
    col = lax.rem(exp, 2)
    row = exp // 2

    def peer(r):
        return lax.rem(col + r % 2, 2) + 2 * lax.rem(row + r // 2, 2)

    def send(src, dst, s, r, device):
        return pltpu.make_async_remote_copy(
            src_ref=src, dst_ref=dst, send_sem=s, recv_sem=r, device_id=device, device_id_type=MESH
        )

    local = [
        pltpu.make_async_copy(mem_hbm, rows.at[1, 0], wsem.at[0]),
        pltpu.make_async_copy(x_hbm, xv, wsem.at[1]),
        pltpu.make_async_copy(wqkv_hbm, wqkv, wsem.at[2]),
        pltpu.make_async_copy(wo_hbm, wo, wsem.at[3]),
        pltpu.make_async_copy(cot_hbm, cot, wsem.at[4]),
    ]
    small = [
        pltpu.make_async_copy(gains_hbm, gains, small_sem.at[0]),
        pltpu.make_async_copy(lengths_hbm, lengths, small_sem.at[1]),
        pltpu.make_async_copy(ids_hbm, ids_t, small_sem.at[2]),
        pltpu.make_async_copy(router_hbm, router_t, small_sem.at[3]),
    ]
    def win_copy(c):
        part = pl.ds(pl.multiple_of(c * WIDE, WIDE), WIDE)
        return pltpu.make_async_copy(win_hbm.at[:, part], win.at[c], winsem.at[c])

    def wout_copy(c):
        part = pl.ds(pl.multiple_of(c * CHUNK, CHUNK), CHUNK)
        return pltpu.make_async_copy(wout_hbm.at[:, part], wout.at[c], woutsem.at[c])

    barrier = pltpu.get_barrier_semaphore()
    others = [(r, d) for r in range(4) for d in range(2) if r + d > 0]
    for r, d in others:
        pl.semaphore_signal(
            barrier, 1, device_id={"expert": peer(r), "dp": lax.rem(dp + d, 2)}, device_id_type=MESH
        )
    pl.semaphore_signal(barrier, 1, device_id={"segment": behind}, device_id_type=MESH)

    @pl.when(seg == 0)
    def _():
        for far in range(1, n_seg):
            for r in (1, 2):
                pl.semaphore_signal(barrier, 1, device_id={"segment": far, "expert": peer(r)}, device_id_type=MESH)

    @pl.when(seg != 0)
    def _():
        pl.semaphore_signal(barrier, 1, device_id={"segment": 0}, device_id_type=MESH)

    for copy in (local[0], local[1], small[0], small[1], *local[2:], *small[2:]):
        copy.start()

    top, low = pl.ds(0, HALF), pl.ds(HALF, HALF)

    def gather_copies(a):
        along_x, along_y = {"expert": peer(1)}, {"expert": peer(2)}
        low_rest, top_rest = (pl.ds(HALF + a * LOAN, HALF - a * LOAN), pl.ds(a * LOAN, HALF - a * LOAN))
        plan = [
            (0, top, 1, along_x), (0, low_rest, 1, along_x), (0, low, 2, along_y), (0, top_rest, 2, along_y),
            (1, top, 3, along_y), (2, low, 3, along_x),
        ]
        return [
            send(rows.at[a, source, part], rows.at[a, slot, part], ag_s.at[a, i], ag_r.at[a, i], dev)
            for i, (source, part, slot, dev) in enumerate(plan)
        ]

    along_x, along_y = {"expert": peer(1)}, {"expert": peer(2)}
    plan = [
        (1, top, 1, along_x), (2, low, 2, along_y), (3, top, 0, along_x), (3, low, 0, along_y),
        (2, top, 2, along_y), (1, low, 1, along_x),
    ]
    shares = [
        send(csend.at[source, part], crecv.at[slot, part], c_s.at[i], c_r.at[i], dev)
        for i, (source, part, slot, dev) in enumerate(plan)
    ]
    norm_ag, mem_ag = gather_copies(0), gather_copies(1)
    loans = [(k, p) for p in range(LOAN // PIECE) for k in range(2)]

    nearest = [n_seg - 1 - LENDERS[p] if LENDERS[p] else 0 for p in range(LOAN // PIECE)]

    def keep(k, p):
        part = pl.ds(HALF * (1 - k) + p * PIECE, PIECE)
        spot = rows.at[1, 1 + k, part]
        return send(rows.at[1, 0, part], spot, near_s.at[k, p], near_r.at[k, p], {"expert": peer(1 + k)})

    def each_loan(lent, kept=None):
        for k, p in loans:
            @pl.when(seg > nearest[p])
            def _(k=k, p=p):
                lent(k, p)

            if kept is not None and nearest[p] > 0:
                @pl.when((seg != 0) & (seg <= nearest[p]))
                def _(k=k, p=p):
                    kept(k, p)

    def lend(i, k, p):
        part = pl.ds(HALF * (1 - k) + p * PIECE, PIECE)
        device = {"segment": 0, "expert": peer(1 + k)}
        spot = loan.at[i, k, pl.ds(p * PIECE, PIECE)]
        return send(rows.at[1, 0, part], spot, ld_s.at[k, p], ld_r.at[i, k, p], device)

    def pass_on(i, k, p):
        part = pl.ds(HALF * (1 - k) + p * PIECE, PIECE)
        spot = loan.at[i, k, pl.ds(p * PIECE, PIECE)]
        return send(spot, rows.at[1, 1 + k, part], lu_s.at[i, k, p], lu_r.at[k, p], {"segment": i + 1})

    mem_relay = send(rows.at[1, 0], memory_out, m_s.at[0], m_r.at[0], {"segment": following})

    local[0].wait()

    @pl.when(seg == 0)
    def _():
        pl.semaphore_wait(barrier, len(others) + n_seg)

    @pl.when(seg != 0)
    def _():
        pl.semaphore_wait(barrier, len(others) + 3)

    early, late = (0, 2), (1, 3)

    @pl.when((seg != 0) & (dp == 0))
    def _():
        for i in early:
            mem_ag[i].start()

    each_loan(lambda k, p: lend(behind, k, p).start())

    local[1].wait()
    small[0].wait()

    def norm_rows(i, _):
        part = pl.ds(pl.multiple_of(i * 32, 32), 32)
        values = xv[part, :].astype(F32)
        normed = layer_norm(values, gains[0:1, :]).astype(BF)
        rows[0, 0, part, :] = normed
        return 0

    lax.fori_loop(0, 4, norm_rows, 0)

    @pl.when((dp == 0))
    def _():
        for i in early:
            norm_ag[i].start()

    def start_weights(c, _):
        win_copy(c).start()
        return 0

    def start_weights_out(c, _):
        wout_copy(c).start()
        return 0

    lax.fori_loop(0, win.shape[0], start_weights, 0)
    lax.fori_loop(0, wout.shape[0], start_weights_out, 0)

    @pl.when((dp == 0) & (seg != 0))
    def _():
        for i in early:
            mem_ag[i].wait_send()

    @pl.when((dp == 0) & (seg == 0))
    def _():
        pl.semaphore_signal(turn, 1, device_id={"dp": 1}, device_id_type=MESH)

    @pl.when(dp == 1)
    def _():
        pl.semaphore_wait(turn, 1)

        @pl.when(seg != 0)
        def _():
            for i in early:
                mem_ag[i].start()

        for i in early:
            norm_ag[i].start()

    @pl.when(seg == 0)
    def _():
        for i in early:
            norm_ag[i].wait_recv()
            norm_ag[4 + i // 2].start()
        for i in late:
            norm_ag[i].start()
        for k, p in loans:
            for i in reversed(range(nearest[p], n_seg - 1)):
                lend(i, k, p).wait_recv()
                pass_on(i, k, p).start()

    local[2].wait()
    local[3].wait()
    small[1].wait()

    tokens = SEQ
    small[2].wait()
    first, second = ids_t[0:1, :], ids_t[1:2, :]
    earlier = (
        lax.broadcasted_iota(jnp.int32, (tokens, tokens), 0)
        < lax.broadcasted_iota(jnp.int32, (tokens, tokens), 1)
    ).astype(BF)
    place, pick0, pick1 = [], [], []
    slot_no = lax.broadcasted_iota(jnp.int32, (HALF, tokens), 0).astype(F32)
    for r in range(4):
        one = (first == peer(r)).astype(F32)
        two = (second == peer(r)).astype(F32)
        named = one + two
        slot = jnp.dot(
            jnp.broadcast_to(named, (16, tokens)).astype(BF), earlier, preferred_element_type=F32
        )[0:1, :]
        hit = (slot_no == slot).astype(F32)
        place.append((hit * named).astype(BF))
        pick0.append(hit * one)
        pick1.append(hit * two)
    back = jnp.concatenate(
        [jnp.concatenate(pick0, axis=0).T, jnp.concatenate(pick1, axis=0).T], axis=0
    ).astype(BF)

    @pl.when((dp == 0) & (seg != 0))
    def _():
        pl.semaphore_signal(turn, 1, device_id={"dp": 1}, device_id_type=MESH)

    def project(r, j):
        source = ((j + 1) // 2) * ((seg + n_seg - 1) // n_seg)
        got = jnp.dot(rows[source, r], wqkv[j], preferred_element_type=F32)
        qkv[lax.rem(r, 3), j] = got.astype(BF)

    def section(step, _):
        r = (lax.rem(step + 1, 3) + 1) * ((step + 2) // 3)

        @pl.when((step == 1) & (seg != 0))
        def _():
            for i in early:
                mem_ag[i].wait_recv()
                mem_ag[4 + i // 2].start()
            for i in early:
                norm_ag[i].wait_recv()
                norm_ag[4 + i // 2].start()
            each_loan(lambda k, p: None, lambda k, p: keep(k, p).start())
            for i in late:
                mem_ag[i].start()
            for i in late:
                norm_ag[i].start()
            for i in (4, 5):
                mem_ag[i].wait_recv()

        @pl.when(step == 1)
        def _():
            for i in (4, 5):
                norm_ag[i].wait_recv()

        @pl.when((step == 2) & (seg != 0))
        def _():
            for i in late:
                mem_ag[i].wait_recv()
            each_loan(lambda k, p: pass_on(0, k, p).wait_recv(), lambda k, p: keep(k, p).wait_recv())
            mem_relay.start()

        @pl.when(step == 2)
        def _():
            @pl.when(seg == 0)
            def _():
                for i in late:
                    norm_ag[i].wait_recv()

            def keys_values(n, _):
                project(1 + n // 2, 1 + lax.rem(n, 2))
                return 0

            lax.fori_loop(0, 4, keys_values, 0)

            @pl.when(seg != 0)
            def _():
                for i in late:
                    norm_ag[i].wait_recv()

        def project_step(j, _):
            project(r, j)
            return 0

        lax.fori_loop(0, 3 - 2 * (step // 2), project_step, 0)
        owner = peer(r)
        held = lax.rem(r, 3)
        live = (lax.broadcasted_iota(jnp.int32, (1, SEQ), 1) < lengths[owner]).astype(F32)
        parts = []
        for h in range(wo.shape[0] // HEAD_DIM):
            cols = slice(h * HEAD_DIM, (h + 1) * HEAD_DIM)
            scores = lax.dot_general(
                qkv[held, 0, :, cols], qkv[held, 1, :, cols], (((1,), (1,)), ((), ())), preferred_element_type=F32
            ) * HEAD_DIM ** (-0.5)
            raised = jnp.exp(scores) * live
            probs = (raised / jnp.sum(raised, axis=-1, keepdims=True)).astype(BF)
            parts.append(jnp.dot(probs, qkv[held, 2, :, cols], preferred_element_type=F32).astype(BF))
        context = jnp.concatenate(parts, axis=1)
        for c in range(4):
            cols = slice(c * CHUNK, (c + 1) * CHUNK)
            csend[r, :, cols] = jnp.dot(context, wo[:, cols], preferred_element_type=F32).astype(BF)

        @pl.when(step == 1)
        def _():
            shares[2].start()
            shares[3].start()

        @pl.when(step == 2)
        def _():
            shares[0].start()

        @pl.when(step == 3)
        def _():
            shares[1].start()

        return 0

    lax.fori_loop(0, 4, section, 0)

    for base, source, came, goes in ((HALF, 1, 3, 5), (0, 2, 2, 4)):
        shares[came].wait_recv()

        def join(i, _, base=base, source=source):
            part = pl.ds(pl.multiple_of(base + i * 32, 32), 32)
            both = csend[source, part, :].astype(F32) + crecv[0, part, :].astype(F32)
            csend[source, part, :] = both.astype(BF)
            return 0

        lax.fori_loop(0, HALF // 32, join, 0)
        shares[goes].start()
    def second_norm(i, _):
        part = pl.ds(pl.multiple_of(i * 32, 32), 32)
        total = csend[0, part, :].astype(F32)
        for r in (1, 2):
            total = total + crecv[r, part, :].astype(F32)
        values = xv[part, :].astype(F32) + total
        resid[part, :] = values
        moe_in[part, :] = layer_norm(values, gains[1:2, :]).astype(BF)
        return 0

    def finish(half, _):
        @pl.when(half == 0)
        def _():
            shares[1].wait_recv()
            shares[5].wait_recv()

        @pl.when(half == 1)
        def _():
            shares[0].wait_recv()
            shares[4].wait_recv()

        lax.fori_loop(2 - 2 * half, 4 - 2 * half, second_norm, 0)
        return 0

    lax.fori_loop(0, 2, finish, 0)

    def dispatch(k, r):
        part = pl.ds(r * HALF, HALF)
        return send(dsend.at[k, part], arr.at[k, part], d_s.at[k, r], d_r.at[k, r], {"expert": peer(r)})

    placed = jnp.concatenate(place, axis=0)

    for k in range(arr.shape[0]):
        for j in range(DEPTH // CHUNK):
            cols = slice(k * DEPTH + j * CHUNK, k * DEPTH + (j + 1) * CHUNK)
            chosen = jnp.dot(placed, moe_in[:, cols], preferred_element_type=F32).astype(BF)
            dsend[k, :, j * CHUNK:(j + 1) * CHUNK] = chosen
            arr[k, 0:HALF, j * CHUNK:(j + 1) * CHUNK] = chosen[0:HALF, :]
        if k == 0:
            @pl.when(dp == 1)
            def _():
                pl.semaphore_wait(turn, 1)

        for r in (3, 1, 2):
            dispatch(k, r).start()

    small[3].wait()
    logits = lax.dot_general(
        router_t[...], moe_in[...].astype(F32), (((1,), (1,)), ((), ())),
        precision=highest, preferred_element_type=F32,
    )
    chosen0 = jnp.zeros((1, tokens), F32)
    chosen1 = jnp.zeros((1, tokens), F32)
    for e in range(4):
        chosen0 = chosen0 + (first == e).astype(F32) * logits[e:e + 1, :]
        chosen1 = chosen1 + (second == e).astype(F32) * logits[e:e + 1, :]
    gate0 = jax.nn.sigmoid(chosen0 - chosen1)
    gate1 = jax.nn.sigmoid(chosen1 - chosen0)
    slope = gate0 * gate1
    gate0 = jnp.broadcast_to(gate0, (tokens, tokens)).T[:, 0:1]
    gate1 = jnp.broadcast_to(gate1, (tokens, tokens)).T[:, 0:1]

    for r in (3, 1, 2):
        dispatch(0, r).wait_recv()

    @pl.when(dp == 0)
    def _():
        pl.semaphore_signal(turn, 1, device_id={"dp": 1}, device_id_type=MESH)

    def columns_first(c, _):
        win_copy(c).wait()
        acc[c] = jnp.dot(arr[0], win[c, 0:DEPTH, :], preferred_element_type=F32)
        return 0

    lax.fori_loop(0, win.shape[0], columns_first, 0)
    for r in (3, 1, 2):
        dispatch(1, r).wait_recv()

    def columns_last(c, _):
        got = jnp.dot(arr[1], win[c, DEPTH:2 * DEPTH, :], preferred_element_type=F32)
        cols = pl.ds(pl.multiple_of(c * WIDE, WIDE), WIDE)
        hidden[:, cols] = jnp.maximum(acc[c] + got, 0.0).astype(BF)
        return 0

    lax.fori_loop(0, win.shape[0], columns_last, 0)

    def give_back(c, r):
        part = pl.ds(r * HALF, HALF)
        return send(rsend.at[c, part], rrecv.at[c, part], r_s.at[c, r], r_r.at[c, r], {"expert": peer(r)})

    def expert_out(c, _):
        wout_copy(c).wait()
        got = jnp.dot(hidden[...], wout[c], preferred_element_type=F32).astype(BF)
        for j in range(CHUNK // STRIP):
            strip = got[:, j * STRIP:(j + 1) * STRIP]
            n = c * (CHUNK // STRIP) + j
            rsend[n] = strip
            rrecv[n, 0:HALF, :] = strip[0:HALF, :]
            for r in (3, 1, 2):
                give_back(n, r).start()
        return 0

    lax.fori_loop(0, wout.shape[0], expert_out, 0)
    local[4].wait()

    def onward(c):
        cols = pl.ds(pl.multiple_of(c * STRIP, STRIP), STRIP)
        return send(lo.at[c], acts_out.at[:, cols], z_s.at[c], z_r.at[c], {"segment": following})

    def combine(c, gap):
        for r in (3, 1, 2):
            give_back(c, r).wait_recv()
        cols = pl.ds(pl.multiple_of(c * STRIP, STRIP), STRIP)
        both = jnp.dot(back, rrecv[c], preferred_element_type=F32)
        sel0, sel1 = both[0:tokens, :], both[tokens:2 * tokens, :]
        lo[c] = (resid[:, cols] + (gate0 * sel0 + gate1 * sel1)).astype(BF)
        onward(c).start()
        terms = cot[:, cols].astype(F32) * (sel0 - sel1)
        for j in range(STRIP // tokens):
            gap = gap + terms[:, j * tokens:(j + 1) * tokens]
        return gap

    strips = rsend.shape[0]
    gap = lax.fori_loop(0, strips, combine, jnp.zeros((tokens, tokens), F32))
    gap_row = jnp.zeros((16, tokens), F32)
    for _ in range(3):
        part = gap.astype(BF)
        gap = gap - part.astype(F32)
        gap_row = gap_row + lax.dot_general(
            jnp.ones((16, tokens), BF), part, (((1,), (1,)), ((), ())), preferred_element_type=F32
        )
    delta = slope * gap_row[0:1, :]
    rest = jnp.concatenate(
        [delta * ((first == e).astype(F32) - (second == e).astype(F32)) for e in range(4)], axis=0
    )
    terms = []
    for _ in range(3):
        terms.append(rest.astype(BF))
        rest = rest - terms[-1].astype(F32)
    terms = jnp.concatenate([term.astype(F32) for term in terms] + [jnp.zeros((4, tokens), F32)], axis=0)
    products = jnp.dot(terms.astype(BF), moe_in[...], preferred_element_type=F32)
    grad = products[0:4, :] + products[4:8, :] + products[8:12, :]
    gsend[...] = jnp.concatenate(
        [grad[0:4, c * CHUNK:(c + 1) * CHUNK] for c in range(4)], axis=0
    ).astype(BF)

    def share(r, d):
        i = r * 2 + d
        device = {"expert": peer(r), "dp": lax.rem(dp + d, 2)}
        return send(gsend, grecv.at[i], g_s.at[i], g_r.at[i], device)

    for r, d in others:
        share(r, d).start()
    @pl.when(seg != 0)
    def _():
        mem_relay.wait_send()

    @pl.when(seg != 1)
    def _():
        mem_relay.wait_recv()

    for i in range(6):
        norm_ag[i].wait_send()

    @pl.when(seg != 0)
    def _():
        for i in (1, 3, 4, 5):
            mem_ag[i].wait_send()
        each_loan(lambda k, p: lend(behind, k, p).wait_send(), lambda k, p: keep(k, p).wait_send())

    @pl.when((seg != 0) & (dp == 1))
    def _():
        for i in early:
            mem_ag[i].wait_send()

    @pl.when(seg == 0)
    def _():
        for k, p in loans:
            for i in range(nearest[p], n_seg - 1):
                pass_on(i, k, p).wait_send()

    for r in (1, 2, 3):
        for c in range(arr.shape[0]):
            dispatch(c, r).wait_send()
        for c in range(strips):
            give_back(c, r).wait_send()
    for copy in shares:
        copy.wait_send()
    def drain(c, _):
        onward(c).wait_send()
        onward(c).wait_recv()
        return 0

    lax.fori_loop(0, strips - 1, drain, 0)
    for r, d in others:
        share(r, d).wait_recv()
    total = gsend[...].astype(F32)
    for r, d in others:
        total = total + grecv[r * 2 + d].astype(F32)
    total = total / (tokens * lax.axis_size("expert") * lax.axis_size("dp"))
    for c in range(4):
        grad_here[:, c * CHUNK:(c + 1) * CHUNK] = total[c * 4:(c + 1) * 4, :]

    for r, d in others:
        share(r, d).wait_send()
    done = pltpu.make_async_copy(grad_here, grad_out, small_sem.at[0])
    done.start()
    drain(strips - 1, 0)
    done.wait()


def hand_over(first_decoder, acts, kept, grad, acts_out, memory_out, grad_out):
    acts_out[...] = acts[...]
    memory_out[...] = jnp.where(first_decoder[0] == 1, acts[...], kept[...])
    grad_out[...] = grad[...]


def fused(
    x_in, memory, w_qkv, w_attn_out, norm_gains, router, w_in, w_exp_out, expert_ids, lengths, cotangent
):
    tokens, width = x_in.shape[2:]
    head_cols = w_attn_out.shape[1]
    hid = w_in.shape[2]
    n_in, n_out, strips, deep = hid // WIDE, width // CHUNK, width // STRIP, width // DEPTH
    n_seg = lax.axis_size("segment")
    hbm = pl.BlockSpec(memory_space=pl.ANY)
    vmem = pl.BlockSpec(memory_space=pltpu.VMEM)
    smem = pl.BlockSpec(memory_space=pltpu.SMEM)
    dma = pltpu.SemaphoreType.DMA
    acts, kept, grad = pl.pallas_call(
        tick,
        out_shape=(
            jax.ShapeDtypeStruct((tokens, width), BF),
            jax.ShapeDtypeStruct((tokens, width), BF),
            jax.ShapeDtypeStruct((4, width), F32),
        ),
        in_specs=[hbm] * 11,
        out_specs=(hbm, hbm, hbm),
        scratch_shapes=[
            pltpu.VMEM((2, width), F32),
            pltpu.VMEM((4, width), F32),
            pltpu.VMEM((2, tokens), jnp.int32),
            pltpu.SMEM((4,), jnp.int32),
            pltpu.VMEM((3, width, head_cols), BF),
            pltpu.VMEM((head_cols, width), BF),
            pltpu.VMEM((n_in, width, WIDE), BF),
            pltpu.VMEM((n_out, hid, CHUNK), BF),
            pltpu.VMEM((tokens, width), BF),
            pltpu.VMEM((2, 4, tokens, width), BF),
            pltpu.VMEM((3, 3, tokens, head_cols), BF),
            pltpu.VMEM((4, tokens, width), BF),
            pltpu.VMEM((3, tokens, width), BF),
            pltpu.VMEM((tokens, width), F32),
            pltpu.VMEM((tokens, width), BF),
            pltpu.VMEM((tokens, width), BF),
            pltpu.VMEM((deep, 4 * HALF, DEPTH), BF),
            pltpu.VMEM((deep, 4 * HALF, DEPTH), BF),
            pltpu.VMEM((n_in, 4 * HALF, WIDE), F32),
            pltpu.VMEM((4 * HALF, hid), BF),
            pltpu.VMEM((strips, 4 * HALF, STRIP), BF),
            pltpu.VMEM((strips, 4 * HALF, STRIP), BF),
            pltpu.VMEM((strips, tokens, STRIP), BF),
            pltpu.VMEM((16, CHUNK), BF),
            pltpu.VMEM((8, 16, CHUNK), BF),
            dma((5,)), dma((n_in,)), dma((n_out,)),
            dma((2, 6)), dma((2, 6)), dma((6,)), dma((6,)), dma((deep, 4)), dma((deep, 4)),
            dma((strips, 4)), dma((strips, 4)), dma((strips,)), dma((strips,)),
            dma((8,)), dma((8,)), dma((1,)), dma((1,)), dma((4,)), pltpu.SemaphoreType.REGULAR,
            pltpu.VMEM((4, width), F32),
            pltpu.VMEM((n_seg - 1, 2, LOAN, width), BF),
            dma((2, LOAN // PIECE)), dma((n_seg - 1, 2, LOAN // PIECE)),
            dma((n_seg - 1, 2, LOAN // PIECE)), dma((2, LOAN // PIECE)), dma((2, LOAN // PIECE)), dma((2, LOAN // PIECE)),
        ],
        compiler_params=pltpu.CompilerParams(
            collective_id=0, has_side_effects=True, vmem_limit_bytes=64 * 2**20 - 2**18
        ),
    )(
        x_in[0, 0], memory[0, 0], w_qkv[0], w_attn_out[0], norm_gains[0], router[0].T, w_in[0],
        w_exp_out[0], expert_ids[0, 0].T, lengths[0, 0], cotangent[0, 0],
    )
    first_decoder = (lax.axis_index("segment") == 1).astype(jnp.int32).reshape(1)
    acts, kept, grad = pl.pallas_call(
        hand_over,
        out_shape=(acts, kept, grad),
        in_specs=[smem, vmem, vmem, vmem],
        out_specs=(vmem, vmem, vmem),
    )(first_decoder, acts, kept, grad)
    return acts[None, None], kept[None, None], grad.T[None]


def solution(mesh):
    small = (mesh.shape["expert"], mesh.shape["dp"]) == (4, 2) and mesh.shape["segment"] > 2
    placed = (
        P("segment", "dp", "expert", None),
        P("segment", "dp", "expert", None),
        P("segment", None, None, "expert"),
        P("segment", "expert", None),
        P("segment", None, None),
        P("segment", None, None),
        P("segment", None, "expert"),
        P("segment", "expert", None),
        P("segment", "dp", "expert", None),
        P("segment", "dp", None),
        P("segment", "dp", "expert", None),
    )
    return jax.shard_map(
        fused if small else shards,
        mesh=mesh,
        in_specs=placed,
        out_specs=(
            P("segment", "dp", "expert", None),
            P("segment", "dp", "expert", None),
            P("segment", None, None),
        ),
        check_vma=False,
    )
```

```python
import jax
import jax.numpy as jnp
from jax import lax
from jax.experimental import pallas as pl
from jax.experimental.pallas import tpu as pltpu
from jax.sharding import PartitionSpec as P

HEAD_DIM = 128
TOP = 2
SEQ = 128


eps = 1e-05
highest = lax.Precision.HIGHEST


def from_behind(block, axis, distance):
    devices = range(lax.axis_size(axis))
    route = [((i - distance) % len(devices), i) for i in devices]
    return lax.ppermute(block, axis, route)


def layer_norm(values, gain):
    centered = values - jnp.mean(values, axis=-1, keepdims=True)
    variance = jnp.mean(centered * centered, axis=-1, keepdims=True)
    return centered * lax.rsqrt(variance + eps) * gain


def shards(
    x_in,
    memory,
    w_qkv,
    w_attn_out,
    norm_gains,
    router,
    w_in,
    w_exp_out,
    expert_ids,
    lengths,
    cotangent,
):
    segment_pos = lax.axis_index("segment")
    rows_here = x_in[0, 0]
    tok_dev = rows_here.shape[0]
    width = rows_here.shape[1]
    head_cols = w_attn_out.shape[1]
    gains = norm_gains[0]
    weights_qkv = w_qkv[0]
    normed = layer_norm(rows_here.astype(jnp.float32), gains[0]).astype(jnp.bfloat16)
    key_source = jnp.where(segment_pos == 0, normed, memory[0, 0])
    stacked = jnp.stack((normed, key_source), axis=0)
    piece = lax.all_gather(stacked, "expert", axis=1, tiled=True)
    query = jnp.dot(piece[0], weights_qkv[0], preferred_element_type=jnp.float32)
    keys = jnp.dot(piece[1], weights_qkv[1], preferred_element_type=jnp.float32)
    values = jnp.dot(piece[1], weights_qkv[2], preferred_element_type=jnp.float32)
    projected = jnp.concatenate((query, keys, values), axis=1).astype(jnp.bfloat16)
    group_rows = projected.shape[0]
    count = group_rows // SEQ
    heads_here = head_cols // HEAD_DIM
    shaped = projected.reshape(count, SEQ, 3, heads_here, HEAD_DIM)
    scores = jnp.einsum(
        "nihd,njhd->nhij", shaped[:, :, 0], shaped[:, :, 1], preferred_element_type=jnp.float32
    ) * HEAD_DIM ** (-0.5)
    live = (jnp.arange(SEQ)[None, :] < lengths[0, 0][:, None]).astype(jnp.float32)
    raised = jnp.exp(scores) * live[:, None, None, :]
    probs = (raised / jnp.sum(raised, axis=-1, keepdims=True)).astype(jnp.bfloat16)
    context = jnp.einsum(
        "nhij,njhd->nihd", probs, shaped[:, :, 2], preferred_element_type=jnp.float32
    )
    context = context.astype(jnp.bfloat16).reshape(group_rows, head_cols)
    attn_sum = lax.psum_scatter(
        jnp.dot(context, w_attn_out[0], preferred_element_type=jnp.float32).astype(jnp.bfloat16),
        "expert",
        scatter_dimension=0,
        tiled=True,
    ).astype(jnp.float32)
    resid = rows_here.astype(jnp.float32) + attn_sum
    moe_in = layer_norm(resid, gains[1]).astype(jnp.bfloat16)
    moe_wide = moe_in.astype(jnp.float32)
    logits = jnp.dot(moe_wide, router[0], precision=highest)
    ids = expert_ids[0, 0]
    n_exp = router.shape[2]
    pick_int = (ids[:, :, None] == jnp.arange(n_exp)[None, None, :]).astype(jnp.int32)
    pick = pick_int.astype(jnp.float32)
    chosen = jnp.sum(pick * logits[:, None, :], axis=2)
    gates = jax.nn.sigmoid(chosen - chosen[:, ::-1])
    flat_pick = pick_int.reshape(tok_dev * TOP, n_exp)
    assigned = flat_pick.shape[0]
    earlier = (jnp.arange(assigned)[:, None] > jnp.arange(assigned)[None, :]).astype(jnp.bfloat16)
    before = jnp.dot(
        earlier, flat_pick.astype(jnp.bfloat16), preferred_element_type=jnp.float32
    ).astype(jnp.int32)
    slot = jnp.sum(before * flat_pick, axis=1)
    capacity = tok_dev * TOP // n_exp
    target = ids.reshape(-1) * capacity + slot
    place = (jnp.arange(n_exp * capacity)[:, None] == target[None, :]).astype(jnp.bfloat16)
    place = jnp.sum(place.reshape(n_exp * capacity, tok_dev, TOP), axis=2)
    send_rows = jnp.dot(place, moe_in, preferred_element_type=jnp.float32).astype(jnp.bfloat16)
    copies = lax.axis_size("expert") // n_exp
    outgoing = jnp.broadcast_to(
        send_rows.reshape(n_exp, 1, capacity, width), (n_exp, copies, capacity, width)
    )
    outgoing = outgoing.reshape(n_exp * copies, capacity, width)
    arrived = lax.all_to_all(outgoing, "expert", split_axis=0, concat_axis=0, tiled=True)
    sources = arrived.shape[0]
    slots_now = arrived.shape[1]
    flat = arrived.reshape(sources * slots_now, width)
    hidden = jnp.maximum(jnp.dot(flat, w_in[0], preferred_element_type=jnp.float32), 0.0).astype(
        jnp.bfloat16
    )
    partial_value = jnp.dot(hidden, w_exp_out[0], preferred_element_type=jnp.float32).astype(
        jnp.bfloat16
    )
    returned = lax.all_to_all(
        partial_value.reshape(sources, slots_now, width),
        "expert",
        split_axis=0,
        concat_axis=0,
        tiled=True,
    )
    expert_out = jnp.sum(
        returned.reshape(n_exp, copies, capacity, width).astype(jnp.float32), axis=1
    )
    expert_out = expert_out.reshape(n_exp * capacity, width)
    selected = expert_out[target].reshape(tok_dev, TOP, width)
    mixed = jnp.sum(gates[:, :, None] * selected, axis=1)
    layer_out = (resid + mixed).astype(jnp.bfloat16)
    cot = cotangent[0, 0].astype(jnp.float32)
    intersection = jnp.sum(cot[:, None, :] * selected, axis=2)
    delta = gates[:, 0] * gates[:, 1] * (intersection[:, 0] - intersection[:, 1])
    dlogits = delta[:, None] * (pick[:, 0] - pick[:, 1])
    local_grad = lax.dot_general(moe_wide, dlogits, (((0,), (0,)), ((), ())), precision=highest)
    total_rows = tok_dev * lax.axis_size("expert") * lax.axis_size("dp")
    router_grad = (
        lax.psum(local_grad.astype(jnp.bfloat16), ("expert", "dp")).astype(jnp.float32) / total_rows
    )
    carry = jnp.where(segment_pos == 0, layer_out, memory[0, 0])
    handed = from_behind(jnp.stack((layer_out, carry), axis=0), "segment", 1)
    return (handed[0][None, None], handed[1][None, None], router_grad[None])


BF = jnp.bfloat16
F32 = jnp.float32
MESH = pl.DeviceIdType.MESH
HALF = 64
CHUNK = 512
DEPTH = 1024
STRIP = 256
WIDE = 1024
LOAN = 32
PIECE = 16
LENDERS = (0, 1)


def tick(
    x_hbm, mem_hbm, wqkv_hbm, wo_hbm, gains_hbm, router_hbm, win_hbm, wout_hbm, ids_hbm, lengths_hbm, cot_hbm,
    acts_out, memory_out, grad_out,
    gains, router_t, ids_t, lengths, wqkv, wo, win, wout, xv, rows, qkv, csend, crecv, resid, moe_in, cot,
    dsend, arr, acc, hidden, rsend, rrecv, lo, gsend, grecv,
    wsem, winsem, woutsem, ag_s, ag_r, c_s, c_r, d_s, d_r, r_s, r_r, z_s, z_r, g_s, g_r, m_s, m_r, small_sem, turn, grad_here,
    loan, ld_s, ld_r, lu_s, lu_r, near_s, near_r,
):
    seg = lax.axis_index("segment")
    exp = lax.axis_index("expert")
    dp = lax.axis_index("dp")
    n_seg = lax.axis_size("segment")
    following = lax.rem(seg + 1, n_seg)
    behind = lax.rem(seg + n_seg - 1, n_seg)
    col = lax.rem(exp, 2)
    row = exp // 2

    def peer(r):
        return lax.rem(col + r % 2, 2) + 2 * lax.rem(row + r // 2, 2)

    def send(src, dst, s, r, device):
        return pltpu.make_async_remote_copy(
            src_ref=src, dst_ref=dst, send_sem=s, recv_sem=r, device_id=device, device_id_type=MESH
        )

    local = [
        pltpu.make_async_copy(mem_hbm, rows.at[1, 0], wsem.at[0]),
        pltpu.make_async_copy(x_hbm, xv, wsem.at[1]),
        pltpu.make_async_copy(wqkv_hbm, wqkv, wsem.at[2]),
        pltpu.make_async_copy(wo_hbm, wo, wsem.at[3]),
        pltpu.make_async_copy(cot_hbm, cot, wsem.at[4]),
    ]
    small = [
        pltpu.make_async_copy(gains_hbm, gains, small_sem.at[0]),
        pltpu.make_async_copy(lengths_hbm, lengths, small_sem.at[1]),
        pltpu.make_async_copy(ids_hbm, ids_t, small_sem.at[2]),
        pltpu.make_async_copy(router_hbm, router_t, small_sem.at[3]),
    ]
    def win_copy(c):
        part = pl.ds(pl.multiple_of(c * WIDE, WIDE), WIDE)
        return pltpu.make_async_copy(win_hbm.at[:, part], win.at[c], winsem.at[c])

    def wout_copy(c):
        part = pl.ds(pl.multiple_of(c * CHUNK, CHUNK), CHUNK)
        return pltpu.make_async_copy(wout_hbm.at[:, part], wout.at[c], woutsem.at[c])

    barrier = pltpu.get_barrier_semaphore()
    others = [(r, d) for r in range(4) for d in range(2) if r + d > 0]
    for r, d in others:
        pl.semaphore_signal(
            barrier, 1, device_id={"expert": peer(r), "dp": lax.rem(dp + d, 2)}, device_id_type=MESH
        )
    pl.semaphore_signal(barrier, 1, device_id={"segment": behind}, device_id_type=MESH)

    @pl.when(seg == 0)
    def _():
        for far in range(1, n_seg):
            for r in (1, 2):
                pl.semaphore_signal(barrier, 1, device_id={"segment": far, "expert": peer(r)}, device_id_type=MESH)

    @pl.when(seg != 0)
    def _():
        pl.semaphore_signal(barrier, 1, device_id={"segment": 0}, device_id_type=MESH)

    for copy in (local[0], local[1], small[0], small[1], *local[2:], *small[2:]):
        copy.start()

    top, low = pl.ds(0, HALF), pl.ds(HALF, HALF)

    def gather_copies(a):
        along_x, along_y = {"expert": peer(1)}, {"expert": peer(2)}
        low_rest, top_rest = (pl.ds(HALF + a * LOAN, HALF - a * LOAN), pl.ds(a * LOAN, HALF - a * LOAN))
        plan = [
            (0, top, 1, along_x), (0, low_rest, 1, along_x), (0, low, 2, along_y), (0, top_rest, 2, along_y),
            (1, top, 3, along_y), (2, low, 3, along_x),
        ]
        return [
            send(rows.at[a, source, part], rows.at[a, slot, part], ag_s.at[a, i], ag_r.at[a, i], dev)
            for i, (source, part, slot, dev) in enumerate(plan)
        ]

    along_x, along_y = {"expert": peer(1)}, {"expert": peer(2)}
    plan = [
        (1, top, 1, along_x), (2, low, 2, along_y), (3, top, 0, along_x), (3, low, 0, along_y),
        (2, top, 2, along_y), (1, low, 1, along_x),
    ]
    shares = [
        send(csend.at[source, part], crecv.at[slot, part], c_s.at[i], c_r.at[i], dev)
        for i, (source, part, slot, dev) in enumerate(plan)
    ]
    norm_ag, mem_ag = gather_copies(0), gather_copies(1)
    loans = [(k, p) for p in range(LOAN // PIECE) for k in range(2)]

    nearest = [n_seg - 1 - LENDERS[p] if LENDERS[p] else 0 for p in range(LOAN // PIECE)]

    def keep(k, p):
        part = pl.ds(HALF * (1 - k) + p * PIECE, PIECE)
        spot = rows.at[1, 1 + k, part]
        return send(rows.at[1, 0, part], spot, near_s.at[k, p], near_r.at[k, p], {"expert": peer(1 + k)})

    def each_loan(lent, kept=None):
        for k, p in loans:
            @pl.when(seg > nearest[p])
            def _(k=k, p=p):
                lent(k, p)

            if kept is not None and nearest[p] > 0:
                @pl.when((seg != 0) & (seg <= nearest[p]))
                def _(k=k, p=p):
                    kept(k, p)

    def lend(i, k, p):
        part = pl.ds(HALF * (1 - k) + p * PIECE, PIECE)
        device = {"segment": 0, "expert": peer(1 + k)}
        spot = loan.at[i, k, pl.ds(p * PIECE, PIECE)]
        return send(rows.at[1, 0, part], spot, ld_s.at[k, p], ld_r.at[i, k, p], device)

    def pass_on(i, k, p):
        part = pl.ds(HALF * (1 - k) + p * PIECE, PIECE)
        spot = loan.at[i, k, pl.ds(p * PIECE, PIECE)]
        return send(spot, rows.at[1, 1 + k, part], lu_s.at[i, k, p], lu_r.at[k, p], {"segment": i + 1})

    mem_relay = send(rows.at[1, 0], memory_out, m_s.at[0], m_r.at[0], {"segment": following})

    local[0].wait()

    @pl.when(seg == 0)
    def _():
        pl.semaphore_wait(barrier, len(others) + n_seg)

    @pl.when(seg != 0)
    def _():
        pl.semaphore_wait(barrier, len(others) + 3)

    early, late = (0, 2), (1, 3)

    @pl.when((seg != 0) & (dp == 0))
    def _():
        for i in early:
            mem_ag[i].start()

    each_loan(lambda k, p: lend(behind, k, p).start())

    local[1].wait()
    small[0].wait()

    def norm_rows(i, _):
        part = pl.ds(pl.multiple_of(i * 32, 32), 32)
        values = xv[part, :].astype(F32)
        normed = layer_norm(values, gains[0:1, :]).astype(BF)
        rows[0, 0, part, :] = normed
        return 0

    lax.fori_loop(0, 4, norm_rows, 0)

    @pl.when((dp == 0))
    def _():
        for i in early:
            norm_ag[i].start()

    def start_weights(c, _):
        win_copy(c).start()
        return 0

    def start_weights_out(c, _):
        wout_copy(c).start()
        return 0

    lax.fori_loop(0, win.shape[0], start_weights, 0)
    lax.fori_loop(0, wout.shape[0], start_weights_out, 0)

    @pl.when((dp == 0) & (seg != 0))
    def _():
        for i in early:
            mem_ag[i].wait_send()

    @pl.when((dp == 0) & (seg == 0))
    def _():
        pl.semaphore_signal(turn, 1, device_id={"dp": 1}, device_id_type=MESH)

    @pl.when(dp == 1)
    def _():
        pl.semaphore_wait(turn, 1)

        @pl.when(seg != 0)
        def _():
            for i in early:
                mem_ag[i].start()

        for i in early:
            norm_ag[i].start()

    @pl.when(seg == 0)
    def _():
        for i in early:
            norm_ag[i].wait_recv()
            norm_ag[4 + i // 2].start()
        for i in late:
            norm_ag[i].start()
        for k, p in loans:
            for i in reversed(range(nearest[p], n_seg - 1)):
                lend(i, k, p).wait_recv()
                pass_on(i, k, p).start()

    local[2].wait()
    local[3].wait()
    small[1].wait()

    tokens = SEQ
    small[2].wait()
    first, second = ids_t[0:1, :], ids_t[1:2, :]
    earlier = (
        lax.broadcasted_iota(jnp.int32, (tokens, tokens), 0)
        < lax.broadcasted_iota(jnp.int32, (tokens, tokens), 1)
    ).astype(BF)
    place, pick0, pick1 = [], [], []
    slot_no = lax.broadcasted_iota(jnp.int32, (HALF, tokens), 0).astype(F32)
    for r in range(4):
        one = (first == peer(r)).astype(F32)
        two = (second == peer(r)).astype(F32)
        named = one + two
        slot = jnp.dot(
            jnp.broadcast_to(named, (16, tokens)).astype(BF), earlier, preferred_element_type=F32
        )[0:1, :]
        hit = (slot_no == slot).astype(F32)
        place.append((hit * named).astype(BF))
        pick0.append(hit * one)
        pick1.append(hit * two)
    back = jnp.concatenate(
        [jnp.concatenate(pick0, axis=0).T, jnp.concatenate(pick1, axis=0).T], axis=0
    ).astype(BF)

    def project(r, j):
        source = ((j + 1) // 2) * ((seg + n_seg - 1) // n_seg)
        got = jnp.dot(rows[source, r], wqkv[j], preferred_element_type=F32)
        qkv[lax.rem(r, 3), j] = got.astype(BF)

    def section(step, _):
        r = (lax.rem(step + 1, 3) + 1) * ((step + 2) // 3)

        @pl.when((step == 1) & (seg != 0))
        def _():
            for i in early:
                mem_ag[i].wait_recv()
                mem_ag[4 + i // 2].start()
            for i in early:
                norm_ag[i].wait_recv()
                norm_ag[4 + i // 2].start()
            each_loan(lambda k, p: None, lambda k, p: keep(k, p).start())
            for i in late:
                mem_ag[i].start()
            for i in late:
                norm_ag[i].start()
            for i in (4, 5):
                mem_ag[i].wait_recv()

        @pl.when(step == 1)
        def _():
            for i in (4, 5):
                norm_ag[i].wait_recv()

        @pl.when((step == 2) & (seg != 0))
        def _():
            for i in late:
                mem_ag[i].wait_recv()
            each_loan(lambda k, p: pass_on(0, k, p).wait_recv(), lambda k, p: keep(k, p).wait_recv())
            mem_relay.start()

        @pl.when(step == 2)
        def _():
            @pl.when(seg == 0)
            def _():
                for i in late:
                    norm_ag[i].wait_recv()

            def keys_values(n, _):
                project(1 + n // 2, 1 + lax.rem(n, 2))
                return 0

            lax.fori_loop(0, 4, keys_values, 0)

            @pl.when(seg != 0)
            def _():
                for i in late:
                    norm_ag[i].wait_recv()

        def project_step(j, _):
            project(r, j)
            return 0

        lax.fori_loop(0, 3 - 2 * (step // 2), project_step, 0)

        @pl.when((step == 0) & (dp == 0) & (seg != 0))
        def _():
            pl.semaphore_signal(turn, 1, device_id={"dp": 1}, device_id_type=MESH)

        owner = peer(r)
        held = lax.rem(r, 3)
        live = (lax.broadcasted_iota(jnp.int32, (1, SEQ), 1) < lengths[owner]).astype(F32)
        parts = []
        for h in range(wo.shape[0] // HEAD_DIM):
            cols = slice(h * HEAD_DIM, (h + 1) * HEAD_DIM)
            scores = lax.dot_general(
                qkv[held, 0, :, cols], qkv[held, 1, :, cols], (((1,), (1,)), ((), ())), preferred_element_type=F32
            ) * HEAD_DIM ** (-0.5)
            raised = jnp.exp(scores) * live
            probs = (raised / jnp.sum(raised, axis=-1, keepdims=True)).astype(BF)
            parts.append(jnp.dot(probs, qkv[held, 2, :, cols], preferred_element_type=F32).astype(BF))
        context = jnp.concatenate(parts, axis=1)
        for c in range(4):
            cols = slice(c * CHUNK, (c + 1) * CHUNK)
            csend[r, :, cols] = jnp.dot(context, wo[:, cols], preferred_element_type=F32).astype(BF)

        @pl.when(step == 1)
        def _():
            shares[2].start()
            shares[3].start()

        @pl.when(step == 2)
        def _():
            shares[0].start()

        @pl.when(step == 3)
        def _():
            shares[1].start()

        return 0

    lax.fori_loop(0, 4, section, 0)

    for base, source, came, goes in ((HALF, 1, 3, 5), (0, 2, 2, 4)):
        shares[came].wait_recv()

        def join(i, _, base=base, source=source):
            part = pl.ds(pl.multiple_of(base + i * 32, 32), 32)
            both = csend[source, part, :].astype(F32) + crecv[0, part, :].astype(F32)
            csend[source, part, :] = both.astype(BF)
            return 0

        lax.fori_loop(0, HALF // 32, join, 0)
        shares[goes].start()
    def second_norm(i, _):
        part = pl.ds(pl.multiple_of(i * 32, 32), 32)
        total = csend[0, part, :].astype(F32)
        for r in (1, 2):
            total = total + crecv[r, part, :].astype(F32)
        values = xv[part, :].astype(F32) + total
        resid[part, :] = values
        moe_in[part, :] = layer_norm(values, gains[1:2, :]).astype(BF)
        return 0

    def finish(half, _):
        @pl.when(half == 0)
        def _():
            shares[1].wait_recv()
            shares[5].wait_recv()

        @pl.when(half == 1)
        def _():
            shares[0].wait_recv()
            shares[4].wait_recv()

        lax.fori_loop(2 - 2 * half, 4 - 2 * half, second_norm, 0)
        return 0

    lax.fori_loop(0, 2, finish, 0)

    def dispatch(k, r):
        part = pl.ds(r * HALF, HALF)
        return send(dsend.at[k, part], arr.at[k, part], d_s.at[k, r], d_r.at[k, r], {"expert": peer(r)})

    placed = jnp.concatenate(place, axis=0)

    for k in range(arr.shape[0]):
        for j in range(DEPTH // CHUNK):
            cols = slice(k * DEPTH + j * CHUNK, k * DEPTH + (j + 1) * CHUNK)
            chosen = jnp.dot(placed, moe_in[:, cols], preferred_element_type=F32).astype(BF)
            dsend[k, :, j * CHUNK:(j + 1) * CHUNK] = chosen
            arr[k, 0:HALF, j * CHUNK:(j + 1) * CHUNK] = chosen[0:HALF, :]
        if k == 0:
            @pl.when(dp == 1)
            def _():
                pl.semaphore_wait(turn, 1)

        for r in (3, 1, 2):
            dispatch(k, r).start()

    small[3].wait()
    logits = lax.dot_general(
        router_t[...], moe_in[...].astype(F32), (((1,), (1,)), ((), ())),
        precision=highest, preferred_element_type=F32,
    )
    chosen0 = jnp.zeros((1, tokens), F32)
    chosen1 = jnp.zeros((1, tokens), F32)
    for e in range(4):
        chosen0 = chosen0 + (first == e).astype(F32) * logits[e:e + 1, :]
        chosen1 = chosen1 + (second == e).astype(F32) * logits[e:e + 1, :]
    gate0 = jax.nn.sigmoid(chosen0 - chosen1)
    gate1 = jax.nn.sigmoid(chosen1 - chosen0)
    slope = gate0 * gate1
    gate0 = jnp.broadcast_to(gate0, (tokens, tokens)).T[:, 0:1]
    gate1 = jnp.broadcast_to(gate1, (tokens, tokens)).T[:, 0:1]

    for r in (3, 1, 2):
        dispatch(0, r).wait_recv()

    @pl.when(dp == 0)
    def _():
        pl.semaphore_signal(turn, 1, device_id={"dp": 1}, device_id_type=MESH)

    def columns_first(c, _):
        win_copy(c).wait()
        acc[c] = jnp.dot(arr[0], win[c, 0:DEPTH, :], preferred_element_type=F32)
        return 0

    lax.fori_loop(0, win.shape[0], columns_first, 0)
    for r in (3, 1, 2):
        dispatch(1, r).wait_recv()

    def columns_last(c, _):
        got = jnp.dot(arr[1], win[c, DEPTH:2 * DEPTH, :], preferred_element_type=F32)
        cols = pl.ds(pl.multiple_of(c * WIDE, WIDE), WIDE)
        hidden[:, cols] = jnp.maximum(acc[c] + got, 0.0).astype(BF)
        return 0

    lax.fori_loop(0, win.shape[0], columns_last, 0)

    def give_back(c, r):
        part = pl.ds(r * HALF, HALF)
        return send(rsend.at[c, part], rrecv.at[c, part], r_s.at[c, r], r_r.at[c, r], {"expert": peer(r)})

    def expert_out(c, _):
        wout_copy(c).wait()
        got = jnp.dot(hidden[...], wout[c], preferred_element_type=F32).astype(BF)
        for j in range(CHUNK // STRIP):
            strip = got[:, j * STRIP:(j + 1) * STRIP]
            n = c * (CHUNK // STRIP) + j
            rsend[n] = strip
            rrecv[n, 0:HALF, :] = strip[0:HALF, :]
            for r in (3, 1, 2):
                give_back(n, r).start()
        return 0

    lax.fori_loop(0, wout.shape[0], expert_out, 0)
    local[4].wait()

    def onward(c):
        cols = pl.ds(pl.multiple_of(c * STRIP, STRIP), STRIP)
        return send(lo.at[c], acts_out.at[:, cols], z_s.at[c], z_r.at[c], {"segment": following})

    def combine(c, gap):
        for r in (3, 1, 2):
            give_back(c, r).wait_recv()
        cols = pl.ds(pl.multiple_of(c * STRIP, STRIP), STRIP)
        both = jnp.dot(back, rrecv[c], preferred_element_type=F32)
        sel0, sel1 = both[0:tokens, :], both[tokens:2 * tokens, :]
        lo[c] = (resid[:, cols] + (gate0 * sel0 + gate1 * sel1)).astype(BF)
        onward(c).start()
        terms = cot[:, cols].astype(F32) * (sel0 - sel1)
        for j in range(STRIP // tokens):
            gap = gap + terms[:, j * tokens:(j + 1) * tokens]
        return gap

    strips = rsend.shape[0]
    gap = lax.fori_loop(0, strips, combine, jnp.zeros((tokens, tokens), F32))
    gap_row = jnp.zeros((16, tokens), F32)
    for _ in range(3):
        part = gap.astype(BF)
        gap = gap - part.astype(F32)
        gap_row = gap_row + lax.dot_general(
            jnp.ones((16, tokens), BF), part, (((1,), (1,)), ((), ())), preferred_element_type=F32
        )
    delta = slope * gap_row[0:1, :]
    rest = jnp.concatenate(
        [delta * ((first == e).astype(F32) - (second == e).astype(F32)) for e in range(4)], axis=0
    )
    terms = []
    for _ in range(3):
        terms.append(rest.astype(BF))
        rest = rest - terms[-1].astype(F32)
    terms = jnp.concatenate([term.astype(F32) for term in terms] + [jnp.zeros((4, tokens), F32)], axis=0)
    products = jnp.dot(terms.astype(BF), moe_in[...], preferred_element_type=F32)
    grad = products[0:4, :] + products[4:8, :] + products[8:12, :]
    gsend[...] = jnp.concatenate(
        [grad[0:4, c * CHUNK:(c + 1) * CHUNK] for c in range(4)], axis=0
    ).astype(BF)

    def share(r, d):
        i = r * 2 + d
        device = {"expert": peer(r), "dp": lax.rem(dp + d, 2)}
        return send(gsend, grecv.at[i], g_s.at[i], g_r.at[i], device)

    for r, d in others:
        share(r, d).start()
    @pl.when(seg != 0)
    def _():
        mem_relay.wait_send()

    @pl.when(seg != 1)
    def _():
        mem_relay.wait_recv()

    for i in range(6):
        norm_ag[i].wait_send()

    @pl.when(seg != 0)
    def _():
        for i in (1, 3, 4, 5):
            mem_ag[i].wait_send()
        each_loan(lambda k, p: lend(behind, k, p).wait_send(), lambda k, p: keep(k, p).wait_send())

    @pl.when((seg != 0) & (dp == 1))
    def _():
        for i in early:
            mem_ag[i].wait_send()

    @pl.when(seg == 0)
    def _():
        for k, p in loans:
            for i in range(nearest[p], n_seg - 1):
                pass_on(i, k, p).wait_send()

    for r in (1, 2, 3):
        for c in range(arr.shape[0]):
            dispatch(c, r).wait_send()
        for c in range(strips):
            give_back(c, r).wait_send()
    for copy in shares:
        copy.wait_send()
    def drain(c, _):
        onward(c).wait_send()
        onward(c).wait_recv()
        return 0

    lax.fori_loop(0, strips - 1, drain, 0)
    for r, d in others:
        share(r, d).wait_recv()
    total = gsend[...].astype(F32)
    for r, d in others:
        total = total + grecv[r * 2 + d].astype(F32)
    total = total / (tokens * lax.axis_size("expert") * lax.axis_size("dp"))
    for c in range(4):
        grad_here[:, c * CHUNK:(c + 1) * CHUNK] = total[c * 4:(c + 1) * 4, :]

    for r, d in others:
        share(r, d).wait_send()
    done = pltpu.make_async_copy(grad_here, grad_out, small_sem.at[0])
    done.start()
    drain(strips - 1, 0)
    done.wait()


def hand_over(acts, kept, grad, acts_out, memory_out, grad_out, here, mem_here, grad_here, came, went):
    seg = lax.axis_index("segment")
    pieces = here.shape[0]
    size = here.shape[1]

    def part(c):
        return pl.ds(c * size, size)

    def arrival(ref, spot, kind, c):
        return pltpu.make_async_copy(ref.at[part(c)], spot.at[c], came.at[kind, c])

    for c in range(pieces):
        arrival(acts, here, 0, c).start()

        @pl.when(seg == 1)
        def _(c=c):
            arrival(acts, mem_here, 1, c).start()

        @pl.when(seg != 1)
        def _(c=c):
            arrival(kept, mem_here, 1, c).start()

    grad_in = pltpu.make_async_copy(grad, grad_here, came.at[2, 0])
    grad_in.start()
    leaving = []
    for c in range(pieces):
        for kind, spot, goal in ((0, here, acts_out), (1, mem_here, memory_out)):
            arrival(acts, spot, kind, c).wait()
            leaving.append(pltpu.make_async_copy(spot.at[c], goal.at[part(c)], went.at[kind, c]))
            leaving[-1].start()
    grad_in.wait()
    leaving.append(pltpu.make_async_copy(grad_here, grad_out, went.at[2, 0]))
    leaving[-1].start()
    for copy in leaving:
        copy.wait()


def fused(
    x_in, memory, w_qkv, w_attn_out, norm_gains, router, w_in, w_exp_out, expert_ids, lengths, cotangent
):
    tokens, width = x_in.shape[2:]
    head_cols = w_attn_out.shape[1]
    hid = w_in.shape[2]
    n_in, n_out, strips, deep = hid // WIDE, width // CHUNK, width // STRIP, width // DEPTH
    n_seg = lax.axis_size("segment")
    hbm = pl.BlockSpec(memory_space=pl.ANY)
    vmem = pl.BlockSpec(memory_space=pltpu.VMEM)
    smem = pl.BlockSpec(memory_space=pltpu.SMEM)
    dma = pltpu.SemaphoreType.DMA
    acts, kept, grad = pl.pallas_call(
        tick,
        out_shape=(
            jax.ShapeDtypeStruct((tokens, width), BF),
            jax.ShapeDtypeStruct((tokens, width), BF),
            jax.ShapeDtypeStruct((4, width), F32),
        ),
        in_specs=[hbm] * 11,
        out_specs=(hbm, hbm, hbm),
        scratch_shapes=[
            pltpu.VMEM((2, width), F32),
            pltpu.VMEM((4, width), F32),
            pltpu.VMEM((2, tokens), jnp.int32),
            pltpu.SMEM((4,), jnp.int32),
            pltpu.VMEM((3, width, head_cols), BF),
            pltpu.VMEM((head_cols, width), BF),
            pltpu.VMEM((n_in, width, WIDE), BF),
            pltpu.VMEM((n_out, hid, CHUNK), BF),
            pltpu.VMEM((tokens, width), BF),
            pltpu.VMEM((2, 4, tokens, width), BF),
            pltpu.VMEM((3, 3, tokens, head_cols), BF),
            pltpu.VMEM((4, tokens, width), BF),
            pltpu.VMEM((3, tokens, width), BF),
            pltpu.VMEM((tokens, width), F32),
            pltpu.VMEM((tokens, width), BF),
            pltpu.VMEM((tokens, width), BF),
            pltpu.VMEM((deep, 4 * HALF, DEPTH), BF),
            pltpu.VMEM((deep, 4 * HALF, DEPTH), BF),
            pltpu.VMEM((n_in, 4 * HALF, WIDE), F32),
            pltpu.VMEM((4 * HALF, hid), BF),
            pltpu.VMEM((strips, 4 * HALF, STRIP), BF),
            pltpu.VMEM((strips, 4 * HALF, STRIP), BF),
            pltpu.VMEM((strips, tokens, STRIP), BF),
            pltpu.VMEM((16, CHUNK), BF),
            pltpu.VMEM((8, 16, CHUNK), BF),
            dma((5,)), dma((n_in,)), dma((n_out,)),
            dma((2, 6)), dma((2, 6)), dma((6,)), dma((6,)), dma((deep, 4)), dma((deep, 4)),
            dma((strips, 4)), dma((strips, 4)), dma((strips,)), dma((strips,)),
            dma((8,)), dma((8,)), dma((1,)), dma((1,)), dma((4,)), pltpu.SemaphoreType.REGULAR,
            pltpu.VMEM((4, width), F32),
            pltpu.VMEM((n_seg - 1, 2, LOAN, width), BF),
            dma((2, LOAN // PIECE)), dma((n_seg - 1, 2, LOAN // PIECE)),
            dma((n_seg - 1, 2, LOAN // PIECE)), dma((2, LOAN // PIECE)), dma((2, LOAN // PIECE)), dma((2, LOAN // PIECE)),
        ],
        compiler_params=pltpu.CompilerParams(
            collective_id=0, has_side_effects=True, vmem_limit_bytes=64 * 2**20 - 2**18
        ),
    )(
        x_in[0, 0], memory[0, 0], w_qkv[0], w_attn_out[0], norm_gains[0], router[0].T, w_in[0],
        w_exp_out[0], expert_ids[0, 0].T, lengths[0, 0], cotangent[0, 0],
    )
    pieces = 4
    acts, kept, grad = pl.pallas_call(
        hand_over,
        out_shape=(acts, kept, grad),
        in_specs=[hbm] * 3,
        out_specs=(hbm, hbm, hbm),
        scratch_shapes=[
            pltpu.VMEM((pieces, tokens // pieces, width), BF),
            pltpu.VMEM((pieces, tokens // pieces, width), BF),
            pltpu.VMEM((4, width), F32),
            dma((3, pieces)),
            dma((3, pieces)),
        ],
    )(acts, kept, grad)
    return acts[None, None], kept[None, None], grad.T[None]


def solution(mesh):
    small = (mesh.shape["expert"], mesh.shape["dp"]) == (4, 2) and mesh.shape["segment"] > 2
    placed = (
        P("segment", "dp", "expert", None),
        P("segment", "dp", "expert", None),
        P("segment", None, None, "expert"),
        P("segment", "expert", None),
        P("segment", None, None),
        P("segment", None, None),
        P("segment", None, "expert"),
        P("segment", "expert", None),
        P("segment", "dp", "expert", None),
        P("segment", "dp", None),
        P("segment", "dp", "expert", None),
    )
    return jax.shard_map(
        fused if small else shards,
        mesh=mesh,
        in_specs=placed,
        out_specs=(
            P("segment", "dp", "expert", None),
            P("segment", "dp", "expert", None),
            P("segment", None, None),
        ),
        check_vma=False,
    )
```
